32 devices in a mesh: dp: 16 (over z, y, core), tensor: 2 (over x).
Axes of the slice: x: 2, y: 2, z: 4, core: 2. Of those that a mesh axis runs over, the one named last changes fastest.
Arguments:
- tokens: bfloat16 [25088, 512], P(('dp', 'tensor')), may hold values from -6 to 6
- cotangent: bfloat16 [25088, 512], P(('dp', 'tensor')), may hold values from -6 to 6
- ln1_scale: float32 [512], P(('dp', 'tensor')), may hold values from 0.5 to 1.5
- ln1_shift: float32 [512], P(('dp', 'tensor')), may hold values from -1.75 to 1.75
- w_qkv: float32 [3, 512, 512], P(None, ('dp', 'tensor')), may hold values from -0.375 to 0.375
- w_out: float32 [512, 512], P(('dp', 'tensor')), may hold values from -0.75 to 0.75
- out_bias: float32 [512], P(('dp', 'tensor')), may hold values from -0.625 to 0.625
- ln2_scale: float32 [512], P(('dp', 'tensor')), may hold values from 0.5 to 1.5
- ln2_shift: float32 [512], P(('dp', 'tensor')), may hold values from -1.75 to 1.75
- w_router: float32 [512, 32], P(('dp', 'tensor')), may hold values from -0.1875 to 0.1875
- w_in: float32 [32, 512, 2048], P(None, 'dp', 'tensor'), may hold values from -0.25 to 0.25
- b_in: float32 [32, 2048], P('dp', 'tensor'), may hold values from -0.625 to 0.625
- w_back: float32 [32, 2048, 512], P(None, 'tensor', 'dp'), may hold values from -1.5 to 1.5
- b_back: float32 [32, 512], P(None, ('dp', 'tensor')), may hold values from -1.25 to 1.25
- choices: int32 [25088, 2], P(('dp', 'tensor')), may hold values from 0 to 31, as said below
- slots: int32 [25088, 2], P(('dp', 'tensor')), may hold values from -1 to 64, as said below
Outputs:
- result: bfloat16 [25088, 512], P(('dp', 'tensor'))
- grad_tokens: float32 [25088, 512], P(('dp', 'tensor'))
- grad_ln1_scale: float32 [512], P(('dp', 'tensor'))
- grad_ln1_shift: float32 [512], P(('dp', 'tensor'))
- grad_w_qkv: float32 [3, 512, 512], P(None, ('dp', 'tensor'))
- grad_w_out: float32 [512, 512], P(('dp', 'tensor'))
- grad_out_bias: float32 [512], P(('dp', 'tensor'))
- grad_ln2_scale: float32 [512], P(('dp', 'tensor'))
- grad_ln2_shift: float32 [512], P(('dp', 'tensor'))
- grad_w_router: float32 [512, 32], P(('dp', 'tensor'))
- grad_w_in: float32 [32, 512, 2048], P(None, 'dp', 'tensor')
- grad_b_in: float32 [32, 2048], P('dp', 'tensor')
- grad_w_back: float32 [32, 2048, 512], P(None, 'tensor', 'dp')
- grad_b_back: float32 [32, 512], P(None, ('dp', 'tensor'))
The draws below stay inside these ranges and needn't reach their ends.
Inputs may be any that keep to these rules, and one draw needn't show every extreme that they name: `choices`: each token names two different experts. slots[t, k] is the number of pairs of the same device and expert that come before pair (t, k), where all first choices of the device's 784 tokens in token order come before all its second choices; it is -1 where that number is 65 or more.
All inputs are finite; a program needn't handle non-finite values.
Results may differ from the reference program's by a relative error of at most 0.015.
The reference program's roundings to bfloat16 on the way count: a program that leaves them out, or rounds other values in their place, can miss the bound.
Values may be sent and summed in bfloat16 or wider, within the bound.
A program may use at most 320 MiB of HBM per device.

```python
import jax
import jax.numpy as jnp
from jax import lax

D = 512
H = 8
HD = 64
FF = 2048
E = 32
SEQ = 196
IMG_PER = 4
TOK_DEV = 784
CAP = 65
TOKENS = 25088
N_TENSOR = 2


def route_tables(key):
    base_key = jax.random.fold_in(key, 11)
    pop_key, heavy_key, first_key, offset_key = jax.random.split(base_key, 4)
    levels = jax.random.randint(pop_key, (E,), 0, 3)
    weights = jnp.left_shift(jnp.ones((E,), jnp.int32), levels)
    heavy_one = jax.random.randint(heavy_key, (), 0, E)
    weights = jnp.where(jnp.arange(E) == heavy_one, 8, weights)
    bounds = jnp.cumsum(weights)
    ticket = jax.random.randint(first_key, (TOKENS,), 0, bounds[E - 1])
    first_pick = jnp.sum((ticket[:, None] >= bounds[None, :]).astype(jnp.int32), axis=1)
    second_pick = (first_pick + 1 + jax.random.randint(offset_key, (TOKENS,), 0, E - 1)) % E
    choice_rows = jnp.stack([first_pick, second_pick], axis=1).astype(jnp.int32)
    devices = TOKENS // TOK_DEV
    pair_order = choice_rows.reshape(devices, TOK_DEV, 2).transpose(0, 2, 1).reshape(devices, 2 * TOK_DEV)
    onehot = (pair_order[:, :, None] == jnp.arange(E)[None, None, :]).astype(jnp.int32)
    before = jnp.cumsum(onehot, axis=1) - onehot
    slot_place = jnp.sum(before * onehot, axis=2)
    slot_place = jnp.where(slot_place < CAP, slot_place, -1)
    slot_place = slot_place.reshape(devices, 2, TOK_DEV).transpose(0, 2, 1).reshape(TOKENS, 2)
    return (choice_rows, slot_place.astype(jnp.int32))


def draw_choices(key, part):
    return route_tables(key)[0]


def draw_slots(key, part):
    return route_tables(key)[1]


def raised(result, stream_key, source, target, blocks, factor):
    owner, partner = [(jnp.arange(result.shape[dim]) // (result.shape[dim] // blocks)).reshape([-1 if axis == dim else 1 for axis in range(result.ndim)]) for dim in (source, target)]
    chosen = jax.random.permutation(stream_key, blocks)[partner]
    strong = (owner == chosen) | (owner == (partner + blocks // 2) % blocks)
    return jnp.where(strong, factor * result, result)


def block_scale(rng, shape, shards, least, largest):
    factor_of = 1.0
    for position, blocks in shards:
        steps = jax.random.uniform(jax.random.fold_in(jax.random.fold_in(rng, 6), position), (blocks,), jnp.float32, least / len(shards), largest / len(shards))
        factor_of = factor_of * jnp.repeat(jnp.exp(steps), shape[position] // blocks).reshape((-1,) + (1,) * (len(shape) - 1 - position))
    return factor_of


def scatter_about(stream_key, extent, width, most, cuts=(), kind=jnp.bfloat16):
    entries = jax.random.normal(stream_key, extent, jnp.float32) * width
    if len(cuts) > 0:
        entries = block_scale(stream_key, extent, cuts, -0.22, 0.18) * entries
    return jnp.clip(entries, min=-most, max=most).astype(kind)


def heavy_noise(key, dims, scale, most, cuts, heavy, kind=jnp.bfloat16):
    entries = scale * jax.random.normal(key, dims, jnp.float32)
    if cuts:
        entries = entries * block_scale(key, dims, cuts, -0.22, 0.18)
    return jnp.clip(raised(entries, jax.random.fold_in(key, 3), *heavy), -most, most).astype(kind)


def setup_inputs(seed: int = 0) -> dict:
    seeds = jax.random.split(jax.random.key(seed), 17)
    return {
        "tokens": scatter_about(seeds[0], (TOKENS, D), 1.0, 6.0, ((0, 32),)),
        "cotangent": heavy_noise(seeds[1], (TOKENS, D), 1.0, 6.0, ((0, 32),), (0, 1, 32, 2.75)),
        "ln1_scale": jnp.clip(1.0 + 0.1 * jax.random.normal(seeds[2], (D,), jnp.float32), 0.5, 1.5),
        "ln1_shift": scatter_about(seeds[3], (D,), 0.3, 1.75, ((0, 32),), jnp.float32),
        "w_qkv": scatter_about(seeds[4], (3, D, D), (D // 2) ** -0.5, 0.375, ((1, 32),), jnp.float32),
        "w_out": scatter_about(seeds[5], (D, D), (D // 8) ** -0.5, 0.75, ((0, 32),), jnp.float32),
        "out_bias": scatter_about(seeds[6], (D,), 0.1, 0.625, ((0, 32),), jnp.float32),
        "ln2_scale": jnp.clip(1.0 + 0.1 * jax.random.normal(seeds[7], (D,), jnp.float32), 0.5, 1.5),
        "ln2_shift": scatter_about(seeds[8], (D,), 0.3, 1.75, ((0, 32),), jnp.float32),
        "w_router": scatter_about(seeds[9], (D, E), (2 * D) ** -0.5, 0.1875, ((0, 32),), jnp.float32),
        "w_in": scatter_about(seeds[10], (E, D, FF), D ** -0.5, 0.25, ((1, 16), (2, 2)), jnp.float32),
        "b_in": scatter_about(seeds[11], (E, FF), 0.1, 0.625, ((0, 16), (1, 2)), jnp.float32),
        "w_back": scatter_about(seeds[12], (E, FF, D), (max(1, FF // 128)) ** -0.5, 1.5, ((1, 2), (2, 16)), jnp.float32),
        "b_back": scatter_about(seeds[13], (E, D), 0.2, 1.25, ((1, 32),), jnp.float32),
        "choices": draw_choices(jax.random.fold_in(seeds[16], 71), 0),
        "slots": draw_slots(jax.random.fold_in(seeds[16], 71), 0),
    }


@jax.custom_vjp
def low(v):
    return lax.optimization_barrier(v.astype(jnp.bfloat16)).astype(jnp.float32)

@jax.custom_vjp
def low_back(v):
    return v

def low_keep(v):
    return (low(v), None)

def low_pass(kept, grad):
    return (grad,)

def back_keep(v):
    return (v, None)

def back_low(kept, grad):
    return (low(grad),)
low.defvjp(low_keep, low_pass)
low_back.defvjp(back_keep, back_low)
exact_mode = lax.Precision.HIGHEST

def norm_affine(values_in, gain_vec, shift_vec):
    center = values_in - lax.optimization_barrier(jnp.mean(values_in, axis=-1, keepdims=True))
    spread = lax.optimization_barrier(jnp.mean(center * center, axis=-1, keepdims=True))
    return center * lax.rsqrt(spread + 1e-06) * gain_vec + shift_vec

def reference(tokens, cotangent, ln1_scale, ln1_shift, w_qkv, w_out, out_bias, ln2_scale, ln2_shift, w_router, w_in, b_in, w_back, b_back, choices, slots):
    target = jnp.where(slots >= 0, choices * CAP + slots, -1).astype(jnp.int32)
    groups = TOKENS // (N_TENSOR * TOK_DEV)
    group_imgs = N_TENSOR * IMG_PER
    slot_total = E * CAP
    score_scale = HD ** (-0.5)

    def attend_block(blocks):
        head_query, head_key, head_value = blocks
        raw_scores = low_back(jnp.einsum('ishd,ithd->ihst', head_query, head_key, precision=exact_mode))
        weights_att = low(jax.nn.softmax(raw_scores * score_scale, axis=-1))
        return jnp.einsum('ihst,ithd->ishd', weights_att, head_value, precision=exact_mode)

    def forward(residual, gain_one, shift_one, qkv_w, out_w, bias_attn, gain_two, shift_two, router, in_w, in_b, back_w, bias_back):
        gain_one, shift_one, qkv_w, out_w, bias_attn, gain_two, shift_two, router, in_w, in_b, back_w, bias_back = [low(member) for member in (gain_one, shift_one, qkv_w, out_w, bias_attn, gain_two, shift_two, router, in_w, in_b, back_w, bias_back)]
        normed_one = low(norm_affine(residual, gain_one, shift_one))
        projected = low_back(low(jnp.einsum('td,jde->jte', normed_one, qkv_w, precision=exact_mode)))
        heads_all = projected.reshape(3, groups, group_imgs, SEQ, H, HD)
        attended = lax.map(jax.checkpoint(attend_block), (heads_all[0], heads_all[1], heads_all[2]))
        attended = low_back(low(attended.reshape(TOKENS, D)))
        middle = residual + low_back(jnp.dot(attended, out_w, precision=exact_mode)) + bias_attn
        normed_two = low(norm_affine(middle, gain_two, shift_two))
        route_p = jax.nn.softmax(jnp.dot(normed_two, router, precision=exact_mode), axis=-1)
        gate_vals = jnp.take_along_axis(route_p, choices, axis=1)

        def expert_group(pieces):
            rows_in, gates_in, target_in = pieces
            onehot = (target_in[:, :, None] == jnp.arange(slot_total, dtype=jnp.int32)[None, None, :]).astype(jnp.float32)
            pair_rows = jnp.repeat(rows_in.reshape(N_TENSOR, TOK_DEV, D), 2, axis=1)
            filled = jnp.einsum('jpx,jpd->jxd', onehot, pair_rows, precision=exact_mode)
            all_slots = filled.reshape(N_TENSOR, E, CAP, D).transpose(1, 0, 2, 3).reshape(E, N_TENSOR * CAP, D)
            pre_act = low_back(jnp.einsum('ecd,edf->ecf', all_slots, in_w, precision=exact_mode) + in_b[:, None, :])
            hidden = low(jax.nn.gelu(pre_act, approximate=True))
            expert_sum = low_back(jnp.einsum('ecf,efd->ecd', hidden, back_w, precision=exact_mode))
            expert_out = (expert_sum + bias_back[:, None, :]).reshape(E, N_TENSOR, CAP, D).transpose(1, 0, 2, 3).reshape(N_TENSOR, slot_total, D)
            picked = jnp.einsum('jpx,jxd->jpd', onehot, expert_out, precision=exact_mode)
            weighted = picked * gates_in.reshape(N_TENSOR, 2 * TOK_DEV)[:, :, None]
            return lax.optimization_barrier(jnp.sum(weighted.reshape(N_TENSOR * TOK_DEV, 2, D), axis=1))
        mixed = lax.map(jax.checkpoint(expert_group), (normed_two.reshape(groups, N_TENSOR * TOK_DEV, D), gate_vals.reshape(groups, N_TENSOR * TOK_DEV, 2), target.reshape(groups, N_TENSOR, 2 * TOK_DEV)))
        return middle + mixed.reshape(TOKENS, D)
    output_rows, pull_back = jax.vjp(forward, tokens.astype(jnp.float32), ln1_scale, ln1_shift, w_qkv, w_out, out_bias, ln2_scale, ln2_shift, w_router, w_in, b_in, w_back, b_back)
    grads = pull_back(cotangent.astype(jnp.float32))
    return (output_rows.astype(jnp.bfloat16), grads[0], grads[1], grads[2], grads[3], grads[4], grads[5], grads[6], grads[7], grads[8], grads[9], grads[10], grads[11], grads[12])
```

```python
import jax
import jax.numpy as jnp
from jax import lax
from jax.sharding import PartitionSpec as P

H = 8
HD = 64
SEQ = 196
CAP = 65
LOW = jnp.bfloat16
WIDE = jnp.float32


def norm_affine(values_in, gain_vec, shift_vec):
    center = values_in - jnp.mean(values_in, axis=-1, keepdims=True)
    spread = jnp.mean(center * center, axis=-1, keepdims=True)
    return center * lax.rsqrt(spread + 1e-06) * gain_vec + shift_vec


def make_per_device(dp, tn):
    everyone = ("dp", "tensor")
    n = dp * tn

    def per_device(
        tokens,
        cotangent,
        ln1_scale,
        ln1_shift,
        w_qkv,
        w_out,
        out_bias,
        ln2_scale,
        ln2_shift,
        w_router,
        w_in,
        b_in,
        w_back,
        b_back,
        choices,
        slots,
    ):
        rows_here, width = tokens.shape
        images = rows_here // SEQ
        experts, blk_d, blk_f = w_in.shape
        ff = blk_f * tn
        dense_blk = w_out.shape[0]
        whole = experts % n == 0
        owners = n if whole else dp
        owned = experts // owners
        expert_axes = ("tensor", "dp") if whole else ("dp",)
        slot_total = experts * CAP
        score_scale = HD ** (-0.5)

        w_pack = jnp.stack([w_in.astype(LOW), jnp.swapaxes(w_back, 1, 2).astype(LOW)], axis=1)
        w_all = lax.all_to_all(w_pack, expert_axes, split_axis=0, concat_axis=0, tiled=True)
        f_parts = tn if whole else 1
        w_all = w_all.reshape(f_parts, dp, owned, 2, blk_d, blk_f)
        w_all = w_all.transpose(3, 2, 1, 4, 0, 5).reshape(2, owned, width, f_parts * blk_f)
        first_w, second_wt = w_all[0], w_all[1]

        vec_rows = jnp.stack([ln1_scale, ln1_shift, out_bias, ln2_scale, ln2_shift])
        pieces = [
            w_qkv.reshape(-1),
            w_out.reshape(-1),
            w_router.reshape(-1),
            b_back.reshape(-1),
            b_in.reshape(-1),
            vec_rows.reshape(-1),
        ]
        sizes = [p.shape[0] for p in pieces]
        total = sum(sizes)
        pad = -total % 512
        packed = jnp.concatenate([p.astype(LOW) for p in pieces] + [jnp.zeros((pad,), LOW)])
        gathered = lax.all_gather(packed.reshape(-1, 512), everyone, axis=0, tiled=False)
        gathered = gathered.reshape(n, -1)
        offs = [sum(sizes[:i]) for i in range(len(sizes))]
        part = [gathered[:, o : o + s] for o, s in zip(offs, sizes)]
        qkv_w = part[0].reshape(n, 3, dense_blk, width).swapaxes(0, 1).reshape(3, width, width)
        out_w = part[1].reshape(width, width)
        router = part[2].reshape(width, experts)
        bias_back = part[3].reshape(n, experts, -1).swapaxes(0, 1).reshape(experts, width)
        bias_back = bias_back.astype(WIDE)
        in_b = part[4].reshape(dp, tn, experts // dp, blk_f).swapaxes(1, 2).reshape(experts, ff)
        vecs = part[5].reshape(n, 5, -1).swapaxes(0, 1).reshape(5, width).astype(WIDE)
        gain_one, shift_one, bias_attn, gain_two, shift_two = vecs
        if whole:
            mine = lax.axis_index("tensor") * dp + lax.axis_index("dp")
            my_b = lax.dynamic_slice(in_b, (mine * owned, 0), (owned, ff)).astype(WIDE)
        else:
            my_b = lax.dynamic_slice(
                in_b,
                (lax.axis_index("dp") * owned, lax.axis_index("tensor") * blk_f),
                (owned, blk_f),
            ).astype(WIDE)

        residual = tokens.astype(WIDE)
        normed_one = norm_affine(residual, gain_one, shift_one).astype(LOW)
        projected = jnp.einsum(
            "td,jde->jte", normed_one, qkv_w, preferred_element_type=WIDE
        ).astype(LOW)
        head_query = projected[0].reshape(images, SEQ, H, HD)
        head_key = projected[1].reshape(images, SEQ, H, HD)
        head_value = projected[2].reshape(images, SEQ, H, HD)
        raw_scores = jnp.einsum(
            "ishd,ithd->ihst", head_query, head_key, preferred_element_type=WIDE
        )
        scaled = raw_scores * score_scale
        row_top = jnp.max(scaled, axis=-1, keepdims=True)
        log_total = row_top + jnp.log(jnp.sum(jnp.exp(scaled - row_top), axis=-1, keepdims=True))
        weights_att = jnp.exp(scaled - log_total).astype(LOW)
        attended = (
            jnp.einsum("ihst,ithd->ishd", weights_att, head_value, preferred_element_type=WIDE)
            .astype(LOW)
            .reshape(rows_here, width)
        )
        attn_sum = jnp.dot(attended, out_w, preferred_element_type=WIDE)
        middle = residual + attn_sum + bias_attn
        normed_two = norm_affine(middle, gain_two, shift_two).astype(LOW)
        route_p = jax.nn.softmax(jnp.dot(normed_two, router, preferred_element_type=WIDE), axis=-1)

        expert_ids = jnp.arange(experts, dtype=jnp.int32)
        chosen = [
            (choices[:, k : k + 1] == expert_ids[None, :]).astype(WIDE) for k in range(2)
        ]
        gate_vals = jnp.concatenate(
            [jnp.sum(route_p * c, axis=1, keepdims=True) for c in chosen], axis=1
        )
        kept_pair = (slots >= 0).astype(WIDE)
        target = jnp.where(slots >= 0, choices * CAP + slots, -1)
        places = jnp.arange(slot_total, dtype=jnp.int32)
        by_slot = [target[:, k][None, :] == places[:, None] for k in range(2)]
        spread_mat = (by_slot[0] | by_slot[1]).astype(LOW)
        by_token = [target[:, k : k + 1] == places[None, :] for k in range(2)]
        pair_weight = gate_vals * kept_pair
        slot_gate = jnp.sum(
            jnp.where(by_slot[0], pair_weight[:, 0][None, :], 0.0)
            + jnp.where(by_slot[1], pair_weight[:, 1][None, :], 0.0),
            axis=1,
            keepdims=True,
        )
        both = jnp.dot(
            spread_mat,
            jnp.concatenate([normed_two, cotangent], axis=1),
            preferred_element_type=WIDE,
        )
        buffer = both[:, :width].astype(LOW).reshape(experts, CAP, width)
        slot_grad = slot_gate * both[:, width:]
        grad_bias_back = jnp.sum(slot_grad.reshape(experts, CAP, width), axis=1)
        slot_grad_low = slot_grad.astype(LOW).reshape(experts, CAP, width)

        def out_to_experts(rows):
            width_c = rows.shape[1]
            if not whole:
                rows = lax.all_gather(rows, "tensor", axis=1, tiled=True)
            rows = lax.all_to_all(rows, expert_axes, split_axis=0, concat_axis=0, tiled=True)
            return rows.reshape(owners, owned, -1, width)

        def back_to_tokens(rows):
            rows = rows.reshape(experts, -1, width)
            rows = lax.all_to_all(rows, expert_axes, split_axis=0, concat_axis=0, tiled=True)
            if not whole:
                rows = lax.psum_scatter(rows, "tensor", scatter_dimension=1, tiled=True)
            return rows

        sent = out_to_experts(jnp.concatenate([buffer, slot_grad_low], axis=1))
        group = sent.shape[2] // (2 * CAP)
        sent = sent.reshape(owners, owned, group, 2, CAP, width).transpose(3, 1, 0, 2, 4, 5)
        sent = sent.reshape(2, owned, owners * group * CAP, width)
        all_slots, slot_grad_all = sent[0], sent[1]

        pre_act = (
            jnp.einsum("ecd,edf->ecf", all_slots, first_w, preferred_element_type=WIDE)
            + my_b[:, None, :]
        )
        hidden, gelu_pull = jax.vjp(lambda member: jax.nn.gelu(member, approximate=True), pre_act)
        hidden = hidden.astype(LOW)
        expert_sum = jnp.einsum("ecf,edf->ecd", hidden, second_wt, preferred_element_type=WIDE)
        grad_hidden = jnp.einsum("ecd,edf->ecf", slot_grad_all, second_wt, preferred_element_type=WIDE)
        grad_pre = gelu_pull(grad_hidden)[0].astype(LOW)
        grad_slots_all = jnp.einsum("ecf,edf->ecd", grad_pre, first_w, preferred_element_type=WIDE)
        returned = jnp.stack([expert_sum.astype(LOW), grad_slots_all.astype(LOW)])
        returned = returned.reshape(2, owned, owners, group, CAP, width).transpose(2, 1, 3, 0, 4, 5)
        returned = returned.reshape(owners * owned, group * 2 * CAP, width)
        home = back_to_tokens(returned).reshape(experts, 2, CAP, width)
        expert_home = home[:, 0].reshape(slot_total, width)
        grad_home = home[:, 1].reshape(slot_total, width)

        grad_first_b = jnp.sum(grad_pre.astype(WIDE), axis=1)
        grad_first_w = jnp.einsum("ecd,ecf->edf", all_slots, grad_pre, preferred_element_type=WIDE)
        grad_second_t = jnp.einsum("ecd,ecf->edf", slot_grad_all, hidden, preferred_element_type=WIDE)
        g_pack = jnp.stack([grad_first_w.astype(LOW), grad_second_t.astype(LOW)])
        g_pack = g_pack.reshape(2, owned, dp, blk_d, f_parts, blk_f).transpose(4, 2, 1, 0, 3, 5)
        g_pack = g_pack.reshape(f_parts * dp * owned, 2, blk_d, blk_f)
        g_home = lax.all_to_all(g_pack, expert_axes, split_axis=0, concat_axis=0, tiled=True)
        g_home = g_home.reshape(experts, 2, blk_d, blk_f).astype(WIDE)
        grad_w_in = g_home[:, 0]
        grad_w_back = jnp.swapaxes(g_home[:, 1], 1, 2)

        picked = []
        for k in range(2):
            rows = jnp.dot(by_token[k].astype(LOW), expert_home, preferred_element_type=WIDE)
            bias_rows = jnp.dot(
                chosen[k].astype(LOW), bias_back.astype(LOW), preferred_element_type=WIDE
            )
            picked.append((rows + bias_rows) * kept_pair[:, k : k + 1])
        result = (
            middle + gate_vals[:, 0:1] * picked[0] + gate_vals[:, 1:2] * picked[1]
        ).astype(LOW)
        grad_out = cotangent.astype(WIDE)
        grad_probs = sum(
            jnp.sum(grad_out * picked[k], axis=1, keepdims=True) * chosen[k] for k in range(2)
        )
        gather_mat = (by_token[0] | by_token[1]).astype(LOW)
        grad_normed_two = jnp.dot(gather_mat, grad_home, preferred_element_type=WIDE)
        grad_logits = route_p * (grad_probs - jnp.sum(grad_probs * route_p, axis=-1, keepdims=True))
        grad_normed_two = grad_normed_two + jnp.dot(
            grad_logits, router.astype(WIDE).T, precision=lax.Precision.HIGHEST
        )
        grad_router = jnp.dot(
            normed_two.astype(WIDE).T, grad_logits, precision=lax.Precision.HIGHEST
        )
        _, pull_two = jax.vjp(norm_affine, middle, gain_two, shift_two)
        grad_mid_norm, grad_gain_two, grad_shift_two = pull_two(grad_normed_two)
        grad_middle = grad_out + grad_mid_norm
        grad_bias_attn = jnp.sum(grad_middle, axis=0)
        grad_mid_low = grad_middle.astype(LOW)
        grad_att = jnp.einsum(
            "td,ed->te", grad_mid_low, out_w, preferred_element_type=WIDE
        ).astype(LOW)
        grad_out_w = jnp.einsum("te,td->ed", attended, grad_mid_low, preferred_element_type=WIDE)
        grad_att_heads = grad_att.reshape(images, SEQ, H, HD)
        probs_again = jnp.exp(
            jnp.einsum("ishd,ithd->ihst", head_query, head_key, preferred_element_type=WIDE)
            * score_scale
            - log_total
        )
        grad_weights = jnp.einsum(
            "ishd,ithd->ihst", grad_att_heads, head_value, preferred_element_type=WIDE
        )
        row_delta = jnp.sum(grad_weights * probs_again, axis=-1, keepdims=True)
        grad_raw = (probs_again * (grad_weights - row_delta) * score_scale).astype(LOW)
        grad_value = jnp.einsum(
            "ihst,ishd->ithd",
            probs_again.astype(LOW),
            grad_att_heads,
            preferred_element_type=WIDE,
        )
        grad_query = jnp.einsum("ihst,ithd->ishd", grad_raw, head_key, preferred_element_type=WIDE)
        grad_key = jnp.einsum("ihst,ishd->ithd", grad_raw, head_query, preferred_element_type=WIDE)
        grad_proj = jnp.stack(
            [
                grad_query.astype(LOW).reshape(rows_here, width),
                grad_key.astype(LOW).reshape(rows_here, width),
                grad_value.astype(LOW).reshape(rows_here, width),
            ]
        )
        grad_qkv_w = jnp.einsum("td,jte->jde", normed_one, grad_proj, preferred_element_type=WIDE)
        grad_normed_one = jnp.einsum("jte,jde->td", grad_proj, qkv_w, preferred_element_type=WIDE)
        _, pull_one = jax.vjp(norm_affine, residual, gain_one, shift_one)
        grad_resid_norm, grad_gain_one, grad_shift_one = pull_one(grad_normed_one)
        grad_tokens = grad_middle + grad_resid_norm

        if whole:
            row_b = jnp.zeros((experts, ff), WIDE)
            row_b = lax.dynamic_update_slice(row_b, grad_first_b, (mine * owned, 0))
        else:
            row_b = jnp.zeros((experts, ff), WIDE)
            row_b = lax.dynamic_update_slice(
                row_b,
                grad_first_b,
                (lax.axis_index("dp") * owned, lax.axis_index("tensor") * blk_f),
            )
        vec_grads = jnp.stack(
            [grad_gain_one, grad_shift_one, grad_bias_attn, grad_gain_two, grad_shift_two]
        )
        out_pieces = [
            grad_qkv_w.reshape(3, n, dense_blk, width).swapaxes(0, 1).reshape(n, -1),
            grad_out_w.reshape(n, -1),
            grad_router.reshape(n, -1),
            grad_bias_back.reshape(experts, n, -1).swapaxes(0, 1).reshape(n, -1),
            row_b.reshape(dp, experts // dp, tn, blk_f).swapaxes(1, 2).reshape(n, -1),
            vec_grads.reshape(5, n, -1).swapaxes(0, 1).reshape(n, -1),
        ]
        out_pack = jnp.concatenate(
            [p.astype(LOW) for p in out_pieces] + [jnp.zeros((n, pad), LOW)], axis=1
        )
        out_all = lax.all_to_all(
            out_pack.reshape(n, -1, 512), everyone, split_axis=0, concat_axis=0, tiled=True
        )
        summed = jnp.sum(out_all.astype(WIDE), axis=0).reshape(-1)
        done = [summed[o : o + s] for o, s in zip(offs, sizes)]
        vec_done = done[5].reshape(5, -1)
        return (
            result,
            grad_tokens,
            vec_done[0],
            vec_done[1],
            done[0].reshape(w_qkv.shape),
            done[1].reshape(w_out.shape),
            vec_done[2],
            vec_done[3],
            vec_done[4],
            done[2].reshape(w_router.shape),
            grad_w_in,
            done[4].reshape(b_in.shape),
            grad_w_back,
            done[3].reshape(b_back.shape),
        )

    return per_device


def solution(mesh):
    everyone = ("dp", "tensor")
    in_specs = (
        P(everyone, None),
        P(everyone, None),
        P(everyone),
        P(everyone),
        P(None, everyone, None),
        P(everyone, None),
        P(everyone),
        P(everyone),
        P(everyone),
        P(everyone, None),
        P(None, "dp", "tensor"),
        P("dp", "tensor"),
        P(None, "tensor", "dp"),
        P(None, everyone),
        P(everyone, None),
        P(everyone, None),
    )
    out_specs = in_specs[:2] + in_specs[2:14]
    return jax.shard_map(
        make_per_device(mesh.shape["dp"], mesh.shape["tensor"]),
        mesh=mesh,
        in_specs=in_specs,
        out_specs=out_specs,
        check_vma=False,
    )
```

```python
import functools

import jax
import jax.numpy as jnp
from jax import lax
from jax.experimental import pallas as pl
from jax.experimental.pallas import tpu as pltpu
from jax.sharding import PartitionSpec as P

H = 8
HD = 64
SEQ = 196
CAP = 65
LOW = jnp.bfloat16
WIDE = jnp.float32


def norm_affine(values_in, gain_vec, shift_vec):
    center = values_in - jnp.mean(values_in, axis=-1, keepdims=True)
    spread = jnp.mean(center * center, axis=-1, keepdims=True)
    return center * lax.rsqrt(spread + 1e-06) * gain_vec + shift_vec


MAIN = CAP - 1
GROUP = 4 * MAIN + 16
WIN = 208
STEP = 192


def dot(a, b, dims=((1,), (0,))):
    return lax.dot_general(a, b, (dims, ((), ())), preferred_element_type=WIDE)


NT = ((1,), (1,))
TN = ((0,), (0,))
MESH = pl.DeviceIdType.MESH


def to_tiles(pieces):
    m = pieces[0].shape[0]
    gap = iota((8 * m, m), 0) - 8 * iota((8 * m, m), 1)
    return sum(
        dot(jnp.where(gap == c, 1.0, 0.0).astype(LOW), piece) for c, piece in enumerate(pieces)
    )


def from_tiles(tiles, c, rows):
    gap = iota((rows, tiles.shape[0]), 1) - 8 * iota((rows, tiles.shape[0]), 0)
    return dot(jnp.where(gap == c, 1.0, 0.0).astype(LOW), tiles)


def lane_blocks(v):
    return [v[:, c * 128 : (c + 1) * 128] for c in range(v.shape[1] // 128)]


def split_two(v):
    high = v.astype(LOW)
    return high, (v - high.astype(WIDE)).astype(LOW)


def iota(shape, dim):
    return lax.broadcasted_iota(jnp.int32, shape, dim)


def normalize(v):
    center = v - jnp.mean(v, axis=-1, keepdims=True)
    rstd = lax.rsqrt(jnp.mean(center * center, axis=-1, keepdims=True) + 1e-06)
    return center * rstd, rstd


def norm_back(grad, xhat, rstd, gain):
    inner = grad * gain
    return rstd * (
        inner
        - jnp.mean(inner, axis=-1, keepdims=True)
        - xhat * jnp.mean(inner * xhat, axis=-1, keepdims=True)
    )


def layer_kernel(
    dp, images, experts, tok_ref, cot_ref, choice_ref, slot_ref, gain_one_ref, shift_one_ref,
    bias_ref, gain_two_ref, shift_two_ref, wqkv_ref, wout_ref, router_ref, bback_ref, bin_ref,
    win_ref, wback_ref,
    out_ref, grad_ref, tail_out, dense_out, qkv_out, att_out, lse_out, mid_out, two_out, route_out,
    col_out, dfirst_out, dsecond_out, db_ref,
    dense_ref, lse_ref, mid_ref, route_ref, col_ref, shard_ref, rows_ref,
    wide_ref, low_first, low_second, first_ref, second_ref, b_ref,
    x_ref, g_ref, xs_ref, sg_ref, hid_ref, pre_ref, backs_ref,
    tails_ref, last_ref, x_tiles, g_tiles, xs_tiles, gs_tiles, home_tiles,
    stage_sem, w_send, w_recv, g_send, g_recv, x_send, x_recv, r_send, r_recv,
    t_send, t_recv, c_send, c_recv, s_send, s_recv, a_sems, own_sem, save_sem,
):
    outs_ref = g_ref
    total, width = g_ref.shape
    rows = tok_ref.shape[0]
    qkv_ref = pre_ref.at[0:rows, 0 : 3 * width]
    att_ref = pre_ref.at[0:rows, 3 * width : 4 * width]
    two_ref = hid_ref.at[0:rows, 0:width]
    n = total // MAIN
    tn = n // dp
    parts, _, half = first_ref.shape
    blk_d = low_first.shape[1]
    dense_blk = shard_ref.shape[0]
    groups = n // 4
    per = GROUP
    t_here, d_here = lax.axis_index("tensor"), lax.axis_index("dp")
    me = t_here * dp + d_here
    my_group, my_place = me // 4, me % 4
    core, y_here, z_here = d_here % 2, (d_here // 2) % 2, d_here // 4
    spots, layers = 2 * tn, dp // 4
    spot = y_here * tn + t_here

    def device(p):
        return (p % dp, p // dp)

    def block(p):
        return pl.ds(pl.multiple_of(p * MAIN, 16), MAIN)

    def landing(p):
        return pl.ds(pl.multiple_of(p // 4 * GROUP + p % 4 * MAIN, 16), MAIN)

    tiles = ((x_tiles, xs_tiles), (g_tiles, gs_tiles), (home_tiles, tail_out))

    def tile(which, p, source):
        src, dst = tiles[which]
        return pltpu.make_async_remote_copy(
            src_ref=src.at[p], dst_ref=dst.at[source],
            send_sem=t_send.at[which, p], recv_sem=t_recv.at[which, source],
            device_id=device(p), device_id_type=MESH,
        )

    def own_tile(which):
        src, dst = tiles[which]
        return pltpu.make_async_copy(src.at[me], dst.at[me], own_sem.at[7 + which])

    def weight_rows(p):
        return pl.ds(pl.multiple_of((p % dp) * blk_d, 16), blk_d)

    def weights(which, p, source):
        src, dst = ((low_first, first_ref), (low_second, second_ref))[which]
        return pltpu.make_async_remote_copy(
            src_ref=src.at[p], dst_ref=dst.at[source // dp, weight_rows(source)],
            send_sem=w_send.at[which, p], recv_sem=w_recv.at[which, source],
            device_id=device(p), device_id_type=MESH,
        )

    def own_weights(which):
        src, dst = ((low_first, first_ref), (low_second, second_ref))[which]
        return pltpu.make_async_copy(
            src.at[me], dst.at[t_here, weight_rows(me)], own_sem.at[3 + which]
        )

    def rows_of(which, p, source):
        src, dst, send, recv = (
            (x_ref, xs_ref, x_send, x_recv), (g_ref, sg_ref, g_send, g_recv)
        )[which]
        return pltpu.make_async_remote_copy(
            src_ref=src.at[block(p)], dst_ref=dst.at[landing(source)],
            send_sem=send.at[p], recv_sem=recv.at[source],
            device_id=device(p), device_id_type=MESH,
        )

    def home(which, p, source):
        src, dst = ((outs_ref, out_ref), (backs_ref, grad_ref))[which]
        return pltpu.make_async_remote_copy(
            src_ref=src.at[block(p)], dst_ref=dst.at[block(source)],
            send_sem=r_send.at[which, p], recv_sem=r_recv.at[which, source],
            device_id=device(p), device_id_type=MESH,
        )

    def own(which):
        src, dst = (
            (x_ref, xs_ref), (outs_ref, out_ref), (backs_ref, grad_ref),
            None, None, (g_ref, sg_ref),
        )[which]
        place = block(me) if which in (1, 2) else landing(me)
        return pltpu.make_async_copy(src.at[block(me)], dst.at[place], own_sem.at[which])

    def to_layer(z, source):
        return pltpu.make_async_remote_copy(
            src_ref=shard_ref, dst_ref=dense_ref.at[source, y_here, core, t_here],
            send_sem=c_send.at[z], recv_sem=c_recv.at[source],
            device_id=((z * 2 + y_here) * 2 + core, t_here), device_id_type=MESH,
        )

    def to_spot(s, source):
        return pltpu.make_async_remote_copy(
            src_ref=dense_ref.at[:, y_here, core, t_here],
            dst_ref=dense_ref.at[:, source // tn, core, source % tn],
            send_sem=s_send.at[s], recv_sem=s_recv.at[source],
            device_id=((z_here * 2 + s // tn) * 2 + core, s % tn), device_id_type=MESH,
        )

    def to_core(source):
        return pltpu.make_async_remote_copy(
            src_ref=dense_ref.at[:, :, core], dst_ref=dense_ref.at[:, :, source],
            send_sem=a_sems.at[0], recv_sem=a_sems.at[1],
            device_id=(d_here + 1 - 2 * core, t_here), device_id_type=MESH,
        )

    own_shard = pltpu.make_async_copy(
        shard_ref, dense_ref.at[z_here, y_here, core, t_here], own_sem.at[6]
    )
    pieces = wide_ref.shape[1]
    chunks = n // pieces

    def stage(which, j):
        src = (win_ref, wback_ref)[which]
        c = (me // pieces + j) % chunks
        return pltpu.make_async_copy(
            src.at[pl.ds(c * pieces, pieces)], wide_ref.at[j % 2], stage_sem.at[j % 2]
        )

    barrier = pltpu.get_barrier_semaphore()

    @pl.loop(1, n)
    def _(r):
        pl.semaphore_signal(barrier, inc=1, device_id=device((me + r) % n), device_id_type=MESH)

    stage(0, 0).start()
    for j in range(3):
        shard_ref[:, j * width : (j + 1) * width] = wqkv_ref[j].astype(LOW)
    shard_ref[:, 3 * width : 4 * width] = wout_ref[...].astype(LOW)
    diagonal = iota((dense_blk, dense_blk), 0) == iota((dense_blk, dense_blk), 1)
    lanes = iota((1, 128), 1)
    spread = iota((experts, 128), 1) - iota((experts, 128), 0)
    misc = dot(router_ref[...].astype(LOW), jnp.where(spread == 0, 1.0, 0.0).astype(LOW))
    misc = misc + dot(
        bback_ref[...].astype(LOW), jnp.where(spread == experts, 1.0, 0.0).astype(LOW)
    )
    vectors = (gain_one_ref, shift_one_ref, bias_ref, gain_two_ref, shift_two_ref)
    for i, vec in enumerate(vectors):
        column = jnp.sum(jnp.where(diagonal, vec[...], 0.0), axis=1, keepdims=True)
        misc = jnp.where(lanes == 64 + i, column, misc)
    shard_ref[:, 4 * width : 4 * width + 128] = misc.astype(LOW)
    lines = half // 128
    slab = jnp.zeros((dense_blk, 128), WIDE)
    for i in range(dense_blk):
        part = bin_ref[i // lines : i // lines + 1, (i % lines) * 128 : (i % lines + 1) * 128]
        slab = jnp.where(iota((dense_blk, 1), 0) == i, part, slab)
    shard_ref[:, 4 * width + 128 : 4 * width + 256] = slab.astype(LOW)
    slot_in = slot_ref[...]
    rows_ref[...] = jnp.where(
        (slot_in >= 0) & (slot_in < MAIN), choice_ref[...] * MAIN + slot_in, -1
    )
    last_ref[...] = jnp.where(slot_in == MAIN, choice_ref[...], -1)
    pick = iota((2, 128), 1) - iota((2, 128), 0)
    turned = dot(
        choice_ref[...].astype(WIDE).astype(LOW), jnp.where(pick == 0, 1.0, 0.0).astype(LOW), TN
    ) + dot(slot_ref[...].astype(WIDE).astype(LOW), jnp.where(pick == 2, 1.0, 0.0).astype(LOW), TN)
    col_ref[...] = turned.astype(jnp.int32)
    own_shard.start()
    db_ref[...] = jnp.zeros_like(db_ref)
    pl.semaphore_wait(barrier, n - 1)
    for i in range(1, layers):
        to_layer((z_here + i) % layers, z_here).start()

    def send_weights(which):
        low = (low_first, low_second)[which]
        for j in range(chunks):
            if j + 1 < chunks:
                stage(which, j + 1).start()
            elif which == 0:
                stage(1, 0).start()
            stage(which, j).wait()
            c = (me // pieces + j) % chunks
            low[pl.ds(c * pieces, pieces)] = wide_ref[j % 2].astype(LOW)

            @pl.loop(0, pieces)
            def _(i):
                p = c * pieces + (me + i) % pieces

                @pl.when(p != me)
                def _():
                    weights(which, p, me).start()

        own_weights(which).start()

    send_weights(0)
    own_shard.wait()
    for i in range(1, layers):
        z = (z_here + i) % layers
        to_layer(z, z).wait_recv()
    for i in range(1, spots):
        to_spot((spot + i) % spots, spot).start()
    send_weights(1)

    some = 8
    big = some * MAIN
    place = iota((n, rows), 0)
    last_hit = (place == last_ref[0:1, :]) | (place == last_ref[1:2, :])
    tails_ref[...] = jnp.where(last_hit, 1.0, 0.0).astype(LOW)
    got = dot(tails_ref[...], cot_ref[...]).astype(LOW)
    g_tiles[...] = to_tiles(lane_blocks(got)).reshape(n, 8, 128).astype(LOW)

    @pl.loop(0, n // some)
    def _(j):
        c = (me // some + j) % (n // some)
        place = iota((big, rows), 0) + c * big
        hit = (place == rows_ref[0:1, :]) | (place == rows_ref[1:2, :])
        got = dot(jnp.where(hit, 1.0, 0.0).astype(LOW), cot_ref[...])
        g_ref[pl.ds(pl.multiple_of(c * big, 16), big), :] = got.astype(LOW)

        @pl.loop(0, some)
        def _(i):
            p = c * some + (me + i) % some

            @pl.when(p != me)
            def _():
                rows_of(1, p, me).start()
                tile(1, p, me).start()

    own(5).start()
    own_tile(1).start()
    for i in range(1, spots):
        s = (spot + i) % spots
        to_spot(s, s).wait_recv()
    to_core(core).start()
    to_core(1 - core).wait_recv()

    def dense(cols):
        return dense_ref[:, :, :, :, :, cols].reshape(width, -1)

    misc = dense(slice(4 * width, 4 * width + 128))
    misc_t = misc.astype(WIDE).T
    gain_one, shift_one, bias, gain_two, shift_two = [
        misc_t[64 + i : 65 + i, :] for i in range(5)
    ]
    base = tok_ref[...].astype(WIDE)
    xhat, _ = normalize(base)
    one = (xhat * gain_one + shift_one).astype(LOW)
    for j in range(3):
        cols = slice(j * width, (j + 1) * width)
        qkv_ref[:, cols] = dot(one, dense(cols)).astype(LOW)
    att_ref[...] = jnp.zeros((rows, width), LOW)
    lse_ref[...] = jnp.zeros_like(lse_ref)
    low_half = iota((1, 128), 1) < HD

    @pl.loop(0, images)
    def _(i):
        win = pl.ds(pl.multiple_of(i * STEP, 16), WIN)
        first = i * (SEQ - STEP)
        key_pos = iota((1, WIN), 1)
        key_ok = (key_pos >= first) & (key_pos < first + SEQ)
        row_pos = iota((WIN, 1), 0)
        row_ok = (row_pos >= first) & (row_pos < first + SEQ)
        lse = jnp.zeros((WIN, 128), WIDE)
        for pair in range(H // 2):
            q = qkv_ref[win, pair * 128 : (pair + 1) * 128]
            k = qkv_ref[win, width + pair * 128 : width + (pair + 1) * 128]
            v = qkv_ref[win, 2 * width + pair * 128 : 2 * width + (pair + 1) * 128]
            outs = []
            for side in range(2):
                mask = low_half if side == 0 else jnp.logical_not(low_half)
                qm = jnp.where(mask, q, jnp.zeros_like(q))
                s = jnp.where(key_ok, dot(qm, k, NT) * HD**-0.5, -1e30)
                top = jnp.max(s, axis=-1, keepdims=True)
                p = jnp.exp(s - top)
                all_p = jnp.sum(p, axis=-1, keepdims=True)
                p = (p / all_p).astype(LOW)
                outs.append(dot(p, v))
                lane = iota((1, 128), 1) == 2 * pair + side
                lse = jnp.where(lane, top + jnp.log(all_p), lse)
            got = jnp.where(low_half, outs[0], outs[1]).astype(LOW)
            cols = slice(pair * 128, (pair + 1) * 128)
            att_ref[win, cols] = jnp.where(row_ok, got, att_ref[win, cols])
        lse_ref[win, :] = jnp.where(row_ok, lse, lse_ref[win, :])

    mid = base + dot(att_ref[...], dense(slice(3 * width, 4 * width))) + bias
    mid_ref[...] = mid
    xhat, _ = normalize(mid)
    two = (xhat * gain_two + shift_two).astype(LOW)
    two_ref[...] = two
    lanes = iota((1, 128), 1)
    logits = jnp.where(lanes < experts, dot(two, misc), -1e30)
    route = jnp.exp(logits - jnp.max(logits, axis=-1, keepdims=True))
    route = route / jnp.sum(route, axis=-1, keepdims=True)
    route_ref[...] = route
    high, low = jnp.zeros((128, 128), WIDE), jnp.zeros((128, 128), WIDE)
    for k in range(2):
        chosen = lanes == col_ref[:, k : k + 1]
        gate = jnp.where(chosen, route, 0.0)
        here = jnp.where(lanes == col_ref[:, 2 + k : 3 + k], 1.0, 0.0).astype(LOW)
        part_high, part_low = split_two(gate)
        high = high + dot(part_high, here, TN)
        low = low + dot(part_low, here, TN)
    last = lane_blocks(dot(tails_ref[...], two_ref[...]).astype(LOW))
    last = last + [high[:experts].astype(LOW), low[:experts].astype(LOW)]
    x_tiles[...] = to_tiles(last).reshape(n, 8, 128).astype(LOW)

    @pl.loop(0, n // some)
    def _(c):
        place = iota((big, rows), 0) + c * big
        hit = (place == rows_ref[0:1, :]) | (place == rows_ref[1:2, :])
        got = dot(jnp.where(hit, 1.0, 0.0).astype(LOW), two_ref[...])
        x_ref[pl.ds(pl.multiple_of(c * big, 16), big), :] = got.astype(LOW)

    def others(j, action):
        for i in range(4):
            if isinstance(j, int) and j == 0:
                if i > 0:
                    action(4 * my_group + (my_place + i) % 4)
            else:
                action(4 * ((my_group + groups + j) % groups) + (my_place + i) % 4)

    def send_slots(p):
        tile(0, p, me).start()
        rows_of(0, p, me).start()

    own(0).start()
    own_tile(0).start()
    others(0, send_slots)

    @pl.loop(1, groups)
    def _(j):
        others(groups - j, send_slots)

    saved = (
        (dense_ref, dense_out), (qkv_ref, qkv_out), (att_ref, att_out), (lse_ref, lse_out),
        (mid_ref, mid_out), (two_ref, two_out), (route_ref, route_out), (col_ref, col_out),
        (low_first, dfirst_out), (low_second, dsecond_out),
    )

    def save(i):
        return pltpu.make_async_copy(saved[i][0], saved[i][1], save_sem.at[i])

    for i in range(8):
        save(i).start()

    per_dp = experts // dp
    for f in range(parts):
        place = me // per_dp
        slab = dense_ref[
            place // 4, (place // 2) % 2, place % 2, f, :, 4 * width + 128 : 4 * width + 256
        ].astype(WIDE)
        lines = dense_blk // per_dp
        mine = slab[:lines]
        for i in range(1, per_dp):
            mine = jnp.where(me % per_dp == i, slab[i * lines : (i + 1) * lines], mine)
        for i in range(lines):
            b_ref[:, f * half + i * 128 : f * half + (i + 1) * 128] = mine[i : i + 1]

    for i in range(8):
        save(i).wait()
    own_weights(0).wait()
    own_weights(1).wait()
    own(5).wait()
    own_tile(1).wait()

    @pl.loop(1, n)
    def _(r):
        p = (me + r) % n
        for which in range(2):
            weights(which, p, p).wait_recv()
            weights(which, p, me).wait_send()
        rows_of(1, p, me).wait_send()

    place = iota((per, 1), 0)
    sender = jnp.where(place < 4 * MAIN, place // MAIN, place - 4 * MAIN)
    slot_at = jnp.where(place < 4 * MAIN, place % MAIN, MAIN)

    def flat(ref, group):
        return ref[pl.ds(4 * group, 4)].astype(WIDE).reshape(32, 128).astype(LOW)

    def compute(group):
        here = pl.ds(pl.multiple_of(group * per, 16), per)
        tail = pl.ds(pl.multiple_of(group * per + 4 * MAIN, 16), 16)
        x_last, g_last = flat(xs_tiles, group), flat(gs_tiles, group)
        for c in range(width // 128):
            cols = slice(c * 128, (c + 1) * 128)
            xs_ref[tail, cols] = from_tiles(x_last, c, 16).astype(LOW)
            sg_ref[tail, cols] = from_tiles(g_last, c, 16).astype(LOW)
        gates = from_tiles(x_last, width // 128, 16) + from_tiles(x_last, width // 128 + 1, 16)
        x = xs_ref[here, :]
        lanes = iota((1, 128), 1)
        gate = jnp.zeros((per, 1), WIDE)
        for s in range(4):
            got = jnp.sum(jnp.where(lanes == slot_at, gates[s : s + 1], 0.0), axis=1, keepdims=True)
            gate = jnp.where(sender == s, got, gate)
        sg = (gate * sg_ref[here, :].astype(WIDE)).astype(LOW)
        sg_ref[here, :] = sg
        out = jnp.zeros((per, width), WIDE)
        back = jnp.zeros((per, width), WIDE)
        for f in range(parts):
            cols = slice(f * half, (f + 1) * half)
            pre = dot(x, first_ref[f]) + b_ref[:, cols]
            t = jnp.tanh(0.7978845608028654 * (pre + 0.044715 * (pre * pre * pre)))
            hid = (0.5 * pre * (1.0 + t)).astype(LOW)
            slope = 0.5 * (1.0 + t) + (0.5 * pre) * (1.0 - t * t) * (
                0.7978845608028654 * (1.0 + 0.134145 * (pre * pre))
            )
            hid_ref[here, cols] = hid
            out = out + dot(hid, second_ref[f], NT)
            gp = (dot(sg, second_ref[f]) * slope).astype(LOW)
            pre_ref[here, cols] = gp
            db_ref[:, cols] += jnp.sum(gp.astype(WIDE), axis=0, keepdims=True)
            back = back + dot(gp, first_ref[f], NT)
        out, back = out.astype(LOW), back.astype(LOW)
        main = pl.ds(pl.multiple_of(group * 4 * MAIN, 16), 4 * MAIN)
        outs_ref[main, :] = out[: 4 * MAIN]
        backs_ref[main, :] = back[: 4 * MAIN]
        made = to_tiles(lane_blocks(out[4 * MAIN :]) + lane_blocks(back[4 * MAIN :]))
        home_tiles[pl.ds(4 * group, 4)] = made[:32].reshape(4, 8, 128).astype(LOW)

    def send_home(j):
        def both(p):
            home(0, p, me).start()
            home(1, p, me).start()
            tile(2, p, me).start()

        others(j, both)

    def arrived(p):
        for which in range(2):
            rows_of(which, p, p).wait_recv()
            tile(which, p, p).wait_recv()

    own(0).wait()
    own_tile(0).wait()
    others(0, arrived)
    compute(my_group)
    own(1).start()
    own(2).start()
    own_tile(2).start()
    send_home(0)

    @pl.loop(1, groups)
    def _(j):
        others(j, arrived)
        compute((my_group + j) % groups)
        send_home(j)

    for f in range(parts):
        mine = slice(f * dp, (f + 1) * dp)
        for q in range(half // 256):
            cols = slice(f * half + q * 256, f * half + (q + 1) * 256)
            sub = slice(q * 256, (q + 1) * 256)
            low_first[mine, :, sub] = (
                dot(xs_ref[...], pre_ref[:, cols], TN).astype(LOW).reshape(dp, blk_d, 256)
            )
            low_second[mine, :, sub] = (
                dot(sg_ref[...], hid_ref[:, cols], TN).astype(LOW).reshape(dp, blk_d, 256)
            )
    save(8).start()
    save(9).start()
    save(8).wait()
    save(9).wait()
    own(1).wait()
    own(2).wait()
    own_tile(2).wait()
    to_core(core).wait_send()
    for i in range(1, spots):
        to_spot((spot + i) % spots, spot).wait_send()
    for i in range(1, layers):
        to_layer((z_here + i) % layers, z_here).wait_send()

    @pl.loop(1, n)
    def _(r):
        p = (me + r) % n
        rows_of(0, p, me).wait_send()
        for which in range(2):
            home(which, p, me).wait_send()
            home(which, p, p).wait_recv()
        for which in range(3):
            tile(which, p, me).wait_send()
        tile(2, p, p).wait_recv()


def backward_kernel(
    dp, images, experts, tok_in, cot_in, dense_in, qkv_in, att_in, lse_in, mid_in,
    two_in, route_in, col_in, out_in, grad_in, tiles_in, db_ref, dfirst_ref, dsecond_ref,
    result_ref, dtok_ref, done_ref, gin_ref, gback_ref,
    tok_ref, cot_ref, dense_ref, qkv_ref, att_ref, lse_ref, mid_ref,
    two_ref, route_ref, col_ref, out_ref, grad_ref, tiles_ref, in_sem,
    dmid_ref, datt_ref, dqkv_ref, ddense_ref, got_a, sum_a, got_b, sum_b, got_c,
    w_send, w_recv, own_sem, a_sems, b_send, b_recv, c_send, c_recv,
):
    rows, width = tok_ref.shape
    n = dfirst_ref.shape[0]
    tn = n // dp
    t_here, d_here = lax.axis_index("tensor"), lax.axis_index("dp")
    me = t_here * dp + d_here
    core, y_here, z_here = d_here % 2, (d_here // 2) % 2, d_here // 4
    spots, layers = 2 * tn, dp // 4
    spot = y_here * tn + t_here

    def device(p):
        return (p % dp, p // dp)

    def grads_to(which, p):
        src, dst = ((dfirst_ref, gin_ref), (dsecond_ref, gback_ref))[which]
        return pltpu.make_async_remote_copy(
            src_ref=src.at[p], dst_ref=dst.at[me],
            send_sem=w_send.at[which, p], recv_sem=w_recv.at[which, me],
            device_id=device(p), device_id_type=MESH,
        )

    def grads_from(which, p):
        src, dst = ((dfirst_ref, gin_ref), (dsecond_ref, gback_ref))[which]
        return pltpu.make_async_remote_copy(
            src_ref=src.at[p], dst_ref=dst.at[p],
            send_sem=w_send.at[which, p], recv_sem=w_recv.at[which, p],
            device_id=device(p), device_id_type=MESH,
        )

    def own(which):
        src, dst = ((dfirst_ref, gin_ref), (dsecond_ref, gback_ref))[which]
        return pltpu.make_async_copy(src.at[me], dst.at[me], own_sem.at[which])

    def to_spot(s):
        return pltpu.make_async_remote_copy(
            src_ref=sum_a.at[:, s], dst_ref=got_b.at[spot],
            send_sem=b_send.at[s], recv_sem=b_recv.at[spot],
            device_id=((z_here * 2 + s // tn) * 2 + core, s % tn), device_id_type=MESH,
        )

    def from_spot(s):
        return pltpu.make_async_remote_copy(
            src_ref=sum_a.at[:, s], dst_ref=got_b.at[s],
            send_sem=b_send.at[s], recv_sem=b_recv.at[s],
            device_id=((z_here * 2 + s // tn) * 2 + core, s % tn), device_id_type=MESH,
        )

    def to_layer(z):
        return pltpu.make_async_remote_copy(
            src_ref=sum_b.at[z], dst_ref=got_c.at[z_here],
            send_sem=c_send.at[z], recv_sem=c_recv.at[z_here],
            device_id=((z * 2 + y_here) * 2 + core, t_here), device_id_type=MESH,
        )

    def from_layer(z):
        return pltpu.make_async_remote_copy(
            src_ref=sum_b.at[z], dst_ref=got_c.at[z],
            send_sem=c_send.at[z], recv_sem=c_recv.at[z],
            device_id=((z * 2 + y_here) * 2 + core, t_here), device_id_type=MESH,
        )

    slots_main = out_in.shape[0]
    moves = (
        (out_in, out_ref.at[0:slots_main]), (grad_in, grad_ref.at[0:slots_main]),
        (tiles_in, tiles_ref), (cot_in, cot_ref), (route_in, route_ref), (mid_in, mid_ref),
        (col_in, col_ref), (two_in, two_ref), (dense_in, dense_ref), (att_in, att_ref),
        (qkv_in, qkv_ref), (lse_in, lse_ref), (tok_in, tok_ref),
    )

    def bring(i):
        return pltpu.make_async_copy(moves[i][0], moves[i][1], in_sem.at[i])

    barrier = pltpu.get_barrier_semaphore()

    @pl.loop(1, n)
    def _(r):
        pl.semaphore_signal(barrier, inc=1, device_id=device((me + r) % n), device_id_type=MESH)

    for i in range(len(moves)):
        bring(i).start()
    pl.semaphore_wait(barrier, n - 1)

    @pl.loop(1, n)
    def _(r):
        grads_to(0, (me + r) % n).start()

    @pl.loop(1, 3 * n // 8)
    def _(r):
        grads_to(1, (me + r) % n).start()

    own(0).start()
    own(1).start()

    def put(cols, val):
        ddense_ref[:, :, :, cols] = val.reshape(ddense_ref.shape[:3] + (-1,)).astype(LOW)

    for i in range(len(moves)):
        bring(i).wait()
    tiles = tiles_ref[...].astype(WIDE).reshape(8 * n, 128).astype(LOW)
    rest = out_ref.shape[0] - slots_main
    for c in range(width // 128):
        cols = slice(c * 128, (c + 1) * 128)
        out_ref[slots_main:, cols] = from_tiles(tiles, c, rest).astype(LOW)
        grad_ref[slots_main:, cols] = from_tiles(tiles, width // 128 + c, rest).astype(LOW)

    misc_t = dense_ref[:, 4 * width : 4 * width + 128].astype(WIDE).T
    misc_low = misc_t.astype(LOW)
    gain_one, shift_one, bias, gain_two, shift_two = [
        misc_t[64 + i : 65 + i, :] for i in range(5)
    ]
    lanes = iota((1, 128), 1)
    per = 112
    slots_all = out_ref.shape[0]

    def chunk(c, carry):
        d_router, d_bias_back, d_gain, d_shift, d_bias = carry
        here = pl.ds(pl.multiple_of(c * per, 16), per)
        g = cot_ref[here, :]
        gw = g.astype(WIDE)
        route = route_ref[here, :]
        mid = mid_ref[here, :]
        result = mid
        probs = jnp.zeros((per, 128), WIDE)
        gate_sel = jnp.zeros((per, 128), WIDE)
        both = jnp.zeros((per, slots_all), WIDE)
        for k in range(2):
            choice = col_ref[here, k : k + 1]
            slot = col_ref[here, 2 + k : 3 + k]
            kept = slot >= 0
            chosen = (lanes == choice) & kept
            where_to = jnp.where(slot < MAIN, choice * MAIN + slot, slots_main + choice)
            where_to = jnp.where(kept, where_to, -1)
            hit = jnp.where(iota((per, slots_all), 1) == where_to, 1.0, 0.0)
            both = both + hit
            add_b = jnp.where((lanes == choice + experts) & kept, 1.0, 0.0).astype(LOW)
            picked = dot(hit.astype(LOW), out_ref[...]) + dot(add_b, misc_low)
            gate = jnp.sum(jnp.where(chosen, route, 0.0), axis=1, keepdims=True)
            result = result + gate * picked
            gg = jnp.sum(gw * picked, axis=1, keepdims=True)
            probs = probs + jnp.where(chosen, gg, 0.0)
            gate_sel = gate_sel + jnp.where(chosen, route, 0.0)
        result_ref[here, :] = result.astype(LOW)
        logits = route * (probs - jnp.sum(probs * route, axis=-1, keepdims=True))
        high, low = split_two(logits)
        d_two = dot(both.astype(LOW), grad_ref[...]) + dot(high, misc_low) + dot(low, misc_low)
        two = two_ref[here, :]
        d_router = d_router + dot(high, two, TN) + dot(low, two, TN)
        gs_high, gs_low = split_two(gate_sel)
        d_bias_back = d_bias_back + dot(gs_high, g, TN) + dot(gs_low, g, TN)
        xhat, rstd = normalize(mid)
        d_gain = d_gain + jnp.sum(d_two * xhat, axis=0, keepdims=True)
        d_shift = d_shift + jnp.sum(d_two, axis=0, keepdims=True)
        d_mid = gw + norm_back(d_two, xhat, rstd, gain_two)
        d_bias = d_bias + jnp.sum(d_mid, axis=0, keepdims=True)
        dtok_ref[here, :] = d_mid
        dmid_ref[here, :] = d_mid.astype(LOW)
        return d_router, d_bias_back, d_gain, d_shift, d_bias

    zero = jnp.zeros((1, width), WIDE)
    wide_zero = jnp.zeros((128, width), WIDE)
    d_router, d_bias_back, d_gain_two, d_shift_two, d_bias = lax.fori_loop(
        0, rows // per, chunk, (wide_zero, wide_zero, zero, zero, zero)
    )
    out_cols = slice(3 * width, 4 * width)
    datt_ref[...] = dot(dmid_ref[...], dense_ref[:, out_cols], NT).astype(LOW)
    put(out_cols, dot(att_ref[...], dmid_ref[...], TN))
    dqkv_ref[...] = jnp.zeros_like(dqkv_ref)
    low_half = iota((1, 128), 1) < HD

    @pl.loop(0, images)
    def _(i):
        win = pl.ds(pl.multiple_of(i * STEP, 16), WIN)
        first = i * (SEQ - STEP)
        key_pos = iota((1, WIN), 1)
        key_ok = (key_pos >= first) & (key_pos < first + SEQ)
        row_pos = iota((WIN, 1), 0)
        row_ok = (row_pos >= first) & (row_pos < first + SEQ)
        lse = lse_ref[win, :]
        for pair in range(H // 2):
            cols = [
                slice(j * width + pair * 128, j * width + (pair + 1) * 128) for j in range(3)
            ]
            q, k, v = [qkv_ref[win, c] for c in cols]
            do = datt_ref[win, pair * 128 : (pair + 1) * 128]
            do = jnp.where(row_ok, do, jnp.zeros_like(do))
            dq, dk, dv = [jnp.zeros((WIN, 128), WIDE) for _ in range(3)]
            for half in range(2):
                mask = low_half if half == 0 else jnp.logical_not(low_half)
                qm, km, dom = [jnp.where(mask, a, jnp.zeros_like(a)) for a in (q, k, do)]
                h = 2 * pair + half
                s = dot(qm, k, NT) * HD**-0.5
                p = jnp.where(key_ok & row_ok, jnp.exp(jnp.minimum(s - lse[:, h : h + 1], 0.0)), 0.0)
                dp = dot(dom, v, NT)
                delta = jnp.sum(dp * p, axis=-1, keepdims=True)
                ds = (p * (dp - delta) * HD**-0.5).astype(LOW)
                dv = dv + dot(p.astype(LOW), dom, TN)
                dq = dq + dot(ds, km)
                dk = dk + dot(ds, qm, TN)
            for c, val in zip(cols, (dq, dk, dv)):
                dqkv_ref[win, c] = jnp.where(row_ok, val.astype(LOW), dqkv_ref[win, c])

    xhat, rstd = normalize(tok_ref[...].astype(WIDE))
    one = (xhat * gain_one + shift_one).astype(LOW)
    d_one = jnp.zeros((rows, width), WIDE)
    for j in range(3):
        cols = slice(j * width, (j + 1) * width)
        put(cols, dot(one, dqkv_ref[:, cols], TN))
        d_one = d_one + dot(dqkv_ref[:, cols], dense_ref[:, cols], NT)
    d_gain_one = jnp.sum(d_one * xhat, axis=0, keepdims=True)
    d_shift_one = jnp.sum(d_one, axis=0, keepdims=True)
    dtok_ref[...] = dtok_ref[...] + norm_back(d_one, xhat, rstd, gain_one)
    row = iota((128, 1), 0)
    grads = jnp.where(row < experts, d_router, 0.0)
    moved = jnp.concatenate([d_bias_back[128 - experts :], d_bias_back[: 128 - experts]], axis=0)
    grads = grads + jnp.where((row >= experts) & (row < 2 * experts), moved, 0.0)
    for i, vec in enumerate((d_gain_one, d_shift_one, d_bias, d_gain_two, d_shift_two)):
        grads = grads + jnp.where(row == 64 + i, vec, 0.0)
    put(slice(4 * width, 4 * width + 128), grads.T)
    per_dp = experts // dp
    lines = ddense_ref.shape[2] // tn // per_dp
    count = tn * lines
    line = iota((count, 1), 0)
    slab = jnp.zeros((count, 128), WIDE)
    for i in range(count):
        slab = jnp.where(line == i, db_ref[:, i * 128 : (i + 1) * 128], slab)
    line = iota((width, count), 1)
    place = (me // per_dp * tn + line // lines) * (lines * per_dp) + me % per_dp * lines + line % lines
    placed = jnp.where(iota((width, count), 0) == place, 1.0, 0.0).astype(LOW)
    put(slice(4 * width + 128, 4 * width + 256), dot(placed, slab.astype(LOW)))

    partner = pltpu.make_async_remote_copy(
        src_ref=ddense_ref.at[:, 1 - core], dst_ref=got_a,
        send_sem=a_sems.at[0], recv_sem=a_sems.at[1],
        device_id=(d_here + 1 - 2 * core, t_here), device_id_type=MESH,
    )
    partner.start()
    partner.wait()
    total = ddense_ref[:, core].astype(WIDE) + got_a[...].astype(WIDE)
    sum_a[...] = total.reshape(sum_a.shape).astype(LOW)
    for i in range(1, spots):
        to_spot((spot + i) % spots).start()

    @pl.loop(3 * n // 8, 3 * n // 4)
    def _(r):
        grads_to(1, (me + r) % n).start()

    total = sum_a[:, spot].astype(WIDE)
    for i in range(1, spots):
        s = (spot + i) % spots
        from_spot(s).wait_recv()
        total = total + got_b[s].astype(WIDE)
    sum_b[...] = total.astype(LOW)
    for i in range(1, layers):
        to_layer((z_here + i) % layers).start()

    @pl.loop(3 * n // 4, n)
    def _(r):
        grads_to(1, (me + r) % n).start()

    total = sum_b[z_here].astype(WIDE)
    for i in range(1, layers):
        z = (z_here + i) % layers
        from_layer(z).wait_recv()
        total = total + got_c[z].astype(WIDE)
    done_ref[...] = total

    own(0).wait()
    own(1).wait()
    for i in range(1, spots):
        to_spot((spot + i) % spots).wait_send()
    for i in range(1, layers):
        to_layer((z_here + i) % layers).wait_send()

    @pl.loop(1, n)
    def _(r):
        p = (me + r) % n
        for which in range(2):
            grads_to(which, p).wait_send()
            grads_from(which, p).wait_recv()


def finish_kernel(
    experts, done_ref, gin_ref, gback_ref, tok_ref, res_ref,
    din_ref, dback_ref, dtok_ref, result_ref, dqkv_ref, dwout_ref, drouter_ref, dbback_ref,
    dbin_ref, *vec_refs,
):
    din_ref[...] = gin_ref[...].astype(WIDE)
    dback_ref[...] = gback_ref[...].astype(WIDE)
    dtok_ref[...] = tok_ref[...]
    result_ref[...] = res_ref[...]

    @pl.when(pl.program_id(0) == 0)
    def _():
        dense_blk, width = dwout_ref.shape
        for j in range(3):
            dqkv_ref[j] = done_ref[:, j * width : (j + 1) * width]
        dwout_ref[...] = done_ref[:, 3 * width : 4 * width]
        misc = done_ref[:, 4 * width : 4 * width + 128]
        drouter_ref[...] = misc[:, :experts]
        dbback_ref[...] = misc[:, experts : 2 * experts]
        diagonal = iota((dense_blk, dense_blk), 0) == iota((dense_blk, dense_blk), 1)
        for i, vec in enumerate(vec_refs):
            column = misc[:, 2 * experts + i : 2 * experts + i + 1]
            vec[...] = jnp.sum(jnp.where(diagonal, column, 0.0), axis=0, keepdims=True)
        lines = dbin_ref.shape[1] // 128
        for i in range(dense_blk):
            dbin_ref[i // lines : i // lines + 1, (i % lines) * 128 : (i % lines + 1) * 128] = (
                done_ref[i : i + 1, 4 * width + 128 : 4 * width + 256]
            )


VMEM = pl.BlockSpec(memory_space=pltpu.VMEM)


def make_owner_device(dp, tn):
    n = dp * tn

    def per_device(
        tokens, cotangent, ln1_scale, ln1_shift, w_qkv, w_out, out_bias, ln2_scale, ln2_shift,
        w_router, w_in, b_in, w_back, b_back, choices, slots,
    ):
        rows, width = tokens.shape
        images = rows // SEQ
        experts, blk_d, blk_f = w_in.shape
        ff = blk_f * tn
        dense_blk = w_out.shape[0]
        places = experts * MAIN
        landed = n // 4 * GROUP
        shape = jax.ShapeDtypeStruct

        cols = 4 * width + 256
        per_layer = dp // 4

        hbm = pl.BlockSpec(memory_space=pl.ANY)
        saved = [
            ((per_layer, 2, 2, tn, dense_blk, cols), LOW),
            ((rows, 3 * width), LOW),
            ((rows, width), LOW),
            ((rows, 128), WIDE),
            ((rows, width), WIDE),
            ((rows, width), LOW),
            ((rows, 128), WIDE),
            ((rows, 128), jnp.int32),
        ]
        weight_shape = (n, blk_d, blk_f)
        out_home, back_home, tails_home, dense, qkv, att, lse, mid, two, route, col, d_first, d_second, d_b = pl.pallas_call(
            functools.partial(layer_kernel, dp, images, experts),
            out_shape=(
                shape((places, width), LOW),
                shape((places, width), LOW),
                shape((n, 8, 128), LOW),
                *[shape(*s) for s in saved],
                shape(weight_shape, LOW),
                shape(weight_shape, LOW),
                shape((1, ff), WIDE),
            ),
            in_specs=[VMEM] * 14 + [hbm, hbm],
            out_specs=(hbm,) * 13 + (VMEM,),
            scratch_shapes=[
                *[pltpu.VMEM(*saved[i]) for i in (0, 3, 4, 6, 7)],
                pltpu.VMEM((dense_blk, cols), LOW),
                pltpu.VMEM((2, rows), jnp.int32),
                pltpu.VMEM((2, 4, blk_d, blk_f), WIDE),
                pltpu.VMEM(weight_shape, LOW),
                pltpu.VMEM(weight_shape, LOW),
                pltpu.VMEM((tn, width, blk_f), LOW),
                pltpu.VMEM((tn, width, blk_f), LOW),
                pltpu.VMEM((1, ff), WIDE),
                pltpu.VMEM((places, width), LOW),
                pltpu.VMEM((places, width), LOW),
                pltpu.VMEM((landed, width), LOW),
                pltpu.VMEM((landed, width), LOW),
                pltpu.VMEM((landed, ff), LOW),
                pltpu.VMEM((landed, ff), LOW),
                pltpu.VMEM((places, width), LOW),
                pltpu.VMEM((n, rows), LOW),
                pltpu.VMEM((2, rows), jnp.int32),
                *[pltpu.VMEM((n, 8, 128), LOW)] * 5,
                pltpu.SemaphoreType.DMA((2,)),
                pltpu.SemaphoreType.DMA((2, n)),
                pltpu.SemaphoreType.DMA((2, n)),
                pltpu.SemaphoreType.DMA((n,)),
                pltpu.SemaphoreType.DMA((n,)),
                pltpu.SemaphoreType.DMA((n,)),
                pltpu.SemaphoreType.DMA((n,)),
                pltpu.SemaphoreType.DMA((2, n)),
                pltpu.SemaphoreType.DMA((2, n)),
                pltpu.SemaphoreType.DMA((3, n)),
                pltpu.SemaphoreType.DMA((3, n)),
                pltpu.SemaphoreType.DMA((per_layer,)),
                pltpu.SemaphoreType.DMA((per_layer,)),
                pltpu.SemaphoreType.DMA((2 * tn,)),
                pltpu.SemaphoreType.DMA((2 * tn,)),
                pltpu.SemaphoreType.DMA((2,)),
                pltpu.SemaphoreType.DMA((10,)),
                pltpu.SemaphoreType.DMA((10,)),
            ],
            compiler_params=pltpu.CompilerParams(
                vmem_limit_bytes=63 * 2**20, collective_id=1, has_side_effects=True
            ),
            cost_estimate=pl.CostEstimate(
                flops=12 * places * width * ff, bytes_accessed=10 * places * width, transcendentals=0
            ),
            name="layer",
        )(
            tokens, cotangent, choices.T, slots.T,
            *[v.reshape(1, dense_blk) for v in (ln1_scale, ln1_shift, out_bias, ln2_scale, ln2_shift)],
            w_qkv, w_out, w_router, b_back.T, b_in, w_in, jnp.swapaxes(w_back, 1, 2),
        )
        dense = dense.reshape(width, cols)
        brought = (
            tokens, cotangent, dense, qkv, att, lse, mid, two, route, col, out_home, back_home,
            tails_home,
        )
        result, d_tok, done, grad_in, grad_back = pl.pallas_call(
            functools.partial(backward_kernel, dp, images, experts),
            out_shape=(
                shape((rows, width), LOW),
                shape((rows, width), WIDE),
                shape((dense_blk, cols), WIDE),
                shape((n, blk_d, blk_f), LOW),
                shape((n, blk_d, blk_f), LOW),
            ),
            in_specs=[hbm] * 13 + [VMEM] + [hbm] * 2,
            out_specs=(VMEM, VMEM, VMEM, hbm, hbm),
            scratch_shapes=[
                *[pltpu.VMEM(v.shape, v.dtype) for v in brought[:10]],
                pltpu.VMEM((places + 128, width), LOW),
                pltpu.VMEM((places + 128, width), LOW),
                pltpu.VMEM((n, 8, 128), LOW),
                pltpu.SemaphoreType.DMA((13,)),
                pltpu.VMEM((rows, width), LOW),
                pltpu.VMEM((rows, width), LOW),
                pltpu.VMEM((rows, 3 * width), LOW),
                pltpu.VMEM((dp // 2, 2, tn * dense_blk, cols), LOW),
                pltpu.VMEM((dp // 2, tn * dense_blk, cols), LOW),
                pltpu.VMEM((per_layer, 2 * tn, dense_blk, cols), LOW),
                pltpu.VMEM((2 * tn, per_layer, dense_blk, cols), LOW),
                pltpu.VMEM((per_layer, dense_blk, cols), LOW),
                pltpu.VMEM((per_layer, dense_blk, cols), LOW),
                pltpu.SemaphoreType.DMA((2, n)),
                pltpu.SemaphoreType.DMA((2, n)),
                pltpu.SemaphoreType.DMA((2,)),
                pltpu.SemaphoreType.DMA((2,)),
                pltpu.SemaphoreType.DMA((2 * tn,)),
                pltpu.SemaphoreType.DMA((2 * tn,)),
                pltpu.SemaphoreType.DMA((per_layer,)),
                pltpu.SemaphoreType.DMA((per_layer,)),
            ],
            compiler_params=pltpu.CompilerParams(
                vmem_limit_bytes=60 * 2**20, collective_id=2, has_side_effects=True
            ),
            cost_estimate=pl.CostEstimate(
                flops=6 * places * rows * width + 20 * rows * width * width,
                bytes_accessed=40 * rows * width, transcendentals=0,
            ),
            name="backward",
        )(
            *brought, d_b, d_first, d_second,
        )
        steps = 8
        tok_rows = rows // 7

        def whole(dims):
            return pl.BlockSpec(dims, lambda i: (0,) * len(dims))

        piece = pl.BlockSpec((n // steps, blk_d, blk_f), lambda i: (i, 0, 0))
        tok_piece = pl.BlockSpec((tok_rows, width), lambda i: (jnp.minimum(i, 6), 0))
        vec = (1, dense_blk)
        small = [w_qkv.shape, w_out.shape, w_router.shape, (dense_blk, experts), b_in.shape] + [vec] * 5
        grad_in, grad_back, d_tok, result, *rest = pl.pallas_call(
            functools.partial(finish_kernel, experts),
            grid=(steps,),
            out_shape=(
                shape(weight_shape, WIDE),
                shape(weight_shape, WIDE),
                shape((rows, width), WIDE),
                shape((rows, width), LOW),
                *[shape(d, WIDE) for d in small],
            ),
            in_specs=[whole(done.shape), piece, piece, tok_piece, tok_piece],
            out_specs=(piece, piece, tok_piece, tok_piece, *[whole(d) for d in small]),
            name="finish",
        )(done, grad_in, grad_back, d_tok, result)
        d_qkv, d_wout, d_router, d_bback, d_bin, *vecs = rest
        d_vecs = [v.reshape(dense_blk) for v in vecs]
        return (
            result,
            d_tok,
            d_vecs[0],
            d_vecs[1],
            d_qkv,
            d_wout,
            d_vecs[2],
            d_vecs[3],
            d_vecs[4],
            d_router,
            grad_in,
            d_bin,
            jnp.swapaxes(grad_back, 1, 2),
            d_bback.T,
        )

    return per_device


def make_per_device(dp, tn):
    everyone = ("dp", "tensor")
    n = dp * tn

    def per_device(
        tokens,
        cotangent,
        ln1_scale,
        ln1_shift,
        w_qkv,
        w_out,
        out_bias,
        ln2_scale,
        ln2_shift,
        w_router,
        w_in,
        b_in,
        w_back,
        b_back,
        choices,
        slots,
    ):
        rows_here, width = tokens.shape
        images = rows_here // SEQ
        experts, blk_d, blk_f = w_in.shape
        ff = blk_f * tn
        dense_blk = w_out.shape[0]
        whole = experts % n == 0
        owners = n if whole else dp
        owned = experts // owners
        expert_axes = ("tensor", "dp") if whole else ("dp",)
        slot_total = experts * CAP
        score_scale = HD ** (-0.5)

        w_pack = jnp.stack([w_in.astype(LOW), jnp.swapaxes(w_back, 1, 2).astype(LOW)], axis=1)
        w_all = lax.all_to_all(w_pack, expert_axes, split_axis=0, concat_axis=0, tiled=True)
        f_parts = tn if whole else 1
        w_all = w_all.reshape(f_parts, dp, owned, 2, blk_d, blk_f)
        w_all = w_all.transpose(3, 2, 1, 4, 0, 5).reshape(2, owned, width, f_parts * blk_f)
        first_w, second_wt = w_all[0], w_all[1]

        vec_rows = jnp.stack([ln1_scale, ln1_shift, out_bias, ln2_scale, ln2_shift])
        pieces = [
            w_qkv.reshape(-1),
            w_out.reshape(-1),
            w_router.reshape(-1),
            b_back.reshape(-1),
            b_in.reshape(-1),
            vec_rows.reshape(-1),
        ]
        sizes = [p.shape[0] for p in pieces]
        total = sum(sizes)
        pad = -total % 512
        packed = jnp.concatenate([p.astype(LOW) for p in pieces] + [jnp.zeros((pad,), LOW)])
        gathered = lax.all_gather(packed.reshape(-1, 512), everyone, axis=0, tiled=False)
        gathered = gathered.reshape(n, -1)
        offs = [sum(sizes[:i]) for i in range(len(sizes))]
        part = [gathered[:, o : o + s] for o, s in zip(offs, sizes)]
        qkv_w = part[0].reshape(n, 3, dense_blk, width).swapaxes(0, 1).reshape(3, width, width)
        out_w = part[1].reshape(width, width)
        router = part[2].reshape(width, experts)
        bias_back = part[3].reshape(n, experts, -1).swapaxes(0, 1).reshape(experts, width)
        bias_back = bias_back.astype(WIDE)
        in_b = part[4].reshape(dp, tn, experts // dp, blk_f).swapaxes(1, 2).reshape(experts, ff)
        vecs = part[5].reshape(n, 5, -1).swapaxes(0, 1).reshape(5, width).astype(WIDE)
        gain_one, shift_one, bias_attn, gain_two, shift_two = vecs
        if whole:
            mine = lax.axis_index("tensor") * dp + lax.axis_index("dp")
            my_b = lax.dynamic_slice(in_b, (mine * owned, 0), (owned, ff)).astype(WIDE)
        else:
            my_b = lax.dynamic_slice(
                in_b,
                (lax.axis_index("dp") * owned, lax.axis_index("tensor") * blk_f),
                (owned, blk_f),
            ).astype(WIDE)

        residual = tokens.astype(WIDE)
        normed_one = norm_affine(residual, gain_one, shift_one).astype(LOW)
        projected = jnp.einsum(
            "td,jde->jte", normed_one, qkv_w, preferred_element_type=WIDE
        ).astype(LOW)
        head_query = projected[0].reshape(images, SEQ, H, HD)
        head_key = projected[1].reshape(images, SEQ, H, HD)
        head_value = projected[2].reshape(images, SEQ, H, HD)
        raw_scores = jnp.einsum(
            "ishd,ithd->ihst", head_query, head_key, preferred_element_type=WIDE
        )
        scaled = raw_scores * score_scale
        row_top = jnp.max(scaled, axis=-1, keepdims=True)
        log_total = row_top + jnp.log(jnp.sum(jnp.exp(scaled - row_top), axis=-1, keepdims=True))
        weights_att = jnp.exp(scaled - log_total).astype(LOW)
        attended = (
            jnp.einsum("ihst,ithd->ishd", weights_att, head_value, preferred_element_type=WIDE)
            .astype(LOW)
            .reshape(rows_here, width)
        )
        attn_sum = jnp.dot(attended, out_w, preferred_element_type=WIDE)
        middle = residual + attn_sum + bias_attn
        normed_two = norm_affine(middle, gain_two, shift_two).astype(LOW)
        route_p = jax.nn.softmax(jnp.dot(normed_two, router, preferred_element_type=WIDE), axis=-1)

        expert_ids = jnp.arange(experts, dtype=jnp.int32)
        chosen = [
            (choices[:, k : k + 1] == expert_ids[None, :]).astype(WIDE) for k in range(2)
        ]
        gate_vals = jnp.concatenate(
            [jnp.sum(route_p * c, axis=1, keepdims=True) for c in chosen], axis=1
        )
        kept_pair = (slots >= 0).astype(WIDE)
        target = jnp.where(slots >= 0, choices * CAP + slots, -1)
        places = jnp.arange(slot_total, dtype=jnp.int32)
        by_slot = [target[:, k][None, :] == places[:, None] for k in range(2)]
        spread_mat = (by_slot[0] | by_slot[1]).astype(LOW)
        by_token = [target[:, k : k + 1] == places[None, :] for k in range(2)]
        pair_weight = gate_vals * kept_pair
        slot_gate = jnp.sum(
            jnp.where(by_slot[0], pair_weight[:, 0][None, :], 0.0)
            + jnp.where(by_slot[1], pair_weight[:, 1][None, :], 0.0),
            axis=1,
            keepdims=True,
        )
        both = jnp.dot(
            spread_mat,
            jnp.concatenate([normed_two, cotangent], axis=1),
            preferred_element_type=WIDE,
        )
        buffer = both[:, :width].astype(LOW).reshape(experts, CAP, width)
        slot_grad = slot_gate * both[:, width:]
        grad_bias_back = jnp.sum(slot_grad.reshape(experts, CAP, width), axis=1)
        slot_grad_low = slot_grad.astype(LOW).reshape(experts, CAP, width)

        def out_to_experts(rows):
            width_c = rows.shape[1]
            if not whole:
                rows = lax.all_gather(rows, "tensor", axis=1, tiled=True)
            rows = lax.all_to_all(rows, expert_axes, split_axis=0, concat_axis=0, tiled=True)
            return rows.reshape(owners, owned, -1, width)

        def back_to_tokens(rows):
            rows = rows.reshape(experts, -1, width)
            rows = lax.all_to_all(rows, expert_axes, split_axis=0, concat_axis=0, tiled=True)
            if not whole:
                rows = lax.psum_scatter(rows, "tensor", scatter_dimension=1, tiled=True)
            return rows

        sent = out_to_experts(jnp.concatenate([buffer, slot_grad_low], axis=1))
        group = sent.shape[2] // (2 * CAP)
        sent = sent.reshape(owners, owned, group, 2, CAP, width).transpose(3, 1, 0, 2, 4, 5)
        sent = sent.reshape(2, owned, owners * group * CAP, width)
        all_slots, slot_grad_all = sent[0], sent[1]

        pre_act = (
            jnp.einsum("ecd,edf->ecf", all_slots, first_w, preferred_element_type=WIDE)
            + my_b[:, None, :]
        )
        hidden, gelu_pull = jax.vjp(lambda member: jax.nn.gelu(member, approximate=True), pre_act)
        hidden = hidden.astype(LOW)
        expert_sum = jnp.einsum("ecf,edf->ecd", hidden, second_wt, preferred_element_type=WIDE)
        grad_hidden = jnp.einsum("ecd,edf->ecf", slot_grad_all, second_wt, preferred_element_type=WIDE)
        grad_pre = gelu_pull(grad_hidden)[0].astype(LOW)
        grad_slots_all = jnp.einsum("ecf,edf->ecd", grad_pre, first_w, preferred_element_type=WIDE)
        returned = jnp.stack([expert_sum.astype(LOW), grad_slots_all.astype(LOW)])
        returned = returned.reshape(2, owned, owners, group, CAP, width).transpose(2, 1, 3, 0, 4, 5)
        returned = returned.reshape(owners * owned, group * 2 * CAP, width)
        home = back_to_tokens(returned).reshape(experts, 2, CAP, width)
        expert_home = home[:, 0].reshape(slot_total, width)
        grad_home = home[:, 1].reshape(slot_total, width)

        grad_first_b = jnp.sum(grad_pre.astype(WIDE), axis=1)
        grad_first_w = jnp.einsum("ecd,ecf->edf", all_slots, grad_pre, preferred_element_type=WIDE)
        grad_second_t = jnp.einsum("ecd,ecf->edf", slot_grad_all, hidden, preferred_element_type=WIDE)
        g_pack = jnp.stack([grad_first_w.astype(LOW), grad_second_t.astype(LOW)])
        g_pack = g_pack.reshape(2, owned, dp, blk_d, f_parts, blk_f).transpose(4, 2, 1, 0, 3, 5)
        g_pack = g_pack.reshape(f_parts * dp * owned, 2, blk_d, blk_f)
        g_home = lax.all_to_all(g_pack, expert_axes, split_axis=0, concat_axis=0, tiled=True)
        g_home = g_home.reshape(experts, 2, blk_d, blk_f).astype(WIDE)
        grad_w_in = g_home[:, 0]
        grad_w_back = jnp.swapaxes(g_home[:, 1], 1, 2)

        picked = []
        for k in range(2):
            rows = jnp.dot(by_token[k].astype(LOW), expert_home, preferred_element_type=WIDE)
            bias_rows = jnp.dot(
                chosen[k].astype(LOW), bias_back.astype(LOW), preferred_element_type=WIDE
            )
            picked.append((rows + bias_rows) * kept_pair[:, k : k + 1])
        result = (
            middle + gate_vals[:, 0:1] * picked[0] + gate_vals[:, 1:2] * picked[1]
        ).astype(LOW)
        grad_out = cotangent.astype(WIDE)
        grad_probs = sum(
            jnp.sum(grad_out * picked[k], axis=1, keepdims=True) * chosen[k] for k in range(2)
        )
        gather_mat = (by_token[0] | by_token[1]).astype(LOW)
        grad_normed_two = jnp.dot(gather_mat, grad_home, preferred_element_type=WIDE)
        grad_logits = route_p * (grad_probs - jnp.sum(grad_probs * route_p, axis=-1, keepdims=True))
        grad_normed_two = grad_normed_two + jnp.dot(
            grad_logits, router.astype(WIDE).T, precision=lax.Precision.HIGHEST
        )
        grad_router = jnp.dot(
            normed_two.astype(WIDE).T, grad_logits, precision=lax.Precision.HIGHEST
        )
        _, pull_two = jax.vjp(norm_affine, middle, gain_two, shift_two)
        grad_mid_norm, grad_gain_two, grad_shift_two = pull_two(grad_normed_two)
        grad_middle = grad_out + grad_mid_norm
        grad_bias_attn = jnp.sum(grad_middle, axis=0)
        grad_mid_low = grad_middle.astype(LOW)
        grad_att = jnp.einsum(
            "td,ed->te", grad_mid_low, out_w, preferred_element_type=WIDE
        ).astype(LOW)
        grad_out_w = jnp.einsum("te,td->ed", attended, grad_mid_low, preferred_element_type=WIDE)
        grad_att_heads = grad_att.reshape(images, SEQ, H, HD)
        probs_again = jnp.exp(
            jnp.einsum("ishd,ithd->ihst", head_query, head_key, preferred_element_type=WIDE)
            * score_scale
            - log_total
        )
        grad_weights = jnp.einsum(
            "ishd,ithd->ihst", grad_att_heads, head_value, preferred_element_type=WIDE
        )
        row_delta = jnp.sum(grad_weights * probs_again, axis=-1, keepdims=True)
        grad_raw = (probs_again * (grad_weights - row_delta) * score_scale).astype(LOW)
        grad_value = jnp.einsum(
            "ihst,ishd->ithd",
            probs_again.astype(LOW),
            grad_att_heads,
            preferred_element_type=WIDE,
        )
        grad_query = jnp.einsum("ihst,ithd->ishd", grad_raw, head_key, preferred_element_type=WIDE)
        grad_key = jnp.einsum("ihst,ishd->ithd", grad_raw, head_query, preferred_element_type=WIDE)
        grad_proj = jnp.stack(
            [
                grad_query.astype(LOW).reshape(rows_here, width),
                grad_key.astype(LOW).reshape(rows_here, width),
                grad_value.astype(LOW).reshape(rows_here, width),
            ]
        )
        grad_qkv_w = jnp.einsum("td,jte->jde", normed_one, grad_proj, preferred_element_type=WIDE)
        grad_normed_one = jnp.einsum("jte,jde->td", grad_proj, qkv_w, preferred_element_type=WIDE)
        _, pull_one = jax.vjp(norm_affine, residual, gain_one, shift_one)
        grad_resid_norm, grad_gain_one, grad_shift_one = pull_one(grad_normed_one)
        grad_tokens = grad_middle + grad_resid_norm

        if whole:
            row_b = jnp.zeros((experts, ff), WIDE)
            row_b = lax.dynamic_update_slice(row_b, grad_first_b, (mine * owned, 0))
        else:
            row_b = jnp.zeros((experts, ff), WIDE)
            row_b = lax.dynamic_update_slice(
                row_b,
                grad_first_b,
                (lax.axis_index("dp") * owned, lax.axis_index("tensor") * blk_f),
            )
        vec_grads = jnp.stack(
            [grad_gain_one, grad_shift_one, grad_bias_attn, grad_gain_two, grad_shift_two]
        )
        out_pieces = [
            grad_qkv_w.reshape(3, n, dense_blk, width).swapaxes(0, 1).reshape(n, -1),
            grad_out_w.reshape(n, -1),
            grad_router.reshape(n, -1),
            grad_bias_back.reshape(experts, n, -1).swapaxes(0, 1).reshape(n, -1),
            row_b.reshape(dp, experts // dp, tn, blk_f).swapaxes(1, 2).reshape(n, -1),
            vec_grads.reshape(5, n, -1).swapaxes(0, 1).reshape(n, -1),
        ]
        out_pack = jnp.concatenate(
            [p.astype(LOW) for p in out_pieces] + [jnp.zeros((n, pad), LOW)], axis=1
        )
        out_all = lax.all_to_all(
            out_pack.reshape(n, -1, 512), everyone, split_axis=0, concat_axis=0, tiled=True
        )
        summed = jnp.sum(out_all.astype(WIDE), axis=0).reshape(-1)
        done = [summed[o : o + s] for o, s in zip(offs, sizes)]
        vec_done = done[5].reshape(5, -1)
        return (
            result,
            grad_tokens,
            vec_done[0],
            vec_done[1],
            done[0].reshape(w_qkv.shape),
            done[1].reshape(w_out.shape),
            vec_done[2],
            vec_done[3],
            vec_done[4],
            done[2].reshape(w_router.shape),
            grad_w_in,
            done[4].reshape(b_in.shape),
            grad_w_back,
            done[3].reshape(b_back.shape),
        )

    return per_device


def solution(mesh):
    everyone = ("dp", "tensor")
    in_specs = (
        P(everyone, None),
        P(everyone, None),
        P(everyone),
        P(everyone),
        P(None, everyone, None),
        P(everyone, None),
        P(everyone),
        P(everyone),
        P(everyone),
        P(everyone, None),
        P(None, "dp", "tensor"),
        P("dp", "tensor"),
        P(None, "tensor", "dp"),
        P(None, everyone),
        P(everyone, None),
        P(everyone, None),
    )
    out_specs = in_specs[:2] + in_specs[2:14]
    dp, tn = mesh.shape["dp"], mesh.shape["tensor"]

    def chosen(*args):
        one_each = args[10].shape[0] == dp * tn and dp % 4 == 0
        return (make_owner_device if one_each else make_per_device)(dp, tn)(*args)

    return jax.shard_map(
        chosen,
        mesh=mesh,
        in_specs=in_specs,
        out_specs=out_specs,
        check_vma=False,
    )
```

```python
import functools

import jax
import jax.numpy as jnp
from jax import lax
from jax.experimental import pallas as pl
from jax.experimental.pallas import tpu as pltpu
from jax.sharding import PartitionSpec as P

H = 8
HD = 64
SEQ = 196
CAP = 65
LOW = jnp.bfloat16
WIDE = jnp.float32


def norm_affine(values_in, gain_vec, shift_vec):
    center = values_in - jnp.mean(values_in, axis=-1, keepdims=True)
    spread = jnp.mean(center * center, axis=-1, keepdims=True)
    return center * lax.rsqrt(spread + 1e-06) * gain_vec + shift_vec


MAIN = CAP - 1
GROUP = 4 * MAIN + 16
WIN = 208
STEP = 192


def dot(a, b, dims=((1,), (0,))):
    return lax.dot_general(a, b, (dims, ((), ())), preferred_element_type=WIDE)


NT = ((1,), (1,))
TN = ((0,), (0,))
MESH = pl.DeviceIdType.MESH


def to_tiles(pieces):
    m = pieces[0].shape[0]
    gap = iota((8 * m, m), 0) - 8 * iota((8 * m, m), 1)
    return sum(
        dot(jnp.where(gap == c, 1.0, 0.0).astype(LOW), piece) for c, piece in enumerate(pieces)
    )


def from_tiles(tiles, c, rows):
    gap = iota((rows, tiles.shape[0]), 1) - 8 * iota((rows, tiles.shape[0]), 0)
    return dot(jnp.where(gap == c, 1.0, 0.0).astype(LOW), tiles)


def lane_blocks(v):
    return [v[:, c * 128 : (c + 1) * 128] for c in range(v.shape[1] // 128)]


def split_two(v):
    high = v.astype(LOW)
    return high, (v - high.astype(WIDE)).astype(LOW)


def iota(shape, dim):
    return lax.broadcasted_iota(jnp.int32, shape, dim)


def normalize(v):
    center = v - jnp.mean(v, axis=-1, keepdims=True)
    rstd = lax.rsqrt(jnp.mean(center * center, axis=-1, keepdims=True) + 1e-06)
    return center * rstd, rstd


def norm_back(grad, xhat, rstd, gain):
    inner = grad * gain
    return rstd * (
        inner
        - jnp.mean(inner, axis=-1, keepdims=True)
        - xhat * jnp.mean(inner * xhat, axis=-1, keepdims=True)
    )


def layer_kernel(
    dp, images, experts, tok_ref, cot_ref, choice_ref, slot_ref, gain_one_ref, shift_one_ref,
    bias_ref, gain_two_ref, shift_two_ref, wqkv_ref, wout_ref, router_ref, bback_ref, bin_ref,
    win_ref, wback_ref,
    out_ref, grad_ref, tail_out, dense_out, qkv_out, att_out, lse_out, mid_out, two_out, route_out,
    col_out, dfirst_out, dsecond_out, db_ref,
    dense_ref, lse_ref, mid_ref, route_ref, col_ref, shard_ref, rows_ref,
    wide_ref, low_first, low_second, first_ref, second_ref, b_ref,
    x_ref, g_ref, xs_ref, sg_ref, hid_ref, pre_ref, backs_ref,
    tails_ref, last_ref, x_tiles, g_tiles, xs_tiles, gs_tiles, home_tiles,
    stage_sem, w_send, w_recv, g_send, g_recv, x_send, x_recv, r_send, r_recv,
    t_send, t_recv, c_send, c_recv, s_send, s_recv, a_sems, own_sem, save_sem,
):
    outs_ref = g_ref
    total, width = g_ref.shape
    rows = tok_ref.shape[0]
    qkv_ref = pre_ref.at[0:rows, 0 : 3 * width]
    att_ref = pre_ref.at[0:rows, 3 * width : 4 * width]
    two_ref = hid_ref.at[0:rows, 0:width]
    n = total // MAIN
    tn = n // dp
    parts, _, half = first_ref.shape
    blk_d = low_first.shape[1]
    dense_blk = shard_ref.shape[0]
    groups = n // 4
    per = GROUP
    t_here, d_here = lax.axis_index("tensor"), lax.axis_index("dp")
    me = t_here * dp + d_here
    my_group, my_place = me // 4, me % 4
    core, y_here, z_here = d_here % 2, (d_here // 2) % 2, d_here // 4
    spots, layers = 2 * tn, dp // 4
    spot = y_here * tn + t_here

    def device(p):
        return (p % dp, p // dp)

    def block(p):
        return pl.ds(pl.multiple_of(p * MAIN, 16), MAIN)

    def landing(p):
        return pl.ds(pl.multiple_of(p // 4 * GROUP + p % 4 * MAIN, 16), MAIN)

    tiles = ((x_tiles, xs_tiles), (g_tiles, gs_tiles), (home_tiles, tail_out))

    def tile(which, p, source):
        src, dst = tiles[which]
        return pltpu.make_async_remote_copy(
            src_ref=src.at[p], dst_ref=dst.at[source],
            send_sem=t_send.at[which, p], recv_sem=t_recv.at[which, source],
            device_id=device(p), device_id_type=MESH,
        )

    def own_tile(which):
        src, dst = tiles[which]
        return pltpu.make_async_copy(src.at[me], dst.at[me], own_sem.at[7 + which])

    def weight_rows(p):
        return pl.ds(pl.multiple_of((p % dp) * blk_d, 16), blk_d)

    def weights(which, p, source):
        src, dst = ((low_first, first_ref), (low_second, second_ref))[which]
        return pltpu.make_async_remote_copy(
            src_ref=src.at[p], dst_ref=dst.at[source // dp, weight_rows(source)],
            send_sem=w_send.at[which, p], recv_sem=w_recv.at[which, source],
            device_id=device(p), device_id_type=MESH,
        )

    def own_weights(which):
        src, dst = ((low_first, first_ref), (low_second, second_ref))[which]
        return pltpu.make_async_copy(
            src.at[me], dst.at[t_here, weight_rows(me)], own_sem.at[3 + which]
        )

    def rows_of(which, p, source):
        src, dst, send, recv = (
            (x_ref, xs_ref, x_send, x_recv), (g_ref, sg_ref, g_send, g_recv)
        )[which]
        return pltpu.make_async_remote_copy(
            src_ref=src.at[block(p)], dst_ref=dst.at[landing(source)],
            send_sem=send.at[p], recv_sem=recv.at[source],
            device_id=device(p), device_id_type=MESH,
        )

    def home(which, p, source):
        src, dst = ((outs_ref, out_ref), (backs_ref, grad_ref))[which]
        return pltpu.make_async_remote_copy(
            src_ref=src.at[block(p)], dst_ref=dst.at[block(source)],
            send_sem=r_send.at[which, p], recv_sem=r_recv.at[which, source],
            device_id=device(p), device_id_type=MESH,
        )

    def own(which):
        src, dst = (
            (x_ref, xs_ref), (outs_ref, out_ref), (backs_ref, grad_ref),
            None, None, (g_ref, sg_ref),
        )[which]
        place = block(me) if which in (1, 2) else landing(me)
        return pltpu.make_async_copy(src.at[block(me)], dst.at[place], own_sem.at[which])

    near, across = z_here + 1 - 2 * (z_here % 2), (z_here + 2) % layers

    def shard_at(source):
        return dense_ref.at[source, y_here, core, t_here]

    def to_layer(src, z, source, place):
        return pltpu.make_async_remote_copy(
            src_ref=src, dst_ref=shard_at(source),
            send_sem=c_send.at[place], recv_sem=c_recv.at[source],
            device_id=((z * 2 + y_here) * 2 + core, t_here), device_id_type=MESH,
        )

    def from_layer(source):
        return to_layer(shard_at(source), near, source, 0)

    layer_sends = (
        to_layer(shard_ref, near, z_here, 0),
        to_layer(shard_ref, across, z_here, 1),
        to_layer(shard_at(across), near, across, 2),
    )

    def to_spot(s, source):
        return pltpu.make_async_remote_copy(
            src_ref=dense_ref.at[:, y_here, core, t_here],
            dst_ref=dense_ref.at[:, source // tn, core, source % tn],
            send_sem=s_send.at[s], recv_sem=s_recv.at[source],
            device_id=((z_here * 2 + s // tn) * 2 + core, s % tn), device_id_type=MESH,
        )

    def to_core(source):
        return pltpu.make_async_remote_copy(
            src_ref=dense_ref.at[:, :, core], dst_ref=dense_ref.at[:, :, source],
            send_sem=a_sems.at[0], recv_sem=a_sems.at[1],
            device_id=(d_here + 1 - 2 * core, t_here), device_id_type=MESH,
        )

    own_shard = pltpu.make_async_copy(
        shard_ref, dense_ref.at[z_here, y_here, core, t_here], own_sem.at[6]
    )
    pieces = wide_ref.shape[1]
    chunks = n // pieces

    def stage(which, j):
        src = (win_ref, wback_ref)[which]
        c = (me // pieces + j) % chunks
        return pltpu.make_async_copy(
            src.at[pl.ds(c * pieces, pieces)], wide_ref.at[j % 2], stage_sem.at[j % 2]
        )

    barrier = pltpu.get_barrier_semaphore()

    @pl.loop(1, n)
    def _(r):
        pl.semaphore_signal(barrier, inc=1, device_id=device((me + r) % n), device_id_type=MESH)

    stage(0, 0).start()
    for j in range(3):
        shard_ref[:, j * width : (j + 1) * width] = wqkv_ref[j].astype(LOW)
    shard_ref[:, 3 * width : 4 * width] = wout_ref[...].astype(LOW)
    diagonal = iota((dense_blk, dense_blk), 0) == iota((dense_blk, dense_blk), 1)
    lanes = iota((1, 128), 1)
    spread = iota((experts, 128), 1) - iota((experts, 128), 0)
    misc = dot(router_ref[...].astype(LOW), jnp.where(spread == 0, 1.0, 0.0).astype(LOW))
    misc = misc + dot(
        bback_ref[...].astype(LOW), jnp.where(spread == experts, 1.0, 0.0).astype(LOW)
    )
    vectors = (gain_one_ref, shift_one_ref, bias_ref, gain_two_ref, shift_two_ref)
    for i, vec in enumerate(vectors):
        column = jnp.sum(jnp.where(diagonal, vec[...], 0.0), axis=1, keepdims=True)
        misc = jnp.where(lanes == 64 + i, column, misc)
    shard_ref[:, 4 * width : 4 * width + 128] = misc.astype(LOW)
    lines = half // 128
    slab = jnp.zeros((dense_blk, 128), WIDE)
    for i in range(dense_blk):
        part = bin_ref[i // lines : i // lines + 1, (i % lines) * 128 : (i % lines + 1) * 128]
        slab = jnp.where(iota((dense_blk, 1), 0) == i, part, slab)
    shard_ref[:, 4 * width + 128 : 4 * width + 256] = slab.astype(LOW)
    slot_in = slot_ref[...]
    rows_ref[...] = jnp.where(
        (slot_in >= 0) & (slot_in < MAIN), choice_ref[...] * MAIN + slot_in, -1
    )
    last_ref[...] = jnp.where(slot_in == MAIN, choice_ref[...], -1)
    pick = iota((2, 128), 1) - iota((2, 128), 0)
    turned = dot(
        choice_ref[...].astype(WIDE).astype(LOW), jnp.where(pick == 0, 1.0, 0.0).astype(LOW), TN
    ) + dot(slot_ref[...].astype(WIDE).astype(LOW), jnp.where(pick == 2, 1.0, 0.0).astype(LOW), TN)
    col_ref[...] = turned.astype(jnp.int32)
    own_shard.start()
    db_ref[...] = jnp.zeros_like(db_ref)
    pl.semaphore_wait(barrier, n - 1)
    layer_sends[1].start()
    layer_sends[0].start()

    def send_weights(which):
        low = (low_first, low_second)[which]
        for j in range(chunks):
            if j + 1 < chunks:
                stage(which, j + 1).start()
            elif which == 0:
                stage(1, 0).start()
            stage(which, j).wait()
            c = (me // pieces + j) % chunks
            low[pl.ds(c * pieces, pieces)] = wide_ref[j % 2].astype(LOW)

            @pl.loop(0, pieces)
            def _(i):
                p = c * pieces + (me + i) % pieces

                @pl.when(p != me)
                def _():
                    weights(which, p, me).start()

        own_weights(which).start()

    send_weights(0)
    from_layer(across).wait_recv()
    layer_sends[2].start()
    send_weights(1)
    own_shard.wait()
    from_layer(near).wait_recv()
    from_layer((near + 2) % layers).wait_recv()
    for i in range(1, spots):
        to_spot((spot + i) % spots, spot).start()

    some = 8
    big = some * MAIN
    place = iota((n, rows), 0)
    last_hit = (place == last_ref[0:1, :]) | (place == last_ref[1:2, :])
    tails_ref[...] = jnp.where(last_hit, 1.0, 0.0).astype(LOW)
    got = dot(tails_ref[...], cot_ref[...]).astype(LOW)
    g_tiles[...] = to_tiles(lane_blocks(got)).reshape(n, 8, 128).astype(LOW)

    @pl.loop(0, n // some)
    def _(j):
        c = (me // some + j) % (n // some)
        place = iota((big, rows), 0) + c * big
        hit = (place == rows_ref[0:1, :]) | (place == rows_ref[1:2, :])
        got = dot(jnp.where(hit, 1.0, 0.0).astype(LOW), cot_ref[...])
        g_ref[pl.ds(pl.multiple_of(c * big, 16), big), :] = got.astype(LOW)

        @pl.loop(0, some)
        def _(i):
            p = c * some + (me + i) % some

            @pl.when(p != me)
            def _():
                rows_of(1, p, me).start()
                tile(1, p, me).start()

    own(5).start()
    own_tile(1).start()
    for i in range(1, spots):
        s = (spot + i) % spots
        to_spot(s, s).wait_recv()
    to_core(core).start()
    to_core(1 - core).wait_recv()

    def dense(cols):
        return dense_ref[:, :, :, :, :, cols].reshape(width, -1)

    misc = dense(slice(4 * width, 4 * width + 128))
    misc_t = misc.astype(WIDE).T
    gain_one, shift_one, bias, gain_two, shift_two = [
        misc_t[64 + i : 65 + i, :] for i in range(5)
    ]
    base = tok_ref[...].astype(WIDE)
    xhat, _ = normalize(base)
    one = (xhat * gain_one + shift_one).astype(LOW)
    for j in range(3):
        cols = slice(j * width, (j + 1) * width)
        qkv_ref[:, cols] = dot(one, dense(cols)).astype(LOW)
    att_ref[...] = jnp.zeros((rows, width), LOW)
    lse_ref[...] = jnp.zeros_like(lse_ref)
    low_half = iota((1, 128), 1) < HD

    @pl.loop(0, images)
    def _(i):
        win = pl.ds(pl.multiple_of(i * STEP, 16), WIN)
        first = i * (SEQ - STEP)
        key_pos = iota((1, WIN), 1)
        key_ok = (key_pos >= first) & (key_pos < first + SEQ)
        row_pos = iota((WIN, 1), 0)
        row_ok = (row_pos >= first) & (row_pos < first + SEQ)
        lse = jnp.zeros((WIN, 128), WIDE)
        for pair in range(H // 2):
            q = qkv_ref[win, pair * 128 : (pair + 1) * 128]
            k = qkv_ref[win, width + pair * 128 : width + (pair + 1) * 128]
            v = qkv_ref[win, 2 * width + pair * 128 : 2 * width + (pair + 1) * 128]
            outs = []
            for side in range(2):
                mask = low_half if side == 0 else jnp.logical_not(low_half)
                qm = jnp.where(mask, q, jnp.zeros_like(q))
                s = jnp.where(key_ok, dot(qm, k, NT) * HD**-0.5, -1e30)
                top = jnp.max(s, axis=-1, keepdims=True)
                p = jnp.exp(s - top)
                all_p = jnp.sum(p, axis=-1, keepdims=True)
                p = (p / all_p).astype(LOW)
                outs.append(dot(p, v))
                lane = iota((1, 128), 1) == 2 * pair + side
                lse = jnp.where(lane, top + jnp.log(all_p), lse)
            got = jnp.where(low_half, outs[0], outs[1]).astype(LOW)
            cols = slice(pair * 128, (pair + 1) * 128)
            att_ref[win, cols] = jnp.where(row_ok, got, att_ref[win, cols])
        lse_ref[win, :] = jnp.where(row_ok, lse, lse_ref[win, :])

    mid = base + dot(att_ref[...], dense(slice(3 * width, 4 * width))) + bias
    mid_ref[...] = mid
    xhat, _ = normalize(mid)
    two = (xhat * gain_two + shift_two).astype(LOW)
    two_ref[...] = two
    lanes = iota((1, 128), 1)
    logits = jnp.where(lanes < experts, dot(two, misc), -1e30)
    route = jnp.exp(logits - jnp.max(logits, axis=-1, keepdims=True))
    route = route / jnp.sum(route, axis=-1, keepdims=True)
    route_ref[...] = route
    high, low = jnp.zeros((128, 128), WIDE), jnp.zeros((128, 128), WIDE)
    for k in range(2):
        chosen = lanes == col_ref[:, k : k + 1]
        gate = jnp.where(chosen, route, 0.0)
        here = jnp.where(lanes == col_ref[:, 2 + k : 3 + k], 1.0, 0.0).astype(LOW)
        part_high, part_low = split_two(gate)
        high = high + dot(part_high, here, TN)
        low = low + dot(part_low, here, TN)
    last = lane_blocks(dot(tails_ref[...], two_ref[...]).astype(LOW))
    last = last + [high[:experts].astype(LOW), low[:experts].astype(LOW)]
    x_tiles[...] = to_tiles(last).reshape(n, 8, 128).astype(LOW)

    @pl.loop(0, n // some)
    def _(c):
        place = iota((big, rows), 0) + c * big
        hit = (place == rows_ref[0:1, :]) | (place == rows_ref[1:2, :])
        got = dot(jnp.where(hit, 1.0, 0.0).astype(LOW), two_ref[...])
        x_ref[pl.ds(pl.multiple_of(c * big, 16), big), :] = got.astype(LOW)

    def others(j, action):
        for i in range(4):
            if isinstance(j, int) and j == 0:
                if i > 0:
                    action(4 * my_group + (my_place + i) % 4)
            else:
                action(4 * ((my_group + groups + j) % groups) + (my_place + i) % 4)

    def send_slots(p):
        tile(0, p, me).start()
        rows_of(0, p, me).start()

    own(0).start()
    own_tile(0).start()
    others(0, send_slots)

    @pl.loop(1, groups)
    def _(j):
        others(groups - j, send_slots)

    saved = (
        (dense_ref, dense_out), (qkv_ref, qkv_out), (att_ref, att_out), (lse_ref, lse_out),
        (mid_ref, mid_out), (two_ref, two_out), (route_ref, route_out), (col_ref, col_out),
        (low_first, dfirst_out), (low_second, dsecond_out),
    )

    def save(i):
        return pltpu.make_async_copy(saved[i][0], saved[i][1], save_sem.at[i])

    for i in range(8):
        save(i).start()

    per_dp = experts // dp
    for f in range(parts):
        place = me // per_dp
        slab = dense_ref[
            place // 4, (place // 2) % 2, place % 2, f, :, 4 * width + 128 : 4 * width + 256
        ].astype(WIDE)
        lines = dense_blk // per_dp
        mine = slab[:lines]
        for i in range(1, per_dp):
            mine = jnp.where(me % per_dp == i, slab[i * lines : (i + 1) * lines], mine)
        for i in range(lines):
            b_ref[:, f * half + i * 128 : f * half + (i + 1) * 128] = mine[i : i + 1]

    for i in range(8):
        save(i).wait()
    own_weights(0).wait()
    own_weights(1).wait()
    own(5).wait()
    own_tile(1).wait()

    @pl.loop(1, n)
    def _(r):
        p = (me + r) % n
        for which in range(2):
            weights(which, p, p).wait_recv()
            weights(which, p, me).wait_send()
        rows_of(1, p, me).wait_send()

    place = iota((per, 1), 0)
    sender = jnp.where(place < 4 * MAIN, place // MAIN, place - 4 * MAIN)
    slot_at = jnp.where(place < 4 * MAIN, place % MAIN, MAIN)

    def flat(ref, group):
        return ref[pl.ds(4 * group, 4)].astype(WIDE).reshape(32, 128).astype(LOW)

    def compute(group):
        here = pl.ds(pl.multiple_of(group * per, 16), per)
        tail = pl.ds(pl.multiple_of(group * per + 4 * MAIN, 16), 16)
        x_last, g_last = flat(xs_tiles, group), flat(gs_tiles, group)
        for c in range(width // 128):
            cols = slice(c * 128, (c + 1) * 128)
            xs_ref[tail, cols] = from_tiles(x_last, c, 16).astype(LOW)
            sg_ref[tail, cols] = from_tiles(g_last, c, 16).astype(LOW)
        gates = from_tiles(x_last, width // 128, 16) + from_tiles(x_last, width // 128 + 1, 16)
        x = xs_ref[here, :]
        lanes = iota((1, 128), 1)
        gate = jnp.zeros((per, 1), WIDE)
        for s in range(4):
            got = jnp.sum(jnp.where(lanes == slot_at, gates[s : s + 1], 0.0), axis=1, keepdims=True)
            gate = jnp.where(sender == s, got, gate)
        sg = (gate * sg_ref[here, :].astype(WIDE)).astype(LOW)
        sg_ref[here, :] = sg
        out = jnp.zeros((per, width), WIDE)
        back = jnp.zeros((per, width), WIDE)
        for f in range(parts):
            cols = slice(f * half, (f + 1) * half)
            pre = dot(x, first_ref[f]) + b_ref[:, cols]
            t = jnp.tanh(0.7978845608028654 * (pre + 0.044715 * (pre * pre * pre)))
            hid = (0.5 * pre * (1.0 + t)).astype(LOW)
            slope = 0.5 * (1.0 + t) + (0.5 * pre) * (1.0 - t * t) * (
                0.7978845608028654 * (1.0 + 0.134145 * (pre * pre))
            )
            hid_ref[here, cols] = hid
            out = out + dot(hid, second_ref[f], NT)
            gp = (dot(sg, second_ref[f]) * slope).astype(LOW)
            pre_ref[here, cols] = gp
            db_ref[:, cols] += jnp.sum(gp.astype(WIDE), axis=0, keepdims=True)
            back = back + dot(gp, first_ref[f], NT)
        out, back = out.astype(LOW), back.astype(LOW)
        main = pl.ds(pl.multiple_of(group * 4 * MAIN, 16), 4 * MAIN)
        outs_ref[main, :] = out[: 4 * MAIN]
        backs_ref[main, :] = back[: 4 * MAIN]
        made = to_tiles(lane_blocks(out[4 * MAIN :]) + lane_blocks(back[4 * MAIN :]))
        home_tiles[pl.ds(4 * group, 4)] = made[:32].reshape(4, 8, 128).astype(LOW)

    def send_home(j):
        def both(p):
            home(0, p, me).start()
            home(1, p, me).start()
            tile(2, p, me).start()

        others(j, both)

    def arrived(p):
        for which in range(2):
            rows_of(which, p, p).wait_recv()
            tile(which, p, p).wait_recv()

    own(0).wait()
    own_tile(0).wait()
    others(0, arrived)
    compute(my_group)
    own(1).start()
    own(2).start()
    own_tile(2).start()
    send_home(0)

    @pl.loop(1, groups)
    def _(j):
        others(j, arrived)
        compute((my_group + j) % groups)
        send_home(j)

    for f in range(parts):
        mine = slice(f * dp, (f + 1) * dp)
        for q in range(half // 256):
            cols = slice(f * half + q * 256, f * half + (q + 1) * 256)
            sub = slice(q * 256, (q + 1) * 256)
            low_first[mine, :, sub] = (
                dot(xs_ref[...], pre_ref[:, cols], TN).astype(LOW).reshape(dp, blk_d, 256)
            )
            low_second[mine, :, sub] = (
                dot(sg_ref[...], hid_ref[:, cols], TN).astype(LOW).reshape(dp, blk_d, 256)
            )
    save(8).start()
    save(9).start()
    save(8).wait()
    save(9).wait()
    own(1).wait()
    own(2).wait()
    own_tile(2).wait()
    to_core(core).wait_send()
    for i in range(1, spots):
        to_spot((spot + i) % spots, spot).wait_send()
    for copy in layer_sends:
        copy.wait_send()

    @pl.loop(1, n)
    def _(r):
        p = (me + r) % n
        rows_of(0, p, me).wait_send()
        for which in range(2):
            home(which, p, me).wait_send()
            home(which, p, p).wait_recv()
        for which in range(3):
            tile(which, p, me).wait_send()
        tile(2, p, p).wait_recv()


def backward_kernel(
    dp, images, experts, tok_in, cot_in, dense_in, qkv_in, att_in, lse_in, mid_in,
    two_in, route_in, col_in, out_in, grad_in, tiles_in, db_ref, dfirst_ref, dsecond_ref,
    result_ref, dtok_ref, done_ref, gin_ref, gback_ref,
    tok_ref, cot_ref, dense_ref, qkv_ref, att_ref, lse_ref, mid_ref,
    two_ref, route_ref, col_ref, out_ref, grad_ref, tiles_ref, in_sem,
    dmid_ref, datt_ref, dqkv_ref, ddense_ref, got_a, sum_a, got_b, sum_b, got_c,
    w_send, w_recv, own_sem, a_sems, b_send, b_recv, c_send, c_recv,
):
    rows, width = tok_ref.shape
    n = dfirst_ref.shape[0]
    tn = n // dp
    t_here, d_here = lax.axis_index("tensor"), lax.axis_index("dp")
    me = t_here * dp + d_here
    core, y_here, z_here = d_here % 2, (d_here // 2) % 2, d_here // 4
    spots, layers = 2 * tn, dp // 4
    spot = y_here * tn + t_here

    def device(p):
        return (p % dp, p // dp)

    def grads_to(which, p):
        src, dst = ((dfirst_ref, gin_ref), (dsecond_ref, gback_ref))[which]
        return pltpu.make_async_remote_copy(
            src_ref=src.at[p], dst_ref=dst.at[me],
            send_sem=w_send.at[which, p], recv_sem=w_recv.at[which, me],
            device_id=device(p), device_id_type=MESH,
        )

    def grads_from(which, p):
        src, dst = ((dfirst_ref, gin_ref), (dsecond_ref, gback_ref))[which]
        return pltpu.make_async_remote_copy(
            src_ref=src.at[p], dst_ref=dst.at[p],
            send_sem=w_send.at[which, p], recv_sem=w_recv.at[which, p],
            device_id=device(p), device_id_type=MESH,
        )

    def own(which):
        src, dst = ((dfirst_ref, gin_ref), (dsecond_ref, gback_ref))[which]
        return pltpu.make_async_copy(src.at[me], dst.at[me], own_sem.at[which])

    def to_spot(s):
        return pltpu.make_async_remote_copy(
            src_ref=sum_a.at[:, s], dst_ref=got_b.at[spot],
            send_sem=b_send.at[s], recv_sem=b_recv.at[spot],
            device_id=((z_here * 2 + s // tn) * 2 + core, s % tn), device_id_type=MESH,
        )

    def from_spot(s):
        return pltpu.make_async_remote_copy(
            src_ref=sum_a.at[:, s], dst_ref=got_b.at[s],
            send_sem=b_send.at[s], recv_sem=b_recv.at[s],
            device_id=((z_here * 2 + s // tn) * 2 + core, s % tn), device_id_type=MESH,
        )

    near, across = z_here + 1 - 2 * (z_here % 2), (z_here + 2) % layers

    def to_layer(src, z, place):
        return pltpu.make_async_remote_copy(
            src_ref=src, dst_ref=got_c.at[place],
            send_sem=c_send.at[place], recv_sem=c_recv.at[place],
            device_id=((z * 2 + y_here) * 2 + core, t_here), device_id_type=MESH,
        )

    layer_sends = (
        to_layer(sum_b.at[(near + 2) % layers], near, 0),
        to_layer(sum_b.at[near], near, 1),
        to_layer(got_c.at[3], across, 2),
    )

    slots_main = out_in.shape[0]
    moves = (
        (out_in, out_ref.at[0:slots_main]), (grad_in, grad_ref.at[0:slots_main]),
        (tiles_in, tiles_ref), (cot_in, cot_ref), (route_in, route_ref), (mid_in, mid_ref),
        (col_in, col_ref), (two_in, two_ref), (dense_in, dense_ref), (att_in, att_ref),
        (qkv_in, qkv_ref), (lse_in, lse_ref), (tok_in, tok_ref),
    )

    def bring(i):
        return pltpu.make_async_copy(moves[i][0], moves[i][1], in_sem.at[i])

    barrier = pltpu.get_barrier_semaphore()

    @pl.loop(1, n)
    def _(r):
        pl.semaphore_signal(barrier, inc=1, device_id=device((me + r) % n), device_id_type=MESH)

    for i in range(len(moves)):
        bring(i).start()
    pl.semaphore_wait(barrier, n - 1)

    @pl.loop(1, n)
    def _(r):
        grads_to(0, (me + r) % n).start()

    @pl.loop(1, 3 * n // 8)
    def _(r):
        grads_to(1, (me + r) % n).start()

    own(0).start()
    own(1).start()

    def put(cols, val):
        ddense_ref[:, :, :, cols] = val.reshape(ddense_ref.shape[:3] + (-1,)).astype(LOW)

    for i in range(len(moves)):
        bring(i).wait()
    tiles = tiles_ref[...].astype(WIDE).reshape(8 * n, 128).astype(LOW)
    rest = out_ref.shape[0] - slots_main
    for c in range(width // 128):
        cols = slice(c * 128, (c + 1) * 128)
        out_ref[slots_main:, cols] = from_tiles(tiles, c, rest).astype(LOW)
        grad_ref[slots_main:, cols] = from_tiles(tiles, width // 128 + c, rest).astype(LOW)

    misc_t = dense_ref[:, 4 * width : 4 * width + 128].astype(WIDE).T
    misc_low = misc_t.astype(LOW)
    gain_one, shift_one, bias, gain_two, shift_two = [
        misc_t[64 + i : 65 + i, :] for i in range(5)
    ]
    lanes = iota((1, 128), 1)
    per = 112
    slots_all = out_ref.shape[0]

    def chunk(c, carry):
        d_router, d_bias_back, d_gain, d_shift, d_bias = carry
        here = pl.ds(pl.multiple_of(c * per, 16), per)
        g = cot_ref[here, :]
        gw = g.astype(WIDE)
        route = route_ref[here, :]
        mid = mid_ref[here, :]
        result = mid
        probs = jnp.zeros((per, 128), WIDE)
        gate_sel = jnp.zeros((per, 128), WIDE)
        both = jnp.zeros((per, slots_all), WIDE)
        for k in range(2):
            choice = col_ref[here, k : k + 1]
            slot = col_ref[here, 2 + k : 3 + k]
            kept = slot >= 0
            chosen = (lanes == choice) & kept
            where_to = jnp.where(slot < MAIN, choice * MAIN + slot, slots_main + choice)
            where_to = jnp.where(kept, where_to, -1)
            hit = jnp.where(iota((per, slots_all), 1) == where_to, 1.0, 0.0)
            both = both + hit
            add_b = jnp.where((lanes == choice + experts) & kept, 1.0, 0.0).astype(LOW)
            picked = dot(hit.astype(LOW), out_ref[...]) + dot(add_b, misc_low)
            gate = jnp.sum(jnp.where(chosen, route, 0.0), axis=1, keepdims=True)
            result = result + gate * picked
            gg = jnp.sum(gw * picked, axis=1, keepdims=True)
            probs = probs + jnp.where(chosen, gg, 0.0)
            gate_sel = gate_sel + jnp.where(chosen, route, 0.0)
        result_ref[here, :] = result.astype(LOW)
        logits = route * (probs - jnp.sum(probs * route, axis=-1, keepdims=True))
        high, low = split_two(logits)
        d_two = dot(both.astype(LOW), grad_ref[...]) + dot(high, misc_low) + dot(low, misc_low)
        two = two_ref[here, :]
        d_router = d_router + dot(high, two, TN) + dot(low, two, TN)
        gs_high, gs_low = split_two(gate_sel)
        d_bias_back = d_bias_back + dot(gs_high, g, TN) + dot(gs_low, g, TN)
        xhat, rstd = normalize(mid)
        d_gain = d_gain + jnp.sum(d_two * xhat, axis=0, keepdims=True)
        d_shift = d_shift + jnp.sum(d_two, axis=0, keepdims=True)
        d_mid = gw + norm_back(d_two, xhat, rstd, gain_two)
        d_bias = d_bias + jnp.sum(d_mid, axis=0, keepdims=True)
        dtok_ref[here, :] = d_mid
        dmid_ref[here, :] = d_mid.astype(LOW)
        return d_router, d_bias_back, d_gain, d_shift, d_bias

    zero = jnp.zeros((1, width), WIDE)
    wide_zero = jnp.zeros((128, width), WIDE)
    d_router, d_bias_back, d_gain_two, d_shift_two, d_bias = lax.fori_loop(
        0, rows // per, chunk, (wide_zero, wide_zero, zero, zero, zero)
    )
    out_cols = slice(3 * width, 4 * width)
    datt_ref[...] = dot(dmid_ref[...], dense_ref[:, out_cols], NT).astype(LOW)
    put(out_cols, dot(att_ref[...], dmid_ref[...], TN))
    dqkv_ref[...] = jnp.zeros_like(dqkv_ref)
    low_half = iota((1, 128), 1) < HD

    @pl.loop(0, images)
    def _(i):
        win = pl.ds(pl.multiple_of(i * STEP, 16), WIN)
        first = i * (SEQ - STEP)
        key_pos = iota((1, WIN), 1)
        key_ok = (key_pos >= first) & (key_pos < first + SEQ)
        row_pos = iota((WIN, 1), 0)
        row_ok = (row_pos >= first) & (row_pos < first + SEQ)
        lse = lse_ref[win, :]
        for pair in range(H // 2):
            cols = [
                slice(j * width + pair * 128, j * width + (pair + 1) * 128) for j in range(3)
            ]
            q, k, v = [qkv_ref[win, c] for c in cols]
            do = datt_ref[win, pair * 128 : (pair + 1) * 128]
            do = jnp.where(row_ok, do, jnp.zeros_like(do))
            dq, dk, dv = [jnp.zeros((WIN, 128), WIDE) for _ in range(3)]
            for half in range(2):
                mask = low_half if half == 0 else jnp.logical_not(low_half)
                qm, km, dom = [jnp.where(mask, a, jnp.zeros_like(a)) for a in (q, k, do)]
                h = 2 * pair + half
                s = dot(qm, k, NT) * HD**-0.5
                p = jnp.where(key_ok & row_ok, jnp.exp(jnp.minimum(s - lse[:, h : h + 1], 0.0)), 0.0)
                dp = dot(dom, v, NT)
                delta = jnp.sum(dp * p, axis=-1, keepdims=True)
                ds = (p * (dp - delta) * HD**-0.5).astype(LOW)
                dv = dv + dot(p.astype(LOW), dom, TN)
                dq = dq + dot(ds, km)
                dk = dk + dot(ds, qm, TN)
            for c, val in zip(cols, (dq, dk, dv)):
                dqkv_ref[win, c] = jnp.where(row_ok, val.astype(LOW), dqkv_ref[win, c])

    xhat, rstd = normalize(tok_ref[...].astype(WIDE))
    one = (xhat * gain_one + shift_one).astype(LOW)
    d_one = jnp.zeros((rows, width), WIDE)
    for j in range(3):
        cols = slice(j * width, (j + 1) * width)
        put(cols, dot(one, dqkv_ref[:, cols], TN))
        d_one = d_one + dot(dqkv_ref[:, cols], dense_ref[:, cols], NT)
    d_gain_one = jnp.sum(d_one * xhat, axis=0, keepdims=True)
    d_shift_one = jnp.sum(d_one, axis=0, keepdims=True)
    dtok_ref[...] = dtok_ref[...] + norm_back(d_one, xhat, rstd, gain_one)
    row = iota((128, 1), 0)
    grads = jnp.where(row < experts, d_router, 0.0)
    moved = jnp.concatenate([d_bias_back[128 - experts :], d_bias_back[: 128 - experts]], axis=0)
    grads = grads + jnp.where((row >= experts) & (row < 2 * experts), moved, 0.0)
    for i, vec in enumerate((d_gain_one, d_shift_one, d_bias, d_gain_two, d_shift_two)):
        grads = grads + jnp.where(row == 64 + i, vec, 0.0)
    put(slice(4 * width, 4 * width + 128), grads.T)
    per_dp = experts // dp
    lines = ddense_ref.shape[2] // tn // per_dp
    count = tn * lines
    line = iota((count, 1), 0)
    slab = jnp.zeros((count, 128), WIDE)
    for i in range(count):
        slab = jnp.where(line == i, db_ref[:, i * 128 : (i + 1) * 128], slab)
    line = iota((width, count), 1)
    place = (me // per_dp * tn + line // lines) * (lines * per_dp) + me % per_dp * lines + line % lines
    placed = jnp.where(iota((width, count), 0) == place, 1.0, 0.0).astype(LOW)
    put(slice(4 * width + 128, 4 * width + 256), dot(placed, slab.astype(LOW)))

    partner = pltpu.make_async_remote_copy(
        src_ref=ddense_ref.at[:, 1 - core], dst_ref=got_a,
        send_sem=a_sems.at[0], recv_sem=a_sems.at[1],
        device_id=(d_here + 1 - 2 * core, t_here), device_id_type=MESH,
    )
    partner.start()
    partner.wait()
    total = ddense_ref[:, core].astype(WIDE) + got_a[...].astype(WIDE)
    sum_a[...] = total.reshape(sum_a.shape).astype(LOW)
    for i in range(1, spots):
        to_spot((spot + i) % spots).start()

    @pl.loop(3 * n // 8, 3 * n // 4)
    def _(r):
        grads_to(1, (me + r) % n).start()

    total = sum_a[:, spot].astype(WIDE)
    for i in range(1, spots):
        s = (spot + i) % spots
        from_spot(s).wait_recv()
        total = total + got_b[s].astype(WIDE)
    sum_b[...] = total.astype(LOW)
    layer_sends[0].start()
    layer_sends[1].start()

    @pl.loop(3 * n // 4, 7 * n // 8)
    def _(r):
        grads_to(1, (me + r) % n).start()

    layer_sends[0].wait_recv()
    got_c[3] = (sum_b[across].astype(WIDE) + got_c[0].astype(WIDE)).astype(LOW)
    layer_sends[2].start()

    @pl.loop(7 * n // 8, n)
    def _(r):
        grads_to(1, (me + r) % n).start()

    layer_sends[1].wait_recv()
    total = sum_b[z_here].astype(WIDE) + got_c[1].astype(WIDE)
    layer_sends[2].wait_recv()
    total = total + got_c[2].astype(WIDE)
    done_ref[...] = total

    own(0).wait()
    own(1).wait()
    for i in range(1, spots):
        to_spot((spot + i) % spots).wait_send()
    for copy in layer_sends:
        copy.wait_send()

    @pl.loop(1, n)
    def _(r):
        p = (me + r) % n
        for which in range(2):
            grads_to(which, p).wait_send()
            grads_from(which, p).wait_recv()


def finish_kernel(
    experts, done_ref, gin_ref, gback_ref, tok_ref, res_ref,
    din_ref, dback_ref, dtok_ref, result_ref, dqkv_ref, dwout_ref, drouter_ref, dbback_ref,
    dbin_ref, *refs,
):
    vec_refs, (low_ref, wide_ref, tok_held, res_held, in_sem, out_sem) = refs[:5], refs[5:]
    pieces = in_sem.shape[0] - 2
    each = low_ref.shape[0] // pieces
    n = gin_ref.shape[0]

    def bring(i):
        if i >= pieces:
            src, dst = ((tok_ref, tok_held), (res_ref, res_held))[i - pieces]
            return pltpu.make_async_copy(src, dst, in_sem.at[i])
        src = (gin_ref, gback_ref)[i * each // n]
        return pltpu.make_async_copy(
            src.at[i * each % n : i * each % n + each],
            low_ref.at[i * each : (i + 1) * each], in_sem.at[i],
        )

    def save(i):
        if i >= pieces:
            src, dst = ((tok_held, dtok_ref), (res_held, result_ref))[i - pieces]
            return pltpu.make_async_copy(src, dst, out_sem.at[i])
        dst = (din_ref, dback_ref)[i * each // n]
        return pltpu.make_async_copy(
            wide_ref.at[i * each : (i + 1) * each],
            dst.at[i * each % n : i * each % n + each], out_sem.at[i],
        )

    for i in range(pieces + 2):
        bring(i).start()
    dense_blk, width = dwout_ref.shape
    for j in range(3):
        dqkv_ref[j] = done_ref[:, j * width : (j + 1) * width]
    dwout_ref[...] = done_ref[:, 3 * width : 4 * width]
    misc = done_ref[:, 4 * width : 4 * width + 128]
    drouter_ref[...] = misc[:, :experts]
    dbback_ref[...] = misc[:, experts : 2 * experts]
    diagonal = iota((dense_blk, dense_blk), 0) == iota((dense_blk, dense_blk), 1)
    for i, vec in enumerate(vec_refs):
        column = misc[:, 2 * experts + i : 2 * experts + i + 1]
        vec[...] = jnp.sum(jnp.where(diagonal, column, 0.0), axis=0, keepdims=True)
    lines = dbin_ref.shape[1] // 128
    for i in range(dense_blk):
        dbin_ref[i // lines : i // lines + 1, (i % lines) * 128 : (i % lines + 1) * 128] = (
            done_ref[i : i + 1, 4 * width + 128 : 4 * width + 256]
        )
    for i in range(pieces + 2):
        bring(i).wait()
        if i < pieces:
            span = slice(i * each, (i + 1) * each)
            wide_ref[span] = low_ref[span].astype(WIDE)
        save(i).start()
    for i in range(pieces + 2):
        save(i).wait()


VMEM = pl.BlockSpec(memory_space=pltpu.VMEM)


def make_owner_device(dp, tn):
    n = dp * tn

    def per_device(
        tokens, cotangent, ln1_scale, ln1_shift, w_qkv, w_out, out_bias, ln2_scale, ln2_shift,
        w_router, w_in, b_in, w_back, b_back, choices, slots,
    ):
        rows, width = tokens.shape
        images = rows // SEQ
        experts, blk_d, blk_f = w_in.shape
        ff = blk_f * tn
        dense_blk = w_out.shape[0]
        places = experts * MAIN
        landed = n // 4 * GROUP
        shape = jax.ShapeDtypeStruct

        cols = 4 * width + 256
        per_layer = dp // 4

        hbm = pl.BlockSpec(memory_space=pl.ANY)
        saved = [
            ((per_layer, 2, 2, tn, dense_blk, cols), LOW),
            ((rows, 3 * width), LOW),
            ((rows, width), LOW),
            ((rows, 128), WIDE),
            ((rows, width), WIDE),
            ((rows, width), LOW),
            ((rows, 128), WIDE),
            ((rows, 128), jnp.int32),
        ]
        weight_shape = (n, blk_d, blk_f)
        out_home, back_home, tails_home, dense, qkv, att, lse, mid, two, route, col, d_first, d_second, d_b = pl.pallas_call(
            functools.partial(layer_kernel, dp, images, experts),
            out_shape=(
                shape((places, width), LOW),
                shape((places, width), LOW),
                shape((n, 8, 128), LOW),
                *[shape(*s) for s in saved],
                shape(weight_shape, LOW),
                shape(weight_shape, LOW),
                shape((1, ff), WIDE),
            ),
            in_specs=[VMEM] * 14 + [hbm, hbm],
            out_specs=(hbm,) * 13 + (VMEM,),
            scratch_shapes=[
                *[pltpu.VMEM(*saved[i]) for i in (0, 3, 4, 6, 7)],
                pltpu.VMEM((dense_blk, cols), LOW),
                pltpu.VMEM((2, rows), jnp.int32),
                pltpu.VMEM((2, 4, blk_d, blk_f), WIDE),
                pltpu.VMEM(weight_shape, LOW),
                pltpu.VMEM(weight_shape, LOW),
                pltpu.VMEM((tn, width, blk_f), LOW),
                pltpu.VMEM((tn, width, blk_f), LOW),
                pltpu.VMEM((1, ff), WIDE),
                pltpu.VMEM((places, width), LOW),
                pltpu.VMEM((places, width), LOW),
                pltpu.VMEM((landed, width), LOW),
                pltpu.VMEM((landed, width), LOW),
                pltpu.VMEM((landed, ff), LOW),
                pltpu.VMEM((landed, ff), LOW),
                pltpu.VMEM((places, width), LOW),
                pltpu.VMEM((n, rows), LOW),
                pltpu.VMEM((2, rows), jnp.int32),
                *[pltpu.VMEM((n, 8, 128), LOW)] * 5,
                pltpu.SemaphoreType.DMA((2,)),
                pltpu.SemaphoreType.DMA((2, n)),
                pltpu.SemaphoreType.DMA((2, n)),
                pltpu.SemaphoreType.DMA((n,)),
                pltpu.SemaphoreType.DMA((n,)),
                pltpu.SemaphoreType.DMA((n,)),
                pltpu.SemaphoreType.DMA((n,)),
                pltpu.SemaphoreType.DMA((2, n)),
                pltpu.SemaphoreType.DMA((2, n)),
                pltpu.SemaphoreType.DMA((3, n)),
                pltpu.SemaphoreType.DMA((3, n)),
                pltpu.SemaphoreType.DMA((per_layer,)),
                pltpu.SemaphoreType.DMA((per_layer,)),
                pltpu.SemaphoreType.DMA((2 * tn,)),
                pltpu.SemaphoreType.DMA((2 * tn,)),
                pltpu.SemaphoreType.DMA((2,)),
                pltpu.SemaphoreType.DMA((10,)),
                pltpu.SemaphoreType.DMA((10,)),
            ],
            compiler_params=pltpu.CompilerParams(
                vmem_limit_bytes=63 * 2**20, collective_id=1, has_side_effects=True
            ),
            cost_estimate=pl.CostEstimate(
                flops=12 * places * width * ff, bytes_accessed=10 * places * width, transcendentals=0
            ),
            name="layer",
        )(
            tokens, cotangent, choices.T, slots.T,
            *[v.reshape(1, dense_blk) for v in (ln1_scale, ln1_shift, out_bias, ln2_scale, ln2_shift)],
            w_qkv, w_out, w_router, b_back.T, b_in, w_in, jnp.swapaxes(w_back, 1, 2),
        )
        dense = dense.reshape(width, cols)
        brought = (
            tokens, cotangent, dense, qkv, att, lse, mid, two, route, col, out_home, back_home,
            tails_home,
        )
        result, d_tok, done, grad_in, grad_back = pl.pallas_call(
            functools.partial(backward_kernel, dp, images, experts),
            out_shape=(
                shape((rows, width), LOW),
                shape((rows, width), WIDE),
                shape((dense_blk, cols), WIDE),
                shape((n, blk_d, blk_f), LOW),
                shape((n, blk_d, blk_f), LOW),
            ),
            in_specs=[hbm] * 13 + [VMEM] + [hbm] * 2,
            out_specs=(VMEM, VMEM, VMEM, hbm, hbm),
            scratch_shapes=[
                *[pltpu.VMEM(v.shape, v.dtype) for v in brought[:10]],
                pltpu.VMEM((places + 128, width), LOW),
                pltpu.VMEM((places + 128, width), LOW),
                pltpu.VMEM((n, 8, 128), LOW),
                pltpu.SemaphoreType.DMA((13,)),
                pltpu.VMEM((rows, width), LOW),
                pltpu.VMEM((rows, width), LOW),
                pltpu.VMEM((rows, 3 * width), LOW),
                pltpu.VMEM((dp // 2, 2, tn * dense_blk, cols), LOW),
                pltpu.VMEM((dp // 2, tn * dense_blk, cols), LOW),
                pltpu.VMEM((per_layer, 2 * tn, dense_blk, cols), LOW),
                pltpu.VMEM((2 * tn, per_layer, dense_blk, cols), LOW),
                pltpu.VMEM((per_layer, dense_blk, cols), LOW),
                pltpu.VMEM((per_layer, dense_blk, cols), LOW),
                pltpu.SemaphoreType.DMA((2, n)),
                pltpu.SemaphoreType.DMA((2, n)),
                pltpu.SemaphoreType.DMA((2,)),
                pltpu.SemaphoreType.DMA((2,)),
                pltpu.SemaphoreType.DMA((2 * tn,)),
                pltpu.SemaphoreType.DMA((2 * tn,)),
                pltpu.SemaphoreType.DMA((per_layer,)),
                pltpu.SemaphoreType.DMA((per_layer,)),
            ],
            compiler_params=pltpu.CompilerParams(
                vmem_limit_bytes=60 * 2**20, collective_id=2, has_side_effects=True
            ),
            cost_estimate=pl.CostEstimate(
                flops=6 * places * rows * width + 20 * rows * width * width,
                bytes_accessed=40 * rows * width, transcendentals=0,
            ),
            name="backward",
        )(
            *brought, d_b, d_first, d_second,
        )
        vec = (1, dense_blk)
        small = [w_qkv.shape, w_out.shape, w_router.shape, (dense_blk, experts), b_in.shape] + [vec] * 5
        grad_in, grad_back, d_tok, result, *rest = pl.pallas_call(
            functools.partial(finish_kernel, experts),
            out_shape=(
                shape(weight_shape, WIDE),
                shape(weight_shape, WIDE),
                shape((rows, width), WIDE),
                shape((rows, width), LOW),
                *[shape(d, WIDE) for d in small],
            ),
            in_specs=[VMEM] + [hbm] * 4,
            out_specs=(hbm,) * 4 + (VMEM,) * len(small),
            scratch_shapes=[
                pltpu.VMEM((2 * n, blk_d, blk_f), LOW),
                pltpu.VMEM((2 * n, blk_d, blk_f), WIDE),
                pltpu.VMEM((rows, width), WIDE),
                pltpu.VMEM((rows, width), LOW),
                pltpu.SemaphoreType.DMA((18,)),
                pltpu.SemaphoreType.DMA((18,)),
            ],
            name="finish",
        )(done, grad_in, grad_back, d_tok, result)
        d_qkv, d_wout, d_router, d_bback, d_bin, *vecs = rest
        d_vecs = [v.reshape(dense_blk) for v in vecs]
        return (
            result,
            d_tok,
            d_vecs[0],
            d_vecs[1],
            d_qkv,
            d_wout,
            d_vecs[2],
            d_vecs[3],
            d_vecs[4],
            d_router,
            grad_in,
            d_bin,
            jnp.swapaxes(grad_back, 1, 2),
            d_bback.T,
        )

    return per_device


def make_per_device(dp, tn):
    everyone = ("dp", "tensor")
    n = dp * tn

    def per_device(
        tokens,
        cotangent,
        ln1_scale,
        ln1_shift,
        w_qkv,
        w_out,
        out_bias,
        ln2_scale,
        ln2_shift,
        w_router,
        w_in,
        b_in,
        w_back,
        b_back,
        choices,
        slots,
    ):
        rows_here, width = tokens.shape
        images = rows_here // SEQ
        experts, blk_d, blk_f = w_in.shape
        ff = blk_f * tn
        dense_blk = w_out.shape[0]
        whole = experts % n == 0
        owners = n if whole else dp
        owned = experts // owners
        expert_axes = ("tensor", "dp") if whole else ("dp",)
        slot_total = experts * CAP
        score_scale = HD ** (-0.5)

        w_pack = jnp.stack([w_in.astype(LOW), jnp.swapaxes(w_back, 1, 2).astype(LOW)], axis=1)
        w_all = lax.all_to_all(w_pack, expert_axes, split_axis=0, concat_axis=0, tiled=True)
        f_parts = tn if whole else 1
        w_all = w_all.reshape(f_parts, dp, owned, 2, blk_d, blk_f)
        w_all = w_all.transpose(3, 2, 1, 4, 0, 5).reshape(2, owned, width, f_parts * blk_f)
        first_w, second_wt = w_all[0], w_all[1]

        vec_rows = jnp.stack([ln1_scale, ln1_shift, out_bias, ln2_scale, ln2_shift])
        pieces = [
            w_qkv.reshape(-1),
            w_out.reshape(-1),
            w_router.reshape(-1),
            b_back.reshape(-1),
            b_in.reshape(-1),
            vec_rows.reshape(-1),
        ]
        sizes = [p.shape[0] for p in pieces]
        total = sum(sizes)
        pad = -total % 512
        packed = jnp.concatenate([p.astype(LOW) for p in pieces] + [jnp.zeros((pad,), LOW)])
        gathered = lax.all_gather(packed.reshape(-1, 512), everyone, axis=0, tiled=False)
        gathered = gathered.reshape(n, -1)
        offs = [sum(sizes[:i]) for i in range(len(sizes))]
        part = [gathered[:, o : o + s] for o, s in zip(offs, sizes)]
        qkv_w = part[0].reshape(n, 3, dense_blk, width).swapaxes(0, 1).reshape(3, width, width)
        out_w = part[1].reshape(width, width)
        router = part[2].reshape(width, experts)
        bias_back = part[3].reshape(n, experts, -1).swapaxes(0, 1).reshape(experts, width)
        bias_back = bias_back.astype(WIDE)
        in_b = part[4].reshape(dp, tn, experts // dp, blk_f).swapaxes(1, 2).reshape(experts, ff)
        vecs = part[5].reshape(n, 5, -1).swapaxes(0, 1).reshape(5, width).astype(WIDE)
        gain_one, shift_one, bias_attn, gain_two, shift_two = vecs
        if whole:
            mine = lax.axis_index("tensor") * dp + lax.axis_index("dp")
            my_b = lax.dynamic_slice(in_b, (mine * owned, 0), (owned, ff)).astype(WIDE)
        else:
            my_b = lax.dynamic_slice(
                in_b,
                (lax.axis_index("dp") * owned, lax.axis_index("tensor") * blk_f),
                (owned, blk_f),
            ).astype(WIDE)

        residual = tokens.astype(WIDE)
        normed_one = norm_affine(residual, gain_one, shift_one).astype(LOW)
        projected = jnp.einsum(
            "td,jde->jte", normed_one, qkv_w, preferred_element_type=WIDE
        ).astype(LOW)
        head_query = projected[0].reshape(images, SEQ, H, HD)
        head_key = projected[1].reshape(images, SEQ, H, HD)
        head_value = projected[2].reshape(images, SEQ, H, HD)
        raw_scores = jnp.einsum(
            "ishd,ithd->ihst", head_query, head_key, preferred_element_type=WIDE
        )
        scaled = raw_scores * score_scale
        row_top = jnp.max(scaled, axis=-1, keepdims=True)
        log_total = row_top + jnp.log(jnp.sum(jnp.exp(scaled - row_top), axis=-1, keepdims=True))
        weights_att = jnp.exp(scaled - log_total).astype(LOW)
        attended = (
            jnp.einsum("ihst,ithd->ishd", weights_att, head_value, preferred_element_type=WIDE)
            .astype(LOW)
            .reshape(rows_here, width)
        )
        attn_sum = jnp.dot(attended, out_w, preferred_element_type=WIDE)
        middle = residual + attn_sum + bias_attn
        normed_two = norm_affine(middle, gain_two, shift_two).astype(LOW)
        route_p = jax.nn.softmax(jnp.dot(normed_two, router, preferred_element_type=WIDE), axis=-1)

        expert_ids = jnp.arange(experts, dtype=jnp.int32)
        chosen = [
            (choices[:, k : k + 1] == expert_ids[None, :]).astype(WIDE) for k in range(2)
        ]
        gate_vals = jnp.concatenate(
            [jnp.sum(route_p * c, axis=1, keepdims=True) for c in chosen], axis=1
        )
        kept_pair = (slots >= 0).astype(WIDE)
        target = jnp.where(slots >= 0, choices * CAP + slots, -1)
        places = jnp.arange(slot_total, dtype=jnp.int32)
        by_slot = [target[:, k][None, :] == places[:, None] for k in range(2)]
        spread_mat = (by_slot[0] | by_slot[1]).astype(LOW)
        by_token = [target[:, k : k + 1] == places[None, :] for k in range(2)]
        pair_weight = gate_vals * kept_pair
        slot_gate = jnp.sum(
            jnp.where(by_slot[0], pair_weight[:, 0][None, :], 0.0)
            + jnp.where(by_slot[1], pair_weight[:, 1][None, :], 0.0),
            axis=1,
            keepdims=True,
        )
        both = jnp.dot(
            spread_mat,
            jnp.concatenate([normed_two, cotangent], axis=1),
            preferred_element_type=WIDE,
        )
        buffer = both[:, :width].astype(LOW).reshape(experts, CAP, width)
        slot_grad = slot_gate * both[:, width:]
        grad_bias_back = jnp.sum(slot_grad.reshape(experts, CAP, width), axis=1)
        slot_grad_low = slot_grad.astype(LOW).reshape(experts, CAP, width)

        def out_to_experts(rows):
            width_c = rows.shape[1]
            if not whole:
                rows = lax.all_gather(rows, "tensor", axis=1, tiled=True)
            rows = lax.all_to_all(rows, expert_axes, split_axis=0, concat_axis=0, tiled=True)
            return rows.reshape(owners, owned, -1, width)

        def back_to_tokens(rows):
            rows = rows.reshape(experts, -1, width)
            rows = lax.all_to_all(rows, expert_axes, split_axis=0, concat_axis=0, tiled=True)
            if not whole:
                rows = lax.psum_scatter(rows, "tensor", scatter_dimension=1, tiled=True)
            return rows

        sent = out_to_experts(jnp.concatenate([buffer, slot_grad_low], axis=1))
        group = sent.shape[2] // (2 * CAP)
        sent = sent.reshape(owners, owned, group, 2, CAP, width).transpose(3, 1, 0, 2, 4, 5)
        sent = sent.reshape(2, owned, owners * group * CAP, width)
        all_slots, slot_grad_all = sent[0], sent[1]

        pre_act = (
            jnp.einsum("ecd,edf->ecf", all_slots, first_w, preferred_element_type=WIDE)
            + my_b[:, None, :]
        )
        hidden, gelu_pull = jax.vjp(lambda member: jax.nn.gelu(member, approximate=True), pre_act)
        hidden = hidden.astype(LOW)
        expert_sum = jnp.einsum("ecf,edf->ecd", hidden, second_wt, preferred_element_type=WIDE)
        grad_hidden = jnp.einsum("ecd,edf->ecf", slot_grad_all, second_wt, preferred_element_type=WIDE)
        grad_pre = gelu_pull(grad_hidden)[0].astype(LOW)
        grad_slots_all = jnp.einsum("ecf,edf->ecd", grad_pre, first_w, preferred_element_type=WIDE)
        returned = jnp.stack([expert_sum.astype(LOW), grad_slots_all.astype(LOW)])
        returned = returned.reshape(2, owned, owners, group, CAP, width).transpose(2, 1, 3, 0, 4, 5)
        returned = returned.reshape(owners * owned, group * 2 * CAP, width)
        home = back_to_tokens(returned).reshape(experts, 2, CAP, width)
        expert_home = home[:, 0].reshape(slot_total, width)
        grad_home = home[:, 1].reshape(slot_total, width)

        grad_first_b = jnp.sum(grad_pre.astype(WIDE), axis=1)
        grad_first_w = jnp.einsum("ecd,ecf->edf", all_slots, grad_pre, preferred_element_type=WIDE)
        grad_second_t = jnp.einsum("ecd,ecf->edf", slot_grad_all, hidden, preferred_element_type=WIDE)
        g_pack = jnp.stack([grad_first_w.astype(LOW), grad_second_t.astype(LOW)])
        g_pack = g_pack.reshape(2, owned, dp, blk_d, f_parts, blk_f).transpose(4, 2, 1, 0, 3, 5)
        g_pack = g_pack.reshape(f_parts * dp * owned, 2, blk_d, blk_f)
        g_home = lax.all_to_all(g_pack, expert_axes, split_axis=0, concat_axis=0, tiled=True)
        g_home = g_home.reshape(experts, 2, blk_d, blk_f).astype(WIDE)
        grad_w_in = g_home[:, 0]
        grad_w_back = jnp.swapaxes(g_home[:, 1], 1, 2)

        picked = []
        for k in range(2):
            rows = jnp.dot(by_token[k].astype(LOW), expert_home, preferred_element_type=WIDE)
            bias_rows = jnp.dot(
                chosen[k].astype(LOW), bias_back.astype(LOW), preferred_element_type=WIDE
            )
            picked.append((rows + bias_rows) * kept_pair[:, k : k + 1])
        result = (
            middle + gate_vals[:, 0:1] * picked[0] + gate_vals[:, 1:2] * picked[1]
        ).astype(LOW)
        grad_out = cotangent.astype(WIDE)
        grad_probs = sum(
            jnp.sum(grad_out * picked[k], axis=1, keepdims=True) * chosen[k] for k in range(2)
        )
        gather_mat = (by_token[0] | by_token[1]).astype(LOW)
        grad_normed_two = jnp.dot(gather_mat, grad_home, preferred_element_type=WIDE)
        grad_logits = route_p * (grad_probs - jnp.sum(grad_probs * route_p, axis=-1, keepdims=True))
        grad_normed_two = grad_normed_two + jnp.dot(
            grad_logits, router.astype(WIDE).T, precision=lax.Precision.HIGHEST
        )
        grad_router = jnp.dot(
            normed_two.astype(WIDE).T, grad_logits, precision=lax.Precision.HIGHEST
        )
        _, pull_two = jax.vjp(norm_affine, middle, gain_two, shift_two)
        grad_mid_norm, grad_gain_two, grad_shift_two = pull_two(grad_normed_two)
        grad_middle = grad_out + grad_mid_norm
        grad_bias_attn = jnp.sum(grad_middle, axis=0)
        grad_mid_low = grad_middle.astype(LOW)
        grad_att = jnp.einsum(
            "td,ed->te", grad_mid_low, out_w, preferred_element_type=WIDE
        ).astype(LOW)
        grad_out_w = jnp.einsum("te,td->ed", attended, grad_mid_low, preferred_element_type=WIDE)
        grad_att_heads = grad_att.reshape(images, SEQ, H, HD)
        probs_again = jnp.exp(
            jnp.einsum("ishd,ithd->ihst", head_query, head_key, preferred_element_type=WIDE)
            * score_scale
            - log_total
        )
        grad_weights = jnp.einsum(
            "ishd,ithd->ihst", grad_att_heads, head_value, preferred_element_type=WIDE
        )
        row_delta = jnp.sum(grad_weights * probs_again, axis=-1, keepdims=True)
        grad_raw = (probs_again * (grad_weights - row_delta) * score_scale).astype(LOW)
        grad_value = jnp.einsum(
            "ihst,ishd->ithd",
            probs_again.astype(LOW),
            grad_att_heads,
            preferred_element_type=WIDE,
        )
        grad_query = jnp.einsum("ihst,ithd->ishd", grad_raw, head_key, preferred_element_type=WIDE)
        grad_key = jnp.einsum("ihst,ishd->ithd", grad_raw, head_query, preferred_element_type=WIDE)
        grad_proj = jnp.stack(
            [
                grad_query.astype(LOW).reshape(rows_here, width),
                grad_key.astype(LOW).reshape(rows_here, width),
                grad_value.astype(LOW).reshape(rows_here, width),
            ]
        )
        grad_qkv_w = jnp.einsum("td,jte->jde", normed_one, grad_proj, preferred_element_type=WIDE)
        grad_normed_one = jnp.einsum("jte,jde->td", grad_proj, qkv_w, preferred_element_type=WIDE)
        _, pull_one = jax.vjp(norm_affine, residual, gain_one, shift_one)
        grad_resid_norm, grad_gain_one, grad_shift_one = pull_one(grad_normed_one)
        grad_tokens = grad_middle + grad_resid_norm

        if whole:
            row_b = jnp.zeros((experts, ff), WIDE)
            row_b = lax.dynamic_update_slice(row_b, grad_first_b, (mine * owned, 0))
        else:
            row_b = jnp.zeros((experts, ff), WIDE)
            row_b = lax.dynamic_update_slice(
                row_b,
                grad_first_b,
                (lax.axis_index("dp") * owned, lax.axis_index("tensor") * blk_f),
            )
        vec_grads = jnp.stack(
            [grad_gain_one, grad_shift_one, grad_bias_attn, grad_gain_two, grad_shift_two]
        )
        out_pieces = [
            grad_qkv_w.reshape(3, n, dense_blk, width).swapaxes(0, 1).reshape(n, -1),
            grad_out_w.reshape(n, -1),
            grad_router.reshape(n, -1),
            grad_bias_back.reshape(experts, n, -1).swapaxes(0, 1).reshape(n, -1),
            row_b.reshape(dp, experts // dp, tn, blk_f).swapaxes(1, 2).reshape(n, -1),
            vec_grads.reshape(5, n, -1).swapaxes(0, 1).reshape(n, -1),
        ]
        out_pack = jnp.concatenate(
            [p.astype(LOW) for p in out_pieces] + [jnp.zeros((n, pad), LOW)], axis=1
        )
        out_all = lax.all_to_all(
            out_pack.reshape(n, -1, 512), everyone, split_axis=0, concat_axis=0, tiled=True
        )
        summed = jnp.sum(out_all.astype(WIDE), axis=0).reshape(-1)
        done = [summed[o : o + s] for o, s in zip(offs, sizes)]
        vec_done = done[5].reshape(5, -1)
        return (
            result,
            grad_tokens,
            vec_done[0],
            vec_done[1],
            done[0].reshape(w_qkv.shape),
            done[1].reshape(w_out.shape),
            vec_done[2],
            vec_done[3],
            vec_done[4],
            done[2].reshape(w_router.shape),
            grad_w_in,
            done[4].reshape(b_in.shape),
            grad_w_back,
            done[3].reshape(b_back.shape),
        )

    return per_device


def solution(mesh):
    everyone = ("dp", "tensor")
    in_specs = (
        P(everyone, None),
        P(everyone, None),
        P(everyone),
        P(everyone),
        P(None, everyone, None),
        P(everyone, None),
        P(everyone),
        P(everyone),
        P(everyone),
        P(everyone, None),
        P(None, "dp", "tensor"),
        P("dp", "tensor"),
        P(None, "tensor", "dp"),
        P(None, everyone),
        P(everyone, None),
        P(everyone, None),
    )
    out_specs = in_specs[:2] + in_specs[2:14]
    dp, tn = mesh.shape["dp"], mesh.shape["tensor"]

    def chosen(*args):
        one_each = args[10].shape[0] == dp * tn and dp // 4 == 4 and dp % 4 == 0
        return (make_owner_device if one_each else make_per_device)(dp, tn)(*args)

    return jax.shard_map(
        chosen,
        mesh=mesh,
        in_specs=in_specs,
        out_specs=out_specs,
        check_vma=False,
    )
```

```python
import functools

import jax
import jax.numpy as jnp
from jax import lax
from jax.experimental import pallas as pl
from jax.experimental.pallas import tpu as pltpu
from jax.sharding import PartitionSpec as P

H = 8
HD = 64
SEQ = 196
CAP = 65
LOW = jnp.bfloat16
WIDE = jnp.float32


def norm_affine(values_in, gain_vec, shift_vec):
    center = values_in - jnp.mean(values_in, axis=-1, keepdims=True)
    spread = jnp.mean(center * center, axis=-1, keepdims=True)
    return center * lax.rsqrt(spread + 1e-06) * gain_vec + shift_vec


MAIN = CAP - 1
GROUP = 4 * MAIN + 16
WIN = 208
STEP = 192


def dot(a, b, dims=((1,), (0,))):
    return lax.dot_general(a, b, (dims, ((), ())), preferred_element_type=WIDE)


NT = ((1,), (1,))
TN = ((0,), (0,))
MESH = pl.DeviceIdType.MESH


def to_tiles(pieces):
    m = pieces[0].shape[0]
    gap = iota((8 * m, m), 0) - 8 * iota((8 * m, m), 1)
    return sum(
        dot(jnp.where(gap == c, 1.0, 0.0).astype(LOW), piece) for c, piece in enumerate(pieces)
    )


def from_tiles(tiles, c, rows):
    gap = iota((rows, tiles.shape[0]), 1) - 8 * iota((rows, tiles.shape[0]), 0)
    return dot(jnp.where(gap == c, 1.0, 0.0).astype(LOW), tiles)


def lane_blocks(v):
    return [v[:, c * 128 : (c + 1) * 128] for c in range(v.shape[1] // 128)]


def split_two(v):
    high = v.astype(LOW)
    return high, (v - high.astype(WIDE)).astype(LOW)


def iota(shape, dim):
    return lax.broadcasted_iota(jnp.int32, shape, dim)


def normalize(v):
    center = v - jnp.mean(v, axis=-1, keepdims=True)
    rstd = lax.rsqrt(jnp.mean(center * center, axis=-1, keepdims=True) + 1e-06)
    return center * rstd, rstd


def norm_back(grad, xhat, rstd, gain):
    inner = grad * gain
    return rstd * (
        inner
        - jnp.mean(inner, axis=-1, keepdims=True)
        - xhat * jnp.mean(inner * xhat, axis=-1, keepdims=True)
    )


def layer_kernel(
    dp, images, experts, tok_ref, cot_ref, choice_ref, slot_ref, gain_one_ref, shift_one_ref,
    bias_ref, gain_two_ref, shift_two_ref, wqkv_ref, wout_ref, router_ref, bback_ref, bin_ref,
    win_ref, wback_ref,
    out_ref, grad_ref, tail_out, dense_out, qkv_out, att_out, lse_out, mid_out, two_out, route_out,
    col_out, dfirst_out, dsecond_out, db_ref,
    dense_ref, lse_ref, mid_ref, route_ref, col_ref, shard_ref, rows_ref,
    wide_ref, low_first, low_second, first_ref, second_ref, b_ref,
    x_ref, g_ref, xs_ref, sg_ref, hid_ref, pre_ref, backs_ref,
    tails_ref, last_ref, x_tiles, g_tiles, xs_tiles, gs_tiles, home_tiles,
    stage_sem, w_send, w_recv, g_send, g_recv, x_send, x_recv, r_send, r_recv,
    t_send, t_recv, c_send, c_recv, s_send, s_recv, a_sems, own_sem, save_sem,
):
    outs_ref = g_ref
    total, width = g_ref.shape
    rows = tok_ref.shape[0]
    qkv_ref = pre_ref.at[0:rows, 0 : 3 * width]
    att_ref = pre_ref.at[0:rows, 3 * width : 4 * width]
    two_ref = hid_ref.at[0:rows, 0:width]
    n = total // MAIN
    tn = n // dp
    parts, _, half = first_ref.shape
    blk_d = low_first.shape[1]
    dense_blk = shard_ref.shape[0]
    groups = n // 4
    per = GROUP
    t_here, d_here = lax.axis_index("tensor"), lax.axis_index("dp")
    me = t_here * dp + d_here
    my_group, my_place = me // 4, me % 4
    core, y_here, z_here = d_here % 2, (d_here // 2) % 2, d_here // 4
    spots, layers = 2 * tn, dp // 4
    spot = y_here * tn + t_here

    def device(p):
        return (p % dp, p // dp)

    def block(p):
        return pl.ds(pl.multiple_of(p * MAIN, 16), MAIN)

    def landing(p):
        return pl.ds(pl.multiple_of(p // 4 * GROUP + p % 4 * MAIN, 16), MAIN)

    tiles = ((x_tiles, xs_tiles), (g_tiles, gs_tiles), (home_tiles, tail_out))

    def tile(which, p, source):
        src, dst = tiles[which]
        return pltpu.make_async_remote_copy(
            src_ref=src.at[p], dst_ref=dst.at[source],
            send_sem=t_send.at[which, p], recv_sem=t_recv.at[which, source],
            device_id=device(p), device_id_type=MESH,
        )

    def own_tile(which):
        src, dst = tiles[which]
        return pltpu.make_async_copy(src.at[me], dst.at[me], own_sem.at[7 + which])

    def weight_rows(p):
        return pl.ds(pl.multiple_of((p % dp) * blk_d, 16), blk_d)

    def weights(which, p, source):
        src, dst = ((low_first, first_ref), (low_second, second_ref))[which]
        return pltpu.make_async_remote_copy(
            src_ref=src.at[p], dst_ref=dst.at[source // dp, weight_rows(source)],
            send_sem=w_send.at[which, p], recv_sem=w_recv.at[which, source],
            device_id=device(p), device_id_type=MESH,
        )

    def own_weights(which):
        src, dst = ((low_first, first_ref), (low_second, second_ref))[which]
        return pltpu.make_async_copy(
            src.at[me], dst.at[t_here, weight_rows(me)], own_sem.at[3 + which]
        )

    def rows_of(which, p, source):
        src, dst, send, recv = (
            (x_ref, xs_ref, x_send, x_recv), (g_ref, sg_ref, g_send, g_recv)
        )[which]
        return pltpu.make_async_remote_copy(
            src_ref=src.at[block(p)], dst_ref=dst.at[landing(source)],
            send_sem=send.at[p], recv_sem=recv.at[source],
            device_id=device(p), device_id_type=MESH,
        )

    def home(which, p, source):
        src, dst = ((outs_ref, out_ref), (backs_ref, grad_ref))[which]
        return pltpu.make_async_remote_copy(
            src_ref=src.at[block(p)], dst_ref=dst.at[block(source)],
            send_sem=r_send.at[which, p], recv_sem=r_recv.at[which, source],
            device_id=device(p), device_id_type=MESH,
        )

    def own(which):
        src, dst = (
            (x_ref, xs_ref), (outs_ref, out_ref), (backs_ref, grad_ref),
            None, None, (g_ref, sg_ref),
        )[which]
        place = block(me) if which in (1, 2) else landing(me)
        return pltpu.make_async_copy(src.at[block(me)], dst.at[place], own_sem.at[which])

    near, across = z_here + 1 - 2 * (z_here % 2), (z_here + 2) % layers

    def shard_at(source):
        return dense_ref.at[source, y_here, core, t_here]

    def to_layer(src, z, source, place):
        return pltpu.make_async_remote_copy(
            src_ref=src, dst_ref=shard_at(source),
            send_sem=c_send.at[place], recv_sem=c_recv.at[source],
            device_id=((z * 2 + y_here) * 2 + core, t_here), device_id_type=MESH,
        )

    def from_layer(source):
        return to_layer(shard_at(source), near, source, 0)

    layer_sends = (
        to_layer(shard_ref, near, z_here, 0),
        to_layer(shard_ref, across, z_here, 1),
        to_layer(shard_at(across), near, across, 2),
    )

    def to_spot(s, source):
        return pltpu.make_async_remote_copy(
            src_ref=dense_ref.at[:, y_here, core, t_here],
            dst_ref=dense_ref.at[:, source // tn, core, source % tn],
            send_sem=s_send.at[s], recv_sem=s_recv.at[source],
            device_id=((z_here * 2 + s // tn) * 2 + core, s % tn), device_id_type=MESH,
        )

    def to_core(source):
        return pltpu.make_async_remote_copy(
            src_ref=dense_ref.at[:, :, core], dst_ref=dense_ref.at[:, :, source],
            send_sem=a_sems.at[0], recv_sem=a_sems.at[1],
            device_id=(d_here + 1 - 2 * core, t_here), device_id_type=MESH,
        )

    own_shard = pltpu.make_async_copy(
        shard_ref, dense_ref.at[z_here, y_here, core, t_here], own_sem.at[6]
    )
    pieces = wide_ref.shape[1]
    chunks = n // pieces

    def stage(which, j):
        src = (win_ref, wback_ref)[which]
        c = (me // pieces + j) % chunks
        return pltpu.make_async_copy(
            src.at[pl.ds(c * pieces, pieces)], wide_ref.at[j % 2], stage_sem.at[j % 2]
        )

    barrier = pltpu.get_barrier_semaphore()

    @pl.loop(1, n)
    def _(r):
        pl.semaphore_signal(barrier, inc=1, device_id=device((me + r) % n), device_id_type=MESH)

    stage(0, 0).start()
    for j in range(3):
        shard_ref[:, j * width : (j + 1) * width] = wqkv_ref[j].astype(LOW)
    shard_ref[:, 3 * width : 4 * width] = wout_ref[...].astype(LOW)
    diagonal = iota((dense_blk, dense_blk), 0) == iota((dense_blk, dense_blk), 1)
    lanes = iota((1, 128), 1)
    spread = iota((experts, 128), 1) - iota((experts, 128), 0)
    misc = dot(router_ref[...].astype(LOW), jnp.where(spread == 0, 1.0, 0.0).astype(LOW))
    misc = misc + dot(
        bback_ref[...].astype(LOW), jnp.where(spread == experts, 1.0, 0.0).astype(LOW)
    )
    vectors = (gain_one_ref, shift_one_ref, bias_ref, gain_two_ref, shift_two_ref)
    for i, vec in enumerate(vectors):
        column = jnp.sum(jnp.where(diagonal, vec[...], 0.0), axis=1, keepdims=True)
        misc = jnp.where(lanes == 64 + i, column, misc)
    shard_ref[:, 4 * width : 4 * width + 128] = misc.astype(LOW)
    lines = half // 128
    slab = jnp.zeros((dense_blk, 128), WIDE)
    for i in range(dense_blk):
        part = bin_ref[i // lines : i // lines + 1, (i % lines) * 128 : (i % lines + 1) * 128]
        slab = jnp.where(iota((dense_blk, 1), 0) == i, part, slab)
    shard_ref[:, 4 * width + 128 : 4 * width + 256] = slab.astype(LOW)
    slot_in = slot_ref[...]
    rows_ref[...] = jnp.where(
        (slot_in >= 0) & (slot_in < MAIN), choice_ref[...] * MAIN + slot_in, -1
    )
    last_ref[...] = jnp.where(slot_in == MAIN, choice_ref[...], -1)
    pick = iota((2, 128), 1) - iota((2, 128), 0)
    turned = dot(
        choice_ref[...].astype(WIDE).astype(LOW), jnp.where(pick == 0, 1.0, 0.0).astype(LOW), TN
    ) + dot(slot_ref[...].astype(WIDE).astype(LOW), jnp.where(pick == 2, 1.0, 0.0).astype(LOW), TN)
    col_ref[...] = turned.astype(jnp.int32)
    own_shard.start()
    db_ref[...] = jnp.zeros_like(db_ref)
    pl.semaphore_wait(barrier, n - 1)
    layer_sends[1].start()
    layer_sends[0].start()

    def send_weights(which):
        low = (low_first, low_second)[which]
        for j in range(chunks):
            if j + 1 < chunks:
                stage(which, j + 1).start()
            elif which == 0:
                stage(1, 0).start()
            stage(which, j).wait()
            c = (me // pieces + j) % chunks
            low[pl.ds(c * pieces, pieces)] = wide_ref[j % 2].astype(LOW)

            @pl.loop(0, pieces)
            def _(i):
                p = c * pieces + (me + i) % pieces

                @pl.when(p != me)
                def _():
                    weights(which, p, me).start()

        own_weights(which).start()

    send_weights(0)
    from_layer(across).wait_recv()
    layer_sends[2].start()
    send_weights(1)
    own_shard.wait()
    from_layer(near).wait_recv()
    from_layer((near + 2) % layers).wait_recv()
    for i in range(1, spots):
        to_spot((spot + i) % spots, spot).start()

    some = 8
    big = some * MAIN
    place = iota((n, rows), 0)
    last_hit = (place == last_ref[0:1, :]) | (place == last_ref[1:2, :])
    tails_ref[...] = jnp.where(last_hit, 1.0, 0.0).astype(LOW)
    got = dot(tails_ref[...], cot_ref[...]).astype(LOW)
    g_tiles[...] = to_tiles(lane_blocks(got)).reshape(n, 8, 128).astype(LOW)

    @pl.loop(0, n // some)
    def _(j):
        c = (me // some + j) % (n // some)
        place = iota((big, rows), 0) + c * big
        hit = (place == rows_ref[0:1, :]) | (place == rows_ref[1:2, :])
        got = dot(jnp.where(hit, 1.0, 0.0).astype(LOW), cot_ref[...])
        g_ref[pl.ds(pl.multiple_of(c * big, 16), big), :] = got.astype(LOW)

        @pl.loop(0, some)
        def _(i):
            p = c * some + (me + i) % some

            @pl.when(p != me)
            def _():
                rows_of(1, p, me).start()
                tile(1, p, me).start()

    own(5).start()
    own_tile(1).start()
    for i in range(1, spots):
        s = (spot + i) % spots
        to_spot(s, s).wait_recv()
    to_core(core).start()
    to_core(1 - core).wait_recv()

    def dense(cols):
        return dense_ref[:, :, :, :, :, cols].reshape(width, -1)

    misc = dense(slice(4 * width, 4 * width + 128))
    misc_t = misc.astype(WIDE).T
    gain_one, shift_one, bias, gain_two, shift_two = [
        misc_t[64 + i : 65 + i, :] for i in range(5)
    ]
    base = tok_ref[...].astype(WIDE)
    xhat, _ = normalize(base)
    one = (xhat * gain_one + shift_one).astype(LOW)
    for j in range(3):
        cols = slice(j * width, (j + 1) * width)
        qkv_ref[:, cols] = dot(one, dense(cols)).astype(LOW)
    att_ref[...] = jnp.zeros((rows, width), LOW)
    lse_ref[...] = jnp.zeros_like(lse_ref)
    low_half = iota((1, 128), 1) < HD

    @pl.loop(0, images)
    def _(i):
        win = pl.ds(pl.multiple_of(i * STEP, 16), WIN)
        first = i * (SEQ - STEP)
        key_pos = iota((1, WIN), 1)
        key_ok = (key_pos >= first) & (key_pos < first + SEQ)
        row_pos = iota((WIN, 1), 0)
        row_ok = (row_pos >= first) & (row_pos < first + SEQ)
        lse = jnp.zeros((WIN, 128), WIDE)
        for pair in range(H // 2):
            q = qkv_ref[win, pair * 128 : (pair + 1) * 128]
            k = qkv_ref[win, width + pair * 128 : width + (pair + 1) * 128]
            v = qkv_ref[win, 2 * width + pair * 128 : 2 * width + (pair + 1) * 128]
            outs = []
            for side in range(2):
                mask = low_half if side == 0 else jnp.logical_not(low_half)
                qm = jnp.where(mask, q, jnp.zeros_like(q))
                s = jnp.where(key_ok, dot(qm, k, NT) * HD**-0.5, -1e30)
                top = jnp.max(s, axis=-1, keepdims=True)
                p = jnp.exp(s - top)
                all_p = jnp.sum(p, axis=-1, keepdims=True)
                p = (p / all_p).astype(LOW)
                outs.append(dot(p, v))
                lane = iota((1, 128), 1) == 2 * pair + side
                lse = jnp.where(lane, top + jnp.log(all_p), lse)
            got = jnp.where(low_half, outs[0], outs[1]).astype(LOW)
            cols = slice(pair * 128, (pair + 1) * 128)
            att_ref[win, cols] = jnp.where(row_ok, got, att_ref[win, cols])
        lse_ref[win, :] = jnp.where(row_ok, lse, lse_ref[win, :])

    mid = base + dot(att_ref[...], dense(slice(3 * width, 4 * width))) + bias
    mid_ref[...] = mid
    xhat, _ = normalize(mid)
    two = (xhat * gain_two + shift_two).astype(LOW)
    two_ref[...] = two
    lanes = iota((1, 128), 1)
    logits = jnp.where(lanes < experts, dot(two, misc), -1e30)
    route = jnp.exp(logits - jnp.max(logits, axis=-1, keepdims=True))
    route = route / jnp.sum(route, axis=-1, keepdims=True)
    route_ref[...] = route
    high, low = jnp.zeros((128, 128), WIDE), jnp.zeros((128, 128), WIDE)
    for k in range(2):
        chosen = lanes == col_ref[:, k : k + 1]
        gate = jnp.where(chosen, route, 0.0)
        here = jnp.where(lanes == col_ref[:, 2 + k : 3 + k], 1.0, 0.0).astype(LOW)
        part_high, part_low = split_two(gate)
        high = high + dot(part_high, here, TN)
        low = low + dot(part_low, here, TN)
    last = lane_blocks(dot(tails_ref[...], two_ref[...]).astype(LOW))
    last = last + [high[:experts].astype(LOW), low[:experts].astype(LOW)]
    x_tiles[...] = to_tiles(last).reshape(n, 8, 128).astype(LOW)

    @pl.loop(0, n // some)
    def _(c):
        place = iota((big, rows), 0) + c * big
        hit = (place == rows_ref[0:1, :]) | (place == rows_ref[1:2, :])
        got = dot(jnp.where(hit, 1.0, 0.0).astype(LOW), two_ref[...])
        x_ref[pl.ds(pl.multiple_of(c * big, 16), big), :] = got.astype(LOW)

    def others(j, action):
        for i in range(4):
            if isinstance(j, int) and j == 0:
                if i > 0:
                    action(4 * my_group + (my_place + i) % 4)
            else:
                action(4 * ((my_group + groups + j) % groups) + (my_place + i) % 4)

    def send_slots(p):
        tile(0, p, me).start()
        rows_of(0, p, me).start()

    own(0).start()
    own_tile(0).start()
    others(0, send_slots)

    @pl.loop(1, groups)
    def _(j):
        others(groups - j, send_slots)

    saved = (
        (dense_ref, dense_out), (qkv_ref, qkv_out), (att_ref, att_out), (lse_ref, lse_out),
        (mid_ref, mid_out), (two_ref, two_out), (route_ref, route_out), (col_ref, col_out),
        (low_first, dfirst_out), (low_second, dsecond_out),
    )

    def save(i):
        return pltpu.make_async_copy(saved[i][0], saved[i][1], save_sem.at[i])

    for i in range(8):
        save(i).start()

    per_dp = experts // dp
    for f in range(parts):
        place = me // per_dp
        slab = dense_ref[
            place // 4, (place // 2) % 2, place % 2, f, :, 4 * width + 128 : 4 * width + 256
        ].astype(WIDE)
        lines = dense_blk // per_dp
        mine = slab[:lines]
        for i in range(1, per_dp):
            mine = jnp.where(me % per_dp == i, slab[i * lines : (i + 1) * lines], mine)
        for i in range(lines):
            b_ref[:, f * half + i * 128 : f * half + (i + 1) * 128] = mine[i : i + 1]

    for i in range(8):
        save(i).wait()
    own_weights(0).wait()
    own_weights(1).wait()
    own(5).wait()
    own_tile(1).wait()

    @pl.loop(1, n)
    def _(r):
        p = (me + r) % n
        for which in range(2):
            weights(which, p, p).wait_recv()
            weights(which, p, me).wait_send()
        rows_of(1, p, me).wait_send()

    place = iota((per, 1), 0)
    sender = jnp.where(place < 4 * MAIN, place // MAIN, place - 4 * MAIN)
    slot_at = jnp.where(place < 4 * MAIN, place % MAIN, MAIN)

    def flat(ref, group):
        return ref[pl.ds(4 * group, 4)].astype(WIDE).reshape(32, 128).astype(LOW)

    def compute(group):
        here = pl.ds(pl.multiple_of(group * per, 16), per)
        tail = pl.ds(pl.multiple_of(group * per + 4 * MAIN, 16), 16)
        x_last, g_last = flat(xs_tiles, group), flat(gs_tiles, group)
        for c in range(width // 128):
            cols = slice(c * 128, (c + 1) * 128)
            xs_ref[tail, cols] = from_tiles(x_last, c, 16).astype(LOW)
            sg_ref[tail, cols] = from_tiles(g_last, c, 16).astype(LOW)
        gates = from_tiles(x_last, width // 128, 16) + from_tiles(x_last, width // 128 + 1, 16)
        x = xs_ref[here, :]
        lanes = iota((1, 128), 1)
        gate = jnp.zeros((per, 1), WIDE)
        for s in range(4):
            got = jnp.sum(jnp.where(lanes == slot_at, gates[s : s + 1], 0.0), axis=1, keepdims=True)
            gate = jnp.where(sender == s, got, gate)
        sg = (gate * sg_ref[here, :].astype(WIDE)).astype(LOW)
        sg_ref[here, :] = sg
        out = jnp.zeros((per, width), WIDE)
        back = jnp.zeros((per, width), WIDE)
        for f in range(parts):
            cols = slice(f * half, (f + 1) * half)
            pre = dot(x, first_ref[f]) + b_ref[:, cols]
            t = jnp.tanh(0.7978845608028654 * (pre + 0.044715 * (pre * pre * pre)))
            hid = (0.5 * pre * (1.0 + t)).astype(LOW)
            slope = 0.5 * (1.0 + t) + (0.5 * pre) * (1.0 - t * t) * (
                0.7978845608028654 * (1.0 + 0.134145 * (pre * pre))
            )
            hid_ref[here, cols] = hid
            out = out + dot(hid, second_ref[f], NT)
            gp = (dot(sg, second_ref[f]) * slope).astype(LOW)
            pre_ref[here, cols] = gp
            db_ref[:, cols] += jnp.sum(gp.astype(WIDE), axis=0, keepdims=True)
            back = back + dot(gp, first_ref[f], NT)
        out, back = out.astype(LOW), back.astype(LOW)
        main = pl.ds(pl.multiple_of(group * 4 * MAIN, 16), 4 * MAIN)
        outs_ref[main, :] = out[: 4 * MAIN]
        backs_ref[main, :] = back[: 4 * MAIN]
        made = to_tiles(lane_blocks(out[4 * MAIN :]) + lane_blocks(back[4 * MAIN :]))
        home_tiles[pl.ds(4 * group, 4)] = made[:32].reshape(4, 8, 128).astype(LOW)

    def send_home(j):
        def both(p):
            home(0, p, me).start()
            home(1, p, me).start()
            tile(2, p, me).start()

        others(j, both)

    def arrived(p):
        for which in range(2):
            rows_of(which, p, p).wait_recv()
            tile(which, p, p).wait_recv()

    own(0).wait()
    own_tile(0).wait()
    others(0, arrived)
    compute(my_group)
    own(1).start()
    own(2).start()
    own_tile(2).start()
    send_home(0)

    @pl.loop(1, groups)
    def _(j):
        others(j, arrived)
        compute((my_group + j) % groups)
        send_home(j)

    for f in range(parts):
        mine = slice(f * dp, (f + 1) * dp)
        for q in range(half // 256):
            cols = slice(f * half + q * 256, f * half + (q + 1) * 256)
            sub = slice(q * 256, (q + 1) * 256)
            low_first[mine, :, sub] = (
                dot(xs_ref[...], pre_ref[:, cols], TN).astype(LOW).reshape(dp, blk_d, 256)
            )
            low_second[mine, :, sub] = (
                dot(sg_ref[...], hid_ref[:, cols], TN).astype(LOW).reshape(dp, blk_d, 256)
            )
    save(8).start()
    save(9).start()
    save(8).wait()
    save(9).wait()
    own(1).wait()
    own(2).wait()
    own_tile(2).wait()
    to_core(core).wait_send()
    for i in range(1, spots):
        to_spot((spot + i) % spots, spot).wait_send()
    for copy in layer_sends:
        copy.wait_send()

    @pl.loop(1, n)
    def _(r):
        p = (me + r) % n
        rows_of(0, p, me).wait_send()
        for which in range(2):
            home(which, p, me).wait_send()
            home(which, p, p).wait_recv()
        for which in range(3):
            tile(which, p, me).wait_send()
        tile(2, p, p).wait_recv()


def backward_kernel(
    dp, images, experts, tok_in, cot_in, dense_in, qkv_in, att_in, lse_in, mid_in,
    two_in, route_in, col_in, out_in, grad_in, tiles_in, db_ref, dfirst_ref, dsecond_ref,
    result_ref, dtok_ref, done_ref, gin_ref, gback_ref,
    tok_ref, cot_ref, dense_ref, qkv_ref, att_ref, lse_ref, mid_ref,
    two_ref, route_ref, col_ref, out_ref, grad_ref, tiles_ref, in_sem,
    dmid_ref, datt_ref, dqkv_ref, ddense_ref, got_a, sum_a, got_b, sum_b, got_c,
    w_send, w_recv, own_sem, a_sems, b_send, b_recv, c_send, c_recv,
):
    rows, width = tok_ref.shape
    n = dfirst_ref.shape[0]
    tn = n // dp
    t_here, d_here = lax.axis_index("tensor"), lax.axis_index("dp")
    me = t_here * dp + d_here
    core, y_here, z_here = d_here % 2, (d_here // 2) % 2, d_here // 4
    spots, layers = 2 * tn, dp // 4
    spot = y_here * tn + t_here

    def device(p):
        return (p % dp, p // dp)

    def grads_to(which, p):
        src, dst = ((dfirst_ref, gin_ref), (dsecond_ref, gback_ref))[which]
        return pltpu.make_async_remote_copy(
            src_ref=src.at[p], dst_ref=dst.at[me],
            send_sem=w_send.at[which, p], recv_sem=w_recv.at[which, me],
            device_id=device(p), device_id_type=MESH,
        )

    def grads_from(which, p):
        src, dst = ((dfirst_ref, gin_ref), (dsecond_ref, gback_ref))[which]
        return pltpu.make_async_remote_copy(
            src_ref=src.at[p], dst_ref=dst.at[p],
            send_sem=w_send.at[which, p], recv_sem=w_recv.at[which, p],
            device_id=device(p), device_id_type=MESH,
        )

    def own(which):
        src, dst = ((dfirst_ref, gin_ref), (dsecond_ref, gback_ref))[which]
        return pltpu.make_async_copy(src.at[me], dst.at[me], own_sem.at[which])

    def to_spot(s):
        return pltpu.make_async_remote_copy(
            src_ref=sum_a.at[:, s], dst_ref=got_b.at[spot],
            send_sem=b_send.at[s], recv_sem=b_recv.at[spot],
            device_id=((z_here * 2 + s // tn) * 2 + core, s % tn), device_id_type=MESH,
        )

    def from_spot(s):
        return pltpu.make_async_remote_copy(
            src_ref=sum_a.at[:, s], dst_ref=got_b.at[s],
            send_sem=b_send.at[s], recv_sem=b_recv.at[s],
            device_id=((z_here * 2 + s // tn) * 2 + core, s % tn), device_id_type=MESH,
        )

    near, across = z_here + 1 - 2 * (z_here % 2), (z_here + 2) % layers

    def to_layer(src, z, place):
        return pltpu.make_async_remote_copy(
            src_ref=src, dst_ref=got_c.at[place],
            send_sem=c_send.at[place], recv_sem=c_recv.at[place],
            device_id=((z * 2 + y_here) * 2 + core, t_here), device_id_type=MESH,
        )

    layer_sends = (
        to_layer(sum_b.at[(near + 2) % layers], near, 0),
        to_layer(sum_b.at[near], near, 1),
        to_layer(got_c.at[3], across, 2),
    )

    slots_main = out_in.shape[0]
    moves = (
        (out_in, out_ref.at[0:slots_main]), (grad_in, grad_ref.at[0:slots_main]),
        (tiles_in, tiles_ref), (cot_in, cot_ref), (route_in, route_ref), (mid_in, mid_ref),
        (col_in, col_ref), (two_in, two_ref), (dense_in, dense_ref), (att_in, att_ref),
        (qkv_in, qkv_ref), (lse_in, lse_ref), (tok_in, tok_ref),
    )

    def bring(i):
        return pltpu.make_async_copy(moves[i][0], moves[i][1], in_sem.at[i])

    barrier = pltpu.get_barrier_semaphore()

    @pl.loop(1, n)
    def _(r):
        pl.semaphore_signal(barrier, inc=1, device_id=device((me + r) % n), device_id_type=MESH)

    for i in range(len(moves)):
        bring(i).start()
    pl.semaphore_wait(barrier, n - 1)

    @pl.loop(1, n)
    def _(r):
        grads_to(0, (me + r) % n).start()

    @pl.loop(1, n // 2)
    def _(r):
        grads_to(1, (me + r) % n).start()

    own(0).start()
    own(1).start()

    def put(cols, val):
        ddense_ref[:, :, :, cols] = val.reshape(ddense_ref.shape[:3] + (-1,)).astype(LOW)

    for i in range(len(moves)):
        bring(i).wait()
    tiles = tiles_ref[...].astype(WIDE).reshape(8 * n, 128).astype(LOW)
    rest = out_ref.shape[0] - slots_main
    for c in range(width // 128):
        cols = slice(c * 128, (c + 1) * 128)
        out_ref[slots_main:, cols] = from_tiles(tiles, c, rest).astype(LOW)
        grad_ref[slots_main:, cols] = from_tiles(tiles, width // 128 + c, rest).astype(LOW)

    misc_t = dense_ref[:, 4 * width : 4 * width + 128].astype(WIDE).T
    misc_low = misc_t.astype(LOW)
    gain_one, shift_one, bias, gain_two, shift_two = [
        misc_t[64 + i : 65 + i, :] for i in range(5)
    ]
    lanes = iota((1, 128), 1)
    per = 112
    slots_all = out_ref.shape[0]

    def chunk(c, carry):
        d_router, d_bias_back, d_gain, d_shift, d_bias = carry
        here = pl.ds(pl.multiple_of(c * per, 16), per)
        g = cot_ref[here, :]
        gw = g.astype(WIDE)
        route = route_ref[here, :]
        mid = mid_ref[here, :]
        result = mid
        probs = jnp.zeros((per, 128), WIDE)
        gate_sel = jnp.zeros((per, 128), WIDE)
        both = jnp.zeros((per, slots_all), WIDE)
        for k in range(2):
            choice = col_ref[here, k : k + 1]
            slot = col_ref[here, 2 + k : 3 + k]
            kept = slot >= 0
            chosen = (lanes == choice) & kept
            where_to = jnp.where(slot < MAIN, choice * MAIN + slot, slots_main + choice)
            where_to = jnp.where(kept, where_to, -1)
            hit = jnp.where(iota((per, slots_all), 1) == where_to, 1.0, 0.0)
            both = both + hit
            add_b = jnp.where((lanes == choice + experts) & kept, 1.0, 0.0).astype(LOW)
            picked = dot(hit.astype(LOW), out_ref[...]) + dot(add_b, misc_low)
            gate = jnp.sum(jnp.where(chosen, route, 0.0), axis=1, keepdims=True)
            result = result + gate * picked
            gg = jnp.sum(gw * picked, axis=1, keepdims=True)
            probs = probs + jnp.where(chosen, gg, 0.0)
            gate_sel = gate_sel + jnp.where(chosen, route, 0.0)
        result_ref[here, :] = result.astype(LOW)
        logits = route * (probs - jnp.sum(probs * route, axis=-1, keepdims=True))
        high, low = split_two(logits)
        d_two = dot(both.astype(LOW), grad_ref[...]) + dot(high, misc_low) + dot(low, misc_low)
        two = two_ref[here, :]
        d_router = d_router + dot(high, two, TN) + dot(low, two, TN)
        gs_high, gs_low = split_two(gate_sel)
        d_bias_back = d_bias_back + dot(gs_high, g, TN) + dot(gs_low, g, TN)
        xhat, rstd = normalize(mid)
        d_gain = d_gain + jnp.sum(d_two * xhat, axis=0, keepdims=True)
        d_shift = d_shift + jnp.sum(d_two, axis=0, keepdims=True)
        d_mid = gw + norm_back(d_two, xhat, rstd, gain_two)
        d_bias = d_bias + jnp.sum(d_mid, axis=0, keepdims=True)
        dtok_ref[here, :] = d_mid
        dmid_ref[here, :] = d_mid.astype(LOW)
        return d_router, d_bias_back, d_gain, d_shift, d_bias

    zero = jnp.zeros((1, width), WIDE)
    wide_zero = jnp.zeros((128, width), WIDE)
    d_router, d_bias_back, d_gain_two, d_shift_two, d_bias = lax.fori_loop(
        0, rows // per, chunk, (wide_zero, wide_zero, zero, zero, zero)
    )
    out_cols = slice(3 * width, 4 * width)
    datt_ref[...] = dot(dmid_ref[...], dense_ref[:, out_cols], NT).astype(LOW)
    put(out_cols, dot(att_ref[...], dmid_ref[...], TN))
    dqkv_ref[...] = jnp.zeros_like(dqkv_ref)
    low_half = iota((1, 128), 1) < HD

    @pl.loop(0, images)
    def _(i):
        win = pl.ds(pl.multiple_of(i * STEP, 16), WIN)
        first = i * (SEQ - STEP)
        key_pos = iota((1, WIN), 1)
        key_ok = (key_pos >= first) & (key_pos < first + SEQ)
        row_pos = iota((WIN, 1), 0)
        row_ok = (row_pos >= first) & (row_pos < first + SEQ)
        lse = lse_ref[win, :]
        for pair in range(H // 2):
            cols = [
                slice(j * width + pair * 128, j * width + (pair + 1) * 128) for j in range(3)
            ]
            q, k, v = [qkv_ref[win, c] for c in cols]
            do = datt_ref[win, pair * 128 : (pair + 1) * 128]
            do = jnp.where(row_ok, do, jnp.zeros_like(do))
            dq, dk, dv = [jnp.zeros((WIN, 128), WIDE) for _ in range(3)]
            for half in range(2):
                mask = low_half if half == 0 else jnp.logical_not(low_half)
                qm, km, dom = [jnp.where(mask, a, jnp.zeros_like(a)) for a in (q, k, do)]
                h = 2 * pair + half
                s = dot(qm, k, NT) * HD**-0.5
                p = jnp.where(key_ok & row_ok, jnp.exp(jnp.minimum(s - lse[:, h : h + 1], 0.0)), 0.0)
                dp = dot(dom, v, NT)
                delta = jnp.sum(dp * p, axis=-1, keepdims=True)
                ds = (p * (dp - delta) * HD**-0.5).astype(LOW)
                dv = dv + dot(p.astype(LOW), dom, TN)
                dq = dq + dot(ds, km)
                dk = dk + dot(ds, qm, TN)
            for c, val in zip(cols, (dq, dk, dv)):
                dqkv_ref[win, c] = jnp.where(row_ok, val.astype(LOW), dqkv_ref[win, c])

    xhat, rstd = normalize(tok_ref[...].astype(WIDE))
    one = (xhat * gain_one + shift_one).astype(LOW)
    d_one = jnp.zeros((rows, width), WIDE)
    for j in range(3):
        cols = slice(j * width, (j + 1) * width)
        put(cols, dot(one, dqkv_ref[:, cols], TN))
        d_one = d_one + dot(dqkv_ref[:, cols], dense_ref[:, cols], NT)
    d_gain_one = jnp.sum(d_one * xhat, axis=0, keepdims=True)
    d_shift_one = jnp.sum(d_one, axis=0, keepdims=True)
    dtok_ref[...] = dtok_ref[...] + norm_back(d_one, xhat, rstd, gain_one)
    row = iota((128, 1), 0)
    grads = jnp.where(row < experts, d_router, 0.0)
    moved = jnp.concatenate([d_bias_back[128 - experts :], d_bias_back[: 128 - experts]], axis=0)
    grads = grads + jnp.where((row >= experts) & (row < 2 * experts), moved, 0.0)
    for i, vec in enumerate((d_gain_one, d_shift_one, d_bias, d_gain_two, d_shift_two)):
        grads = grads + jnp.where(row == 64 + i, vec, 0.0)
    put(slice(4 * width, 4 * width + 128), grads.T)
    per_dp = experts // dp
    lines = ddense_ref.shape[2] // tn // per_dp
    count = tn * lines
    line = iota((count, 1), 0)
    slab = jnp.zeros((count, 128), WIDE)
    for i in range(count):
        slab = jnp.where(line == i, db_ref[:, i * 128 : (i + 1) * 128], slab)
    line = iota((width, count), 1)
    place = (me // per_dp * tn + line // lines) * (lines * per_dp) + me % per_dp * lines + line % lines
    placed = jnp.where(iota((width, count), 0) == place, 1.0, 0.0).astype(LOW)
    put(slice(4 * width + 128, 4 * width + 256), dot(placed, slab.astype(LOW)))

    partner = pltpu.make_async_remote_copy(
        src_ref=ddense_ref.at[:, 1 - core], dst_ref=got_a,
        send_sem=a_sems.at[0], recv_sem=a_sems.at[1],
        device_id=(d_here + 1 - 2 * core, t_here), device_id_type=MESH,
    )
    partner.start()
    partner.wait()
    total = ddense_ref[:, core].astype(WIDE) + got_a[...].astype(WIDE)
    sum_a[...] = total.reshape(sum_a.shape).astype(LOW)
    for i in range(1, spots):
        to_spot((spot + i) % spots).start()

    @pl.loop(n // 2, 3 * n // 4)
    def _(r):
        grads_to(1, (me + r) % n).start()

    total = sum_a[:, spot].astype(WIDE)
    for i in range(1, spots):
        s = (spot + i) % spots
        from_spot(s).wait_recv()
        total = total + got_b[s].astype(WIDE)
    sum_b[...] = total.astype(LOW)
    layer_sends[0].start()
    layer_sends[1].start()

    @pl.loop(3 * n // 4, 7 * n // 8)
    def _(r):
        grads_to(1, (me + r) % n).start()

    layer_sends[0].wait_recv()
    got_c[3] = (sum_b[across].astype(WIDE) + got_c[0].astype(WIDE)).astype(LOW)
    layer_sends[2].start()

    @pl.loop(7 * n // 8, n)
    def _(r):
        grads_to(1, (me + r) % n).start()

    layer_sends[1].wait_recv()
    total = sum_b[z_here].astype(WIDE) + got_c[1].astype(WIDE)
    layer_sends[2].wait_recv()
    total = total + got_c[2].astype(WIDE)
    done_ref[...] = total

    own(0).wait()
    own(1).wait()
    for i in range(1, spots):
        to_spot((spot + i) % spots).wait_send()
    for copy in layer_sends:
        copy.wait_send()

    @pl.loop(1, n)
    def _(r):
        p = (me + r) % n
        for which in range(2):
            grads_to(which, p).wait_send()
            grads_from(which, p).wait_recv()


def finish_kernel(
    experts, done_ref, gin_ref, gback_ref, tok_ref, res_ref,
    din_ref, dback_ref, dtok_ref, result_ref, dqkv_ref, dwout_ref, drouter_ref, dbback_ref,
    dbin_ref, *refs,
):
    vec_refs, (low_ref, wide_ref, tok_held, res_held, in_sem, out_sem) = refs[:5], refs[5:]
    pieces = in_sem.shape[0] - 2
    each = low_ref.shape[0] // pieces
    n = gin_ref.shape[0]

    def bring(i):
        if i >= pieces:
            src, dst = ((tok_ref, tok_held), (res_ref, res_held))[i - pieces]
            return pltpu.make_async_copy(src, dst, in_sem.at[i])
        src = (gin_ref, gback_ref)[i * each // n]
        return pltpu.make_async_copy(
            src.at[i * each % n : i * each % n + each],
            low_ref.at[i * each : (i + 1) * each], in_sem.at[i],
        )

    def save(i):
        if i >= pieces:
            src, dst = ((tok_held, dtok_ref), (res_held, result_ref))[i - pieces]
            return pltpu.make_async_copy(src, dst, out_sem.at[i])
        dst = (din_ref, dback_ref)[i * each // n]
        return pltpu.make_async_copy(
            wide_ref.at[i * each : (i + 1) * each],
            dst.at[i * each % n : i * each % n + each], out_sem.at[i],
        )

    for i in range(pieces + 2):
        bring(i).start()
    dense_blk, width = dwout_ref.shape
    for j in range(3):
        dqkv_ref[j] = done_ref[:, j * width : (j + 1) * width]
    dwout_ref[...] = done_ref[:, 3 * width : 4 * width]
    misc = done_ref[:, 4 * width : 4 * width + 128]
    drouter_ref[...] = misc[:, :experts]
    dbback_ref[...] = misc[:, experts : 2 * experts]
    diagonal = iota((dense_blk, dense_blk), 0) == iota((dense_blk, dense_blk), 1)
    for i, vec in enumerate(vec_refs):
        column = misc[:, 2 * experts + i : 2 * experts + i + 1]
        vec[...] = jnp.sum(jnp.where(diagonal, column, 0.0), axis=0, keepdims=True)
    lines = dbin_ref.shape[1] // 128
    for i in range(dense_blk):
        dbin_ref[i // lines : i // lines + 1, (i % lines) * 128 : (i % lines + 1) * 128] = (
            done_ref[i : i + 1, 4 * width + 128 : 4 * width + 256]
        )
    for i in range(pieces + 2):
        bring(i).wait()
        if i < pieces:
            span = slice(i * each, (i + 1) * each)
            wide_ref[span] = low_ref[span].astype(WIDE)
        save(i).start()
    for i in range(pieces + 2):
        save(i).wait()


VMEM = pl.BlockSpec(memory_space=pltpu.VMEM)


def make_owner_device(dp, tn):
    n = dp * tn

    def per_device(
        tokens, cotangent, ln1_scale, ln1_shift, w_qkv, w_out, out_bias, ln2_scale, ln2_shift,
        w_router, w_in, b_in, w_back, b_back, choices, slots,
    ):
        rows, width = tokens.shape
        images = rows // SEQ
        experts, blk_d, blk_f = w_in.shape
        ff = blk_f * tn
        dense_blk = w_out.shape[0]
        places = experts * MAIN
        landed = n // 4 * GROUP
        shape = jax.ShapeDtypeStruct

        cols = 4 * width + 256
        per_layer = dp // 4

        hbm = pl.BlockSpec(memory_space=pl.ANY)
        saved = [
            ((per_layer, 2, 2, tn, dense_blk, cols), LOW),
            ((rows, 3 * width), LOW),
            ((rows, width), LOW),
            ((rows, 128), WIDE),
            ((rows, width), WIDE),
            ((rows, width), LOW),
            ((rows, 128), WIDE),
            ((rows, 128), jnp.int32),
        ]
        weight_shape = (n, blk_d, blk_f)
        out_home, back_home, tails_home, dense, qkv, att, lse, mid, two, route, col, d_first, d_second, d_b = pl.pallas_call(
            functools.partial(layer_kernel, dp, images, experts),
            out_shape=(
                shape((places, width), LOW),
                shape((places, width), LOW),
                shape((n, 8, 128), LOW),
                *[shape(*s) for s in saved],
                shape(weight_shape, LOW),
                shape(weight_shape, LOW),
                shape((1, ff), WIDE),
            ),
            in_specs=[VMEM] * 14 + [hbm, hbm],
            out_specs=(hbm,) * 13 + (VMEM,),
            scratch_shapes=[
                *[pltpu.VMEM(*saved[i]) for i in (0, 3, 4, 6, 7)],
                pltpu.VMEM((dense_blk, cols), LOW),
                pltpu.VMEM((2, rows), jnp.int32),
                pltpu.VMEM((2, 4, blk_d, blk_f), WIDE),
                pltpu.VMEM(weight_shape, LOW),
                pltpu.VMEM(weight_shape, LOW),
                pltpu.VMEM((tn, width, blk_f), LOW),
                pltpu.VMEM((tn, width, blk_f), LOW),
                pltpu.VMEM((1, ff), WIDE),
                pltpu.VMEM((places, width), LOW),
                pltpu.VMEM((places, width), LOW),
                pltpu.VMEM((landed, width), LOW),
                pltpu.VMEM((landed, width), LOW),
                pltpu.VMEM((landed, ff), LOW),
                pltpu.VMEM((landed, ff), LOW),
                pltpu.VMEM((places, width), LOW),
                pltpu.VMEM((n, rows), LOW),
                pltpu.VMEM((2, rows), jnp.int32),
                *[pltpu.VMEM((n, 8, 128), LOW)] * 5,
                pltpu.SemaphoreType.DMA((2,)),
                pltpu.SemaphoreType.DMA((2, n)),
                pltpu.SemaphoreType.DMA((2, n)),
                pltpu.SemaphoreType.DMA((n,)),
                pltpu.SemaphoreType.DMA((n,)),
                pltpu.SemaphoreType.DMA((n,)),
                pltpu.SemaphoreType.DMA((n,)),
                pltpu.SemaphoreType.DMA((2, n)),
                pltpu.SemaphoreType.DMA((2, n)),
                pltpu.SemaphoreType.DMA((3, n)),
                pltpu.SemaphoreType.DMA((3, n)),
                pltpu.SemaphoreType.DMA((per_layer,)),
                pltpu.SemaphoreType.DMA((per_layer,)),
                pltpu.SemaphoreType.DMA((2 * tn,)),
                pltpu.SemaphoreType.DMA((2 * tn,)),
                pltpu.SemaphoreType.DMA((2,)),
                pltpu.SemaphoreType.DMA((10,)),
                pltpu.SemaphoreType.DMA((10,)),
            ],
            compiler_params=pltpu.CompilerParams(
                vmem_limit_bytes=63 * 2**20, collective_id=1, has_side_effects=True
            ),
            cost_estimate=pl.CostEstimate(
                flops=12 * places * width * ff, bytes_accessed=10 * places * width, transcendentals=0
            ),
            name="layer",
        )(
            tokens, cotangent, choices.T, slots.T,
            *[v.reshape(1, dense_blk) for v in (ln1_scale, ln1_shift, out_bias, ln2_scale, ln2_shift)],
            w_qkv, w_out, w_router, b_back.T, b_in, w_in, jnp.swapaxes(w_back, 1, 2),
        )
        dense = dense.reshape(width, cols)
        brought = (
            tokens, cotangent, dense, qkv, att, lse, mid, two, route, col, out_home, back_home,
            tails_home,
        )
        result, d_tok, done, grad_in, grad_back = pl.pallas_call(
            functools.partial(backward_kernel, dp, images, experts),
            out_shape=(
                shape((rows, width), LOW),
                shape((rows, width), WIDE),
                shape((dense_blk, cols), WIDE),
                shape((n, blk_d, blk_f), LOW),
                shape((n, blk_d, blk_f), LOW),
            ),
            in_specs=[hbm] * 13 + [VMEM] + [hbm] * 2,
            out_specs=(VMEM, VMEM, VMEM, hbm, hbm),
            scratch_shapes=[
                *[pltpu.VMEM(v.shape, v.dtype) for v in brought[:10]],
                pltpu.VMEM((places + 128, width), LOW),
                pltpu.VMEM((places + 128, width), LOW),
                pltpu.VMEM((n, 8, 128), LOW),
                pltpu.SemaphoreType.DMA((13,)),
                pltpu.VMEM((rows, width), LOW),
                pltpu.VMEM((rows, width), LOW),
                pltpu.VMEM((rows, 3 * width), LOW),
                pltpu.VMEM((dp // 2, 2, tn * dense_blk, cols), LOW),
                pltpu.VMEM((dp // 2, tn * dense_blk, cols), LOW),
                pltpu.VMEM((per_layer, 2 * tn, dense_blk, cols), LOW),
                pltpu.VMEM((2 * tn, per_layer, dense_blk, cols), LOW),
                pltpu.VMEM((per_layer, dense_blk, cols), LOW),
                pltpu.VMEM((per_layer, dense_blk, cols), LOW),
                pltpu.SemaphoreType.DMA((2, n)),
                pltpu.SemaphoreType.DMA((2, n)),
                pltpu.SemaphoreType.DMA((2,)),
                pltpu.SemaphoreType.DMA((2,)),
                pltpu.SemaphoreType.DMA((2 * tn,)),
                pltpu.SemaphoreType.DMA((2 * tn,)),
                pltpu.SemaphoreType.DMA((per_layer,)),
                pltpu.SemaphoreType.DMA((per_layer,)),
            ],
            compiler_params=pltpu.CompilerParams(
                vmem_limit_bytes=60 * 2**20, collective_id=2, has_side_effects=True
            ),
            cost_estimate=pl.CostEstimate(
                flops=6 * places * rows * width + 20 * rows * width * width,
                bytes_accessed=40 * rows * width, transcendentals=0,
            ),
            name="backward",
        )(
            *brought, d_b, d_first, d_second,
        )
        vec = (1, dense_blk)
        small = [w_qkv.shape, w_out.shape, w_router.shape, (dense_blk, experts), b_in.shape] + [vec] * 5
        grad_in, grad_back, d_tok, result, *rest = pl.pallas_call(
            functools.partial(finish_kernel, experts),
            out_shape=(
                shape(weight_shape, WIDE),
                shape(weight_shape, WIDE),
                shape((rows, width), WIDE),
                shape((rows, width), LOW),
                *[shape(d, WIDE) for d in small],
            ),
            in_specs=[VMEM] + [hbm] * 4,
            out_specs=(hbm,) * 4 + (VMEM,) * len(small),
            scratch_shapes=[
                pltpu.VMEM((2 * n, blk_d, blk_f), LOW),
                pltpu.VMEM((2 * n, blk_d, blk_f), WIDE),
                pltpu.VMEM((rows, width), WIDE),
                pltpu.VMEM((rows, width), LOW),
                pltpu.SemaphoreType.DMA((18,)),
                pltpu.SemaphoreType.DMA((18,)),
            ],
            name="finish",
        )(done, grad_in, grad_back, d_tok, result)
        d_qkv, d_wout, d_router, d_bback, d_bin, *vecs = rest
        d_vecs = [v.reshape(dense_blk) for v in vecs]
        return (
            result,
            d_tok,
            d_vecs[0],
            d_vecs[1],
            d_qkv,
            d_wout,
            d_vecs[2],
            d_vecs[3],
            d_vecs[4],
            d_router,
            grad_in,
            d_bin,
            jnp.swapaxes(grad_back, 1, 2),
            d_bback.T,
        )

    return per_device


def make_per_device(dp, tn):
    everyone = ("dp", "tensor")
    n = dp * tn

    def per_device(
        tokens,
        cotangent,
        ln1_scale,
        ln1_shift,
        w_qkv,
        w_out,
        out_bias,
        ln2_scale,
        ln2_shift,
        w_router,
        w_in,
        b_in,
        w_back,
        b_back,
        choices,
        slots,
    ):
        rows_here, width = tokens.shape
        images = rows_here // SEQ
        experts, blk_d, blk_f = w_in.shape
        ff = blk_f * tn
        dense_blk = w_out.shape[0]
        whole = experts % n == 0
        owners = n if whole else dp
        owned = experts // owners
        expert_axes = ("tensor", "dp") if whole else ("dp",)
        slot_total = experts * CAP
        score_scale = HD ** (-0.5)

        w_pack = jnp.stack([w_in.astype(LOW), jnp.swapaxes(w_back, 1, 2).astype(LOW)], axis=1)
        w_all = lax.all_to_all(w_pack, expert_axes, split_axis=0, concat_axis=0, tiled=True)
        f_parts = tn if whole else 1
        w_all = w_all.reshape(f_parts, dp, owned, 2, blk_d, blk_f)
        w_all = w_all.transpose(3, 2, 1, 4, 0, 5).reshape(2, owned, width, f_parts * blk_f)
        first_w, second_wt = w_all[0], w_all[1]

        vec_rows = jnp.stack([ln1_scale, ln1_shift, out_bias, ln2_scale, ln2_shift])
        pieces = [
            w_qkv.reshape(-1),
            w_out.reshape(-1),
            w_router.reshape(-1),
            b_back.reshape(-1),
            b_in.reshape(-1),
            vec_rows.reshape(-1),
        ]
        sizes = [p.shape[0] for p in pieces]
        total = sum(sizes)
        pad = -total % 512
        packed = jnp.concatenate([p.astype(LOW) for p in pieces] + [jnp.zeros((pad,), LOW)])
        gathered = lax.all_gather(packed.reshape(-1, 512), everyone, axis=0, tiled=False)
        gathered = gathered.reshape(n, -1)
        offs = [sum(sizes[:i]) for i in range(len(sizes))]
        part = [gathered[:, o : o + s] for o, s in zip(offs, sizes)]
        qkv_w = part[0].reshape(n, 3, dense_blk, width).swapaxes(0, 1).reshape(3, width, width)
        out_w = part[1].reshape(width, width)
        router = part[2].reshape(width, experts)
        bias_back = part[3].reshape(n, experts, -1).swapaxes(0, 1).reshape(experts, width)
        bias_back = bias_back.astype(WIDE)
        in_b = part[4].reshape(dp, tn, experts // dp, blk_f).swapaxes(1, 2).reshape(experts, ff)
        vecs = part[5].reshape(n, 5, -1).swapaxes(0, 1).reshape(5, width).astype(WIDE)
        gain_one, shift_one, bias_attn, gain_two, shift_two = vecs
        if whole:
            mine = lax.axis_index("tensor") * dp + lax.axis_index("dp")
            my_b = lax.dynamic_slice(in_b, (mine * owned, 0), (owned, ff)).astype(WIDE)
        else:
            my_b = lax.dynamic_slice(
                in_b,
                (lax.axis_index("dp") * owned, lax.axis_index("tensor") * blk_f),
                (owned, blk_f),
            ).astype(WIDE)

        residual = tokens.astype(WIDE)
        normed_one = norm_affine(residual, gain_one, shift_one).astype(LOW)
        projected = jnp.einsum(
            "td,jde->jte", normed_one, qkv_w, preferred_element_type=WIDE
        ).astype(LOW)
        head_query = projected[0].reshape(images, SEQ, H, HD)
        head_key = projected[1].reshape(images, SEQ, H, HD)
        head_value = projected[2].reshape(images, SEQ, H, HD)
        raw_scores = jnp.einsum(
            "ishd,ithd->ihst", head_query, head_key, preferred_element_type=WIDE
        )
        scaled = raw_scores * score_scale
        row_top = jnp.max(scaled, axis=-1, keepdims=True)
        log_total = row_top + jnp.log(jnp.sum(jnp.exp(scaled - row_top), axis=-1, keepdims=True))
        weights_att = jnp.exp(scaled - log_total).astype(LOW)
        attended = (
            jnp.einsum("ihst,ithd->ishd", weights_att, head_value, preferred_element_type=WIDE)
            .astype(LOW)
            .reshape(rows_here, width)
        )
        attn_sum = jnp.dot(attended, out_w, preferred_element_type=WIDE)
        middle = residual + attn_sum + bias_attn
        normed_two = norm_affine(middle, gain_two, shift_two).astype(LOW)
        route_p = jax.nn.softmax(jnp.dot(normed_two, router, preferred_element_type=WIDE), axis=-1)

        expert_ids = jnp.arange(experts, dtype=jnp.int32)
        chosen = [
            (choices[:, k : k + 1] == expert_ids[None, :]).astype(WIDE) for k in range(2)
        ]
        gate_vals = jnp.concatenate(
            [jnp.sum(route_p * c, axis=1, keepdims=True) for c in chosen], axis=1
        )
        kept_pair = (slots >= 0).astype(WIDE)
        target = jnp.where(slots >= 0, choices * CAP + slots, -1)
        places = jnp.arange(slot_total, dtype=jnp.int32)
        by_slot = [target[:, k][None, :] == places[:, None] for k in range(2)]
        spread_mat = (by_slot[0] | by_slot[1]).astype(LOW)
        by_token = [target[:, k : k + 1] == places[None, :] for k in range(2)]
        pair_weight = gate_vals * kept_pair
        slot_gate = jnp.sum(
            jnp.where(by_slot[0], pair_weight[:, 0][None, :], 0.0)
            + jnp.where(by_slot[1], pair_weight[:, 1][None, :], 0.0),
            axis=1,
            keepdims=True,
        )
        both = jnp.dot(
            spread_mat,
            jnp.concatenate([normed_two, cotangent], axis=1),
            preferred_element_type=WIDE,
        )
        buffer = both[:, :width].astype(LOW).reshape(experts, CAP, width)
        slot_grad = slot_gate * both[:, width:]
        grad_bias_back = jnp.sum(slot_grad.reshape(experts, CAP, width), axis=1)
        slot_grad_low = slot_grad.astype(LOW).reshape(experts, CAP, width)

        def out_to_experts(rows):
            width_c = rows.shape[1]
            if not whole:
                rows = lax.all_gather(rows, "tensor", axis=1, tiled=True)
            rows = lax.all_to_all(rows, expert_axes, split_axis=0, concat_axis=0, tiled=True)
            return rows.reshape(owners, owned, -1, width)

        def back_to_tokens(rows):
            rows = rows.reshape(experts, -1, width)
            rows = lax.all_to_all(rows, expert_axes, split_axis=0, concat_axis=0, tiled=True)
            if not whole:
                rows = lax.psum_scatter(rows, "tensor", scatter_dimension=1, tiled=True)
            return rows

        sent = out_to_experts(jnp.concatenate([buffer, slot_grad_low], axis=1))
        group = sent.shape[2] // (2 * CAP)
        sent = sent.reshape(owners, owned, group, 2, CAP, width).transpose(3, 1, 0, 2, 4, 5)
        sent = sent.reshape(2, owned, owners * group * CAP, width)
        all_slots, slot_grad_all = sent[0], sent[1]

        pre_act = (
            jnp.einsum("ecd,edf->ecf", all_slots, first_w, preferred_element_type=WIDE)
            + my_b[:, None, :]
        )
        hidden, gelu_pull = jax.vjp(lambda member: jax.nn.gelu(member, approximate=True), pre_act)
        hidden = hidden.astype(LOW)
        expert_sum = jnp.einsum("ecf,edf->ecd", hidden, second_wt, preferred_element_type=WIDE)
        grad_hidden = jnp.einsum("ecd,edf->ecf", slot_grad_all, second_wt, preferred_element_type=WIDE)
        grad_pre = gelu_pull(grad_hidden)[0].astype(LOW)
        grad_slots_all = jnp.einsum("ecf,edf->ecd", grad_pre, first_w, preferred_element_type=WIDE)
        returned = jnp.stack([expert_sum.astype(LOW), grad_slots_all.astype(LOW)])
        returned = returned.reshape(2, owned, owners, group, CAP, width).transpose(2, 1, 3, 0, 4, 5)
        returned = returned.reshape(owners * owned, group * 2 * CAP, width)
        home = back_to_tokens(returned).reshape(experts, 2, CAP, width)
        expert_home = home[:, 0].reshape(slot_total, width)
        grad_home = home[:, 1].reshape(slot_total, width)

        grad_first_b = jnp.sum(grad_pre.astype(WIDE), axis=1)
        grad_first_w = jnp.einsum("ecd,ecf->edf", all_slots, grad_pre, preferred_element_type=WIDE)
        grad_second_t = jnp.einsum("ecd,ecf->edf", slot_grad_all, hidden, preferred_element_type=WIDE)
        g_pack = jnp.stack([grad_first_w.astype(LOW), grad_second_t.astype(LOW)])
        g_pack = g_pack.reshape(2, owned, dp, blk_d, f_parts, blk_f).transpose(4, 2, 1, 0, 3, 5)
        g_pack = g_pack.reshape(f_parts * dp * owned, 2, blk_d, blk_f)
        g_home = lax.all_to_all(g_pack, expert_axes, split_axis=0, concat_axis=0, tiled=True)
        g_home = g_home.reshape(experts, 2, blk_d, blk_f).astype(WIDE)
        grad_w_in = g_home[:, 0]
        grad_w_back = jnp.swapaxes(g_home[:, 1], 1, 2)

        picked = []
        for k in range(2):
            rows = jnp.dot(by_token[k].astype(LOW), expert_home, preferred_element_type=WIDE)
            bias_rows = jnp.dot(
                chosen[k].astype(LOW), bias_back.astype(LOW), preferred_element_type=WIDE
            )
            picked.append((rows + bias_rows) * kept_pair[:, k : k + 1])
        result = (
            middle + gate_vals[:, 0:1] * picked[0] + gate_vals[:, 1:2] * picked[1]
        ).astype(LOW)
        grad_out = cotangent.astype(WIDE)
        grad_probs = sum(
            jnp.sum(grad_out * picked[k], axis=1, keepdims=True) * chosen[k] for k in range(2)
        )
        gather_mat = (by_token[0] | by_token[1]).astype(LOW)
        grad_normed_two = jnp.dot(gather_mat, grad_home, preferred_element_type=WIDE)
        grad_logits = route_p * (grad_probs - jnp.sum(grad_probs * route_p, axis=-1, keepdims=True))
        grad_normed_two = grad_normed_two + jnp.dot(
            grad_logits, router.astype(WIDE).T, precision=lax.Precision.HIGHEST
        )
        grad_router = jnp.dot(
            normed_two.astype(WIDE).T, grad_logits, precision=lax.Precision.HIGHEST
        )
        _, pull_two = jax.vjp(norm_affine, middle, gain_two, shift_two)
        grad_mid_norm, grad_gain_two, grad_shift_two = pull_two(grad_normed_two)
        grad_middle = grad_out + grad_mid_norm
        grad_bias_attn = jnp.sum(grad_middle, axis=0)
        grad_mid_low = grad_middle.astype(LOW)
        grad_att = jnp.einsum(
            "td,ed->te", grad_mid_low, out_w, preferred_element_type=WIDE
        ).astype(LOW)
        grad_out_w = jnp.einsum("te,td->ed", attended, grad_mid_low, preferred_element_type=WIDE)
        grad_att_heads = grad_att.reshape(images, SEQ, H, HD)
        probs_again = jnp.exp(
            jnp.einsum("ishd,ithd->ihst", head_query, head_key, preferred_element_type=WIDE)
            * score_scale
            - log_total
        )
        grad_weights = jnp.einsum(
            "ishd,ithd->ihst", grad_att_heads, head_value, preferred_element_type=WIDE
        )
        row_delta = jnp.sum(grad_weights * probs_again, axis=-1, keepdims=True)
        grad_raw = (probs_again * (grad_weights - row_delta) * score_scale).astype(LOW)
        grad_value = jnp.einsum(
            "ihst,ishd->ithd",
            probs_again.astype(LOW),
            grad_att_heads,
            preferred_element_type=WIDE,
        )
        grad_query = jnp.einsum("ihst,ithd->ishd", grad_raw, head_key, preferred_element_type=WIDE)
        grad_key = jnp.einsum("ihst,ishd->ithd", grad_raw, head_query, preferred_element_type=WIDE)
        grad_proj = jnp.stack(
            [
                grad_query.astype(LOW).reshape(rows_here, width),
                grad_key.astype(LOW).reshape(rows_here, width),
                grad_value.astype(LOW).reshape(rows_here, width),
            ]
        )
        grad_qkv_w = jnp.einsum("td,jte->jde", normed_one, grad_proj, preferred_element_type=WIDE)
        grad_normed_one = jnp.einsum("jte,jde->td", grad_proj, qkv_w, preferred_element_type=WIDE)
        _, pull_one = jax.vjp(norm_affine, residual, gain_one, shift_one)
        grad_resid_norm, grad_gain_one, grad_shift_one = pull_one(grad_normed_one)
        grad_tokens = grad_middle + grad_resid_norm

        if whole:
            row_b = jnp.zeros((experts, ff), WIDE)
            row_b = lax.dynamic_update_slice(row_b, grad_first_b, (mine * owned, 0))
        else:
            row_b = jnp.zeros((experts, ff), WIDE)
            row_b = lax.dynamic_update_slice(
                row_b,
                grad_first_b,
                (lax.axis_index("dp") * owned, lax.axis_index("tensor") * blk_f),
            )
        vec_grads = jnp.stack(
            [grad_gain_one, grad_shift_one, grad_bias_attn, grad_gain_two, grad_shift_two]
        )
        out_pieces = [
            grad_qkv_w.reshape(3, n, dense_blk, width).swapaxes(0, 1).reshape(n, -1),
            grad_out_w.reshape(n, -1),
            grad_router.reshape(n, -1),
            grad_bias_back.reshape(experts, n, -1).swapaxes(0, 1).reshape(n, -1),
            row_b.reshape(dp, experts // dp, tn, blk_f).swapaxes(1, 2).reshape(n, -1),
            vec_grads.reshape(5, n, -1).swapaxes(0, 1).reshape(n, -1),
        ]
        out_pack = jnp.concatenate(
            [p.astype(LOW) for p in out_pieces] + [jnp.zeros((n, pad), LOW)], axis=1
        )
        out_all = lax.all_to_all(
            out_pack.reshape(n, -1, 512), everyone, split_axis=0, concat_axis=0, tiled=True
        )
        summed = jnp.sum(out_all.astype(WIDE), axis=0).reshape(-1)
        done = [summed[o : o + s] for o, s in zip(offs, sizes)]
        vec_done = done[5].reshape(5, -1)
        return (
            result,
            grad_tokens,
            vec_done[0],
            vec_done[1],
            done[0].reshape(w_qkv.shape),
            done[1].reshape(w_out.shape),
            vec_done[2],
            vec_done[3],
            vec_done[4],
            done[2].reshape(w_router.shape),
            grad_w_in,
            done[4].reshape(b_in.shape),
            grad_w_back,
            done[3].reshape(b_back.shape),
        )

    return per_device


def solution(mesh):
    everyone = ("dp", "tensor")
    in_specs = (
        P(everyone, None),
        P(everyone, None),
        P(everyone),
        P(everyone),
        P(None, everyone, None),
        P(everyone, None),
        P(everyone),
        P(everyone),
        P(everyone),
        P(everyone, None),
        P(None, "dp", "tensor"),
        P("dp", "tensor"),
        P(None, "tensor", "dp"),
        P(None, everyone),
        P(everyone, None),
        P(everyone, None),
    )
    out_specs = in_specs[:2] + in_specs[2:14]
    dp, tn = mesh.shape["dp"], mesh.shape["tensor"]

    def chosen(*args):
        one_each = args[10].shape[0] == dp * tn and dp // 4 == 4 and dp % 4 == 0
        return (make_owner_device if one_each else make_per_device)(dp, tn)(*args)

    return jax.shard_map(
        chosen,
        mesh=mesh,
        in_specs=in_specs,
        out_specs=out_specs,
        check_vma=False,
    )
```
